32 devices in a mesh: fsdp: 2 (over y), ctx: 4 (over x, core), tp: 4 (over z).
Axes of the slice: x: 2, y: 2, z: 4, core: 2. Of those that a mesh axis runs over, the one named last changes fastest.
Arguments:
- tokens: bfloat16 [8192, 2048], P(('fsdp', 'ctx')), may hold values from -6 to 6
- cotangent: bfloat16 [8192, 2048], P(('fsdp', 'ctx')), may hold values from -6 to 6
- piece_ids: int32 [8192], P(('fsdp', 'ctx')), may hold values from 0 to 32, as said below
- positions: int32 [8192], P(('fsdp', 'ctx')), may hold values from 0 to 12285, as said below
- norm_gain: bfloat16 [2048], replicated, may hold values from 0.5 to 1.5
- norm_shift: bfloat16 [2048], replicated, may hold values from -1.1953125 to 1.1953125
- in_proj: bfloat16 [3, 2048, 2048], P(None, ('fsdp', 'ctx'), 'tp'), may hold values from -0.125 to 0.125
- in_bias: bfloat16 [3, 2048], P(None, 'tp'), may hold values from -0.119628906 to 0.119628906
- out_proj: bfloat16 [2048, 2048], P('tp', ('fsdp', 'ctx')), may hold values from -3 to 3
- up_proj: bfloat16 [2048, 8192], P(('fsdp', 'ctx'), 'tp'), may hold values from -0.125 to 0.125
- up_bias: bfloat16 [8192], P('tp'), may hold values from -3 to 3
- down_proj: bfloat16 [8192, 2048], P('tp', ('fsdp', 'ctx')), may hold values from -0.0625 to 0.0625
- out_bias: bfloat16 [2048], replicated, may hold values from -1.1953125 to 1.1953125
Outputs:
- layer_out: bfloat16 [8192, 2048], P(('fsdp', 'ctx', 'tp'))
- input_grad: bfloat16 [8192, 2048], P(('fsdp', 'ctx', 'tp'))
- gain_grad: float32 [2048], replicated
- shift_grad: float32 [2048], replicated
- inproj_grad: float32 [3, 2048, 2048], P(None, ('fsdp', 'ctx'), 'tp')
- inbias_grad: float32 [3, 2048], P(None, 'tp')
- outproj_grad: float32 [2048, 2048], P('tp', ('fsdp', 'ctx'))
- upproj_grad: float32 [2048, 8192], P(('fsdp', 'ctx'), 'tp')
- upbias_grad: float32 [8192], P('tp')
- downproj_grad: float32 [8192, 2048], P('tp', ('fsdp', 'ctx'))
- outbias_grad: float32 [2048], replicated
The draws below stay inside these ranges and needn't reach their ends.
Inputs may be any that keep to these rules, and one draw needn't show every extreme that they name: `piece_ids`: each aligned run of 256 rows carries one number: 0 for text, or for a picture piece a number that no other run carries; the last run of all is a picture piece. Within each sequence of 4096 consecutive rows positions start at 0 and rise by 1, 2 or 3 from one row to the next; in the last sequence they rise by 3 throughout.
All inputs are finite; a program needn't handle non-finite values.
Results may differ from the reference program's by a relative error of at most 0.015.
Values may be sent and summed in bfloat16 or wider, within the bound.
A program may use at most 192 MiB of HBM per device.

```python
import math
import jax
import jax.numpy as jnp
from jax import lax

D = 2048
HD = 64
ROT = 32
FF = 8192
LEN = 4096
PIECE = 256
TOKENS = 8192


def draw_piece_ids(key, part):
    slot_count = TOKENS // PIECE
    picture_bits = jax.random.randint(key, (slot_count,), 0, 2, dtype=jnp.int32)
    slot_index = jnp.arange(slot_count, dtype=jnp.int32)
    picture_bits = jnp.where(slot_index == slot_count - 1, 1, picture_bits)
    labels = picture_bits * (slot_index + 1)
    return jnp.broadcast_to(labels[:, None], (slot_count, PIECE)).reshape(-1).astype(jnp.int32)


def draw_positions(key, part):
    sequence_count = TOKENS // LEN
    steps_drawn = jax.random.randint(key, (sequence_count, LEN - 1), 1, 4, dtype=jnp.int32)
    seq_index = jnp.arange(sequence_count, dtype=jnp.int32)
    steps_drawn = jnp.where((seq_index == sequence_count - 1)[:, None], 3, steps_drawn)
    starts = jnp.zeros((sequence_count, 1), jnp.int32)
    places = jnp.concatenate([starts, jnp.cumsum(steps_drawn, axis=1).astype(jnp.int32)], axis=1)
    return places.reshape(-1).astype(jnp.int32)


def levels(key, extent, cuts, smallest, largest):
    factor_of = 1.0
    for position, shards_of in cuts:
        draws = jax.random.uniform(jax.random.fold_in(jax.random.fold_in(key, 6), position), (shards_of,), jnp.float32, smallest / len(cuts), largest / len(cuts))
        factor_of = factor_of * jnp.repeat(jnp.exp(draws), extent[position] // shards_of).reshape((-1,) + (1,) * (len(extent) - 1 - position))
    return factor_of


def normal_values(stream_key, extent, deviation, most, shards=(), kind=jnp.bfloat16):
    gain = levels(stream_key, extent, shards, -0.22, 0.18) if shards else 1.0
    values = jax.random.normal(stream_key, extent, jnp.float32) * deviation * gain
    return jnp.minimum(jnp.maximum(values, -most), most).astype(kind)


def setup_inputs(seed: int = 0) -> dict:
    splits = jax.random.split(jax.random.key(seed), 14)
    tokens = normal_values(splits[0], (TOKENS, D), 1.0, 6.0, ((0, 8),))
    cotangent = normal_values(splits[1], (TOKENS, D), 1.0, 6.0, ((0, 8),))
    piece_ids = draw_piece_ids(jax.random.fold_in(splits[13], 71), 0)
    positions = draw_positions(jax.random.fold_in(splits[13], 71), 0)
    norm_gain = jnp.clip(1.0 + 0.1 * jax.random.normal(splits[4], (D,), jnp.float32), 0.5, 1.5).astype(jnp.bfloat16)
    norm_shift = normal_values(splits[5], (D,), 0.2, 1.1953125)
    in_proj = normal_values(splits[6], (3, D, D), D ** -0.5, 0.125, ((1, 8), (2, 4)))
    in_bias = normal_values(splits[7], (3, D), 0.02, 0.119628906, ((1, 4),))
    out_proj = normal_values(splits[8], (D, D), 4 ** -0.5, 3.0, ((0, 4), (1, 8)))
    up_proj = normal_values(splits[9], (D, FF), D ** -0.5, 0.125, ((0, 8), (1, 4)))
    up_bias = normal_values(splits[10], (FF,), 0.5, 3.0, ((0, 4),))
    down_proj = normal_values(splits[11], (FF, D), FF ** -0.5, 0.0625, ((0, 4), (1, 8)))
    out_bias = normal_values(splits[12], (D,), 0.2, 1.1953125)
    return {"tokens": tokens, "cotangent": cotangent, "piece_ids": piece_ids, "positions": positions, "norm_gain": norm_gain, "norm_shift": norm_shift, "in_proj": in_proj, "in_bias": in_bias, "out_proj": out_proj, "up_proj": up_proj, "up_bias": up_bias, "down_proj": down_proj, "out_bias": out_bias}


EPS = 1e-05
NEG = -1e+30
HIGH = lax.Precision.HIGHEST

@jax.custom_vjp
def low(v):
    return lax.optimization_barrier(v.astype(jnp.bfloat16)).astype(jnp.float32)

@jax.custom_vjp
def low_back(v):
    return v

def low_keep(v):
    return (low(v), None)

def low_pass(kept, grad):
    return (grad,)

def back_keep(v):
    return (v, None)

def back_low(kept, grad):
    return (low(grad),)
low.defvjp(low_keep, low_pass)
low_back.defvjp(back_keep, back_low)

def layer_norm(values, scaling, offset):
    center = values - lax.optimization_barrier(jnp.mean(values, axis=-1, keepdims=True))
    spread = lax.optimization_barrier(jnp.mean(center * center, axis=-1, keepdims=True))
    return center * lax.rsqrt(spread + EPS) * scaling + offset

def rotary_angles(places):
    frequency = 10000.0 ** (-2.0 * jnp.arange(ROT // 2, dtype=jnp.float32) / ROT)
    return places.astype(jnp.float32)[:, None] * frequency[None, :]

def rotate(values, angles):
    shaped = values.reshape(values.shape[0], -1, HD)
    half_rot = ROT // 2
    lower_half = shaped[..., :half_rot]
    upper_half = shaped[..., half_rot:ROT]
    remainder = shaped[..., ROT:]
    cos_part = jnp.cos(angles)[:, None, :]
    sin_part = jnp.sin(angles)[:, None, :]
    turned = jnp.concatenate([lower_half * cos_part - upper_half * sin_part, upper_half * cos_part + lower_half * sin_part, remainder], axis=-1)
    return turned.reshape(values.shape)

def attend(queries, keys, values, pieces, places):
    length = queries.shape[0]
    head_count = queries.shape[1] // HD
    query_block = min(length, 256)
    key_heads = keys.reshape(length, head_count, HD)
    value_heads = values.reshape(length, head_count, HD)
    score_scale = 1.0 / math.sqrt(HD)

    def one_block(block_args):
        query_rows, query_pieces, query_places = block_args
        scores = jnp.einsum('qhd,khd->hqk', query_rows, key_heads, precision=HIGH) * score_scale
        scores = low_back(scores)
        before = places[None, :] <= query_places[:, None]
        picture = (pieces[None, :] == query_pieces[:, None]) & (query_pieces[:, None] > 0)
        scores = jnp.where((before | picture)[None], scores, NEG)
        totals = jax.nn.logsumexp(scores, axis=-1, keepdims=True)
        softmax = low(jnp.exp(scores - totals))
        mixed = jnp.einsum('hqk,khd->qhd', softmax, value_heads, precision=HIGH)
        return mixed.reshape(query_rows.shape[0], head_count * HD)
    blocks = lax.map(jax.checkpoint(one_block), (queries.reshape(length // query_block, query_block, head_count, HD), pieces.reshape(-1, query_block), places.reshape(-1, query_block)))
    return blocks.reshape(length, head_count * HD)

def layer(seq_tokens, seq_pieces, seq_places, params):
    scaling, offset, in_proj, in_bias, out_proj, up_proj, up_bias, down_proj, out_bias = params
    normed = low(layer_norm(seq_tokens, scaling, offset))
    packed = low_back(jnp.einsum('td,jde->jte', normed, in_proj, precision=HIGH) + in_bias[:, None, :])
    angles = rotary_angles(seq_places)
    queries = low(rotate(packed[0], angles))
    keys = low(rotate(packed[1], angles))
    values = low(packed[2])
    attended = low(low_back(attend(queries, keys, values, seq_pieces, seq_places)))
    upward = low_back(jnp.dot(normed, up_proj, precision=HIGH) + up_bias)
    active = low(jax.nn.gelu(upward, approximate=True))
    return seq_tokens + jnp.dot(attended, out_proj, precision=HIGH) + jnp.dot(active, down_proj, precision=HIGH) + out_bias

def reference(tokens, cotangent, piece_ids, positions, norm_gain, norm_shift, in_proj, in_bias, out_proj, up_proj, up_bias, down_proj, out_bias):
    params = tuple((item.astype(jnp.float32) for item in (norm_gain, norm_shift, in_proj, in_bias, out_proj, up_proj, up_bias, down_proj, out_bias)))
    sequence_count = TOKENS // LEN

    def forward(flat_tokens, *weights):

        def per_sequence(seq_args):
            seq_tokens, seq_pieces, seq_places = seq_args
            return layer(seq_tokens, seq_pieces, seq_places, weights)
        outputs = lax.map(per_sequence, (flat_tokens.reshape(sequence_count, LEN, D), piece_ids.reshape(sequence_count, LEN), positions.reshape(sequence_count, LEN)))
        return outputs.reshape(TOKENS, D)
    result, pullback = jax.vjp(forward, tokens.astype(jnp.float32), *params)
    gradients = pullback(cotangent.astype(jnp.float32))
    return (result.astype(jnp.bfloat16), gradients[0].astype(jnp.bfloat16), gradients[1], gradients[2], gradients[3], gradients[4], gradients[5], gradients[6], gradients[7], gradients[8], gradients[9])
```

```python
import functools
import math

import jax
import jax.numpy as jnp
from jax import lax
from jax.experimental import pallas as pl
from jax.experimental.pallas import tpu as pltpu
from jax.sharding import Mesh
from jax.sharding import PartitionSpec as P

HD = 64
ROT = 32
RUN = 256
EPS = 1e-05
NEG = -1e30
F32 = jnp.float32
BF = jnp.bfloat16
NN = (((1,), (0,)), ((), ()))
NT = (((1,), (1,)), ((), ()))
TN = (((0,), (0,)), ((), ()))
SWAP = [(0, 1), (1, 0)]
GELU_A = math.sqrt(2.0 / math.pi)
GELU_B = 0.044715


def dot(a, b, dims=NN):
    return lax.dot_general(a, b, dims, preferred_element_type=F32)


def call(body, name, grid, in_specs, out_specs, out_shape, scratch, flops, moved, prefetch=1, vmem=56):
    return pl.pallas_call(
        body,
        out_shape=out_shape,
        grid_spec=pltpu.PrefetchScalarGridSpec(
            num_scalar_prefetch=prefetch,
            grid=grid,
            in_specs=in_specs,
            out_specs=out_specs,
            scratch_shapes=scratch,
        ),
        compiler_params=pltpu.CompilerParams(
            vmem_limit_bytes=vmem << 20, dimension_semantics=("arbitrary",) * len(grid)
        ),
        cost_estimate=pl.CostEstimate(flops=int(flops), bytes_accessed=int(moved), transcendentals=0),
        name=name,
    )


def row_block(size, width):
    return pl.BlockSpec((size, width), lambda i, s: (i, 0))


def fixed(shape, index=None):
    place = index or (0,) * len(shape)
    return pl.BlockSpec(shape, lambda i, s: place, pipeline_mode=pl.Buffered(1))


def norm_parts(rows):
    center = rows - jnp.mean(rows, axis=-1, keepdims=True)
    inverse = lax.rsqrt(jnp.mean(center * center, axis=-1, keepdims=True) + EPS)
    return center * inverse, inverse


def lanes_of(info, chunk, piece):
    return pl.ds(pl.multiple_of((piece ^ info[0]) * chunk, chunk), chunk)


def prepare_body(info, tok, cot, gain, shift, nrm, cot_out, cot_sum, *, chunk):
    xhat, _ = norm_parts(tok[...].astype(F32))
    full = (xhat * gain[...].astype(F32) + shift[...].astype(F32)).astype(BF)
    pieces = tok.shape[1] // chunk

    @pl.when(pl.program_id(0) == 0)
    def _():
        cot_sum[...] = jnp.zeros_like(cot_sum)

    cot_sum[...] += jnp.sum(cot[...].astype(F32), axis=0, keepdims=True)
    for r in range(pieces):
        nrm[:, lanes_of(info, chunk, r)] = full[:, r * chunk : r * chunk + chunk]
        cot_out[:, lanes_of(info, chunk, r)] = cot[:, r * chunk : r * chunk + chunk]


def prepare(info, tok, cot, gain, shift, chunk):
    rows, width = tok.shape
    size = min(rows, 256)
    spec = row_block(size, width)
    return call(
        functools.partial(prepare_body, chunk=chunk),
        "normalize",
        (rows // size,),
        [spec, spec, fixed((1, width)), fixed((1, width))],
        [spec, spec, pl.BlockSpec((1, width), lambda i, s: (0, 0))],
        [jax.ShapeDtypeStruct(tok.shape, BF)] * 2 + [jax.ShapeDtypeStruct((1, width), F32)],
        [],
        10 * tok.size,
        8 * tok.size,
    )(info, tok, cot, gain[None], shift[None])


def turn(values, cos_part, down, up):
    return (
        values * cos_part
        + pltpu.roll(values, 128 - ROT // 2, 1) * down
        + pltpu.roll(values, ROT // 2, 1) * up
    )


def project_body(info, nrm, cot, weights, bias, cos_t, down_t, up_t, q_out, kv_out, do_out, *, width):
    packed = dot(nrm[...], weights[:, : 3 * width]) + bias[...].astype(F32)
    c, d, u = cos_t[...], down_t[...], up_t[...]
    for p in range(width // 128):
        lanes = slice(128 * p, 128 * p + 128)
        q_out[:, lanes] = turn(packed[:, lanes], c, d, u).astype(BF)
        shifted = slice(width + 128 * p, width + 128 * p + 128)
        kv_out[:, lanes] = turn(packed[:, shifted], c, d, u).astype(BF)
    kv_out[:, width:] = packed[:, 2 * width :].astype(BF)
    do_out[...] = dot(cot[...], weights[:, 3 * width :]).astype(BF)


def project(info, nrm, cot, weights, bias, tables, width):
    rows, depth = nrm.shape
    size = min(rows, 256)
    spec = row_block(size, depth)
    table = row_block(size, 128)
    return call(
        functools.partial(project_body, width=width),
        "project",
        (rows // size,),
        [spec, spec, fixed((depth, 4 * width)), fixed((1, 3 * width)), table, table, table],
        [row_block(size, width), row_block(size, 2 * width), row_block(size, width)],
        [
            jax.ShapeDtypeStruct((rows, width), BF),
            jax.ShapeDtypeStruct((rows, 2 * width), BF),
            jax.ShapeDtypeStruct((rows, width), BF),
        ],
        [],
        2 * rows * depth * 4 * width,
        2 * (2 * rows * depth + depth * 4 * width + 4 * rows * width),
    )(info, nrm, cot, weights, bias, *tables)


def hidden_body(info, nrm, cot, up, down, bias, act_out, grad_out, sum_out):
    u = dot(nrm[...], up[...]) + bias[...].astype(F32)
    g = dot(cot[...], down[...])
    square = u * u
    t = jnp.tanh(GELU_A * (u + GELU_B * square * u))
    half = 0.5 * (1.0 + t)
    act_out[...] = (u * half).astype(BF)
    slope = half + 0.5 * u * (1.0 - t * t) * (GELU_A * (1.0 + 3.0 * GELU_B * square))
    low = (g * slope).astype(BF)
    grad_out[...] = low

    @pl.when(pl.program_id(0) == 0)
    def _():
        sum_out[...] = jnp.zeros_like(sum_out)

    sum_out[...] += jnp.sum(low.astype(F32), axis=0, keepdims=True)


def hidden(info, nrm, cot, weights, bias, width):
    rows, depth = nrm.shape
    size = min(rows, 256)
    spec = row_block(size, depth)
    return call(
        hidden_body,
        "hidden",
        (rows // size,),
        [spec, spec, fixed((depth, width)), fixed((depth, width), (0, 1)), fixed((1, width))],
        [row_block(size, width), row_block(size, width), pl.BlockSpec((1, width), lambda i, s: (0, 0))],
        [jax.ShapeDtypeStruct((rows, width), BF)] * 2 + [jax.ShapeDtypeStruct((1, width), F32)],
        [],
        4 * rows * depth * width,
        2 * (2 * rows * depth + 2 * depth * width + 2 * rows * width),
    )(info, nrm, cot, weights, weights, bias)


def spread_body(info, a, b, wa, wb, *rest):
    total = dot(a[...], wa[...], NT) + dot(b[...], wb[...], NT)
    if len(rest) == 2:
        total = total + rest[0][...].astype(F32)
    rest[-1][...] = total.astype(BF)


def spread(info, a, b, wa, wb, ia, ib, half, rows, received, name):
    depth = wa.shape[0]
    size = min(rows, 256)
    first = half * (rows // size)
    at = lambda width: pl.BlockSpec((size, width), lambda i, s: (i + first, 0))
    wide_a, wide_b = a.shape[1], b.shape[1]
    extra = [] if received is None else [received]
    return call(
        spread_body,
        name,
        (rows // size,),
        [at(wide_a), at(wide_b), fixed((depth, wide_a), (0, ia)), fixed((depth, wide_b), (0, ib))]
        + [row_block(size, depth)] * len(extra),
        [row_block(size, depth)],
        [jax.ShapeDtypeStruct((rows, depth), BF)],
        [],
        2 * rows * depth * (wide_a + wide_b),
        2 * (rows + depth) * (wide_a + wide_b) + 2 * rows * depth * (1 + len(extra)),
    )(info, a, b, wa, wb, *extra)[0]


def outer_body(info, left, right, out):
    out[...] = dot(left[...], right[...], TN).astype(BF)


def outer(info, left, right, blocks, chunk, name):
    rows = left.shape[0]
    width = right.shape[1]
    size = min(chunk, 256)
    per = chunk // size
    first, step = blocks
    count = (left.shape[1] // chunk if step == 0 else 2) * per

    def place(i, s):
        return (0, i) if step == 0 else (0, (first + step * (i // per)) * per + i % per)

    return call(
        outer_body,
        name,
        (count,),
        [pl.BlockSpec((rows, size), place), fixed((rows, width))],
        [row_block(size, width)],
        [jax.ShapeDtypeStruct((count * size, width), BF)],
        [],
        2 * rows * count * size * width,
        2 * (rows * count * size + rows * width + count * size * width),
    )(info, left, right)[0]


def head_masks(block, scale):
    lane = lax.broadcasted_iota(jnp.int32, block.shape, 1)
    v = block.astype(F32) * scale
    return (jnp.where(lane < HD, v, 0.0).astype(BF), jnp.where(lane < HD, 0.0, v).astype(BF))


def own_mask(flag, width):
    kk = lax.broadcasted_iota(jnp.int32, (RUN, width), 0)
    qq = lax.broadcasted_iota(jnp.int32, (RUN, width), 1)
    return kk <= qq + flag * RUN


def each_prefix(here, half, runs, work):
    size = runs // 2
    while size:

        @pl.when((here & size) != 0)
        def _(size=size):
            low = here & ((runs - 1) & ~(2 * size - 1))
            work(pl.multiple_of((low ^ half) * RUN, RUN), size * RUN)

        size //= 2


def forward_body(info, q_ref, do_ref, k_ref, v_ref, kx_ref, vx_ref, att_ref, stat_ref, vt, vxt, acc, ml, *, pairs, cut):
    i = pl.program_id(0)
    half = info[0]
    here = i ^ half
    has_cross = info[1]
    heads = 2 * pairs
    runs = k_ref.shape[0] // RUN

    @pl.when(i == 0)
    def _():
        vt[...] = v_ref[...].astype(F32).T.astype(BF)

    @pl.when((i == 0) & (has_cross > 0))
    def _():
        vxt[...] = vx_ref[...].astype(F32).T.astype(BF)

    qm = [head_masks(q_ref[:, 128 * p : 128 * p + 128], 1.0 / math.sqrt(HD)) for p in range(pairs)]

    def block(k_r, vt_r, start, size, mask=None):
        def score(n):
            p, h = divmod(n, 2)
            s = dot(k_r[pl.ds(start, size), 128 * p : 128 * p + 128], qm[p][h], NT)
            return s if mask is None else jnp.where(mask, s, NEG)

        def rest(n, s):
            top = jnp.max(s, axis=0, keepdims=True)
            rows = slice(HD * n, HD * n + HD)
            vb = vt_r[rows, pl.ds(start, size)]
            if mask is not None:
                e = jnp.exp(s - top)
                ml[n : n + 1, :] = top
                ml[heads + n : heads + n + 1, :] = jnp.sum(e, axis=0, keepdims=True)
                acc[rows, :] = dot(vb, e.astype(BF))
            else:
                m = ml[n : n + 1, :]
                new = jnp.maximum(m, top)
                alpha = jnp.exp(m - new)
                e = jnp.exp(s - new)
                ml[n : n + 1, :] = new
                ml[heads + n : heads + n + 1, :] = (
                    ml[heads + n : heads + n + 1, :] * alpha + jnp.sum(e, axis=0, keepdims=True)
                )
                acc[rows, :] = acc[rows, :] * alpha + dot(vb, e.astype(BF))

        s = score(0)
        for n in range(heads):
            following = score(n + 1) if n + 1 < heads else None
            rest(n, s)
            s = following

    block(k_ref, vt, pl.multiple_of(i * RUN, RUN), RUN, own_mask(info[2 + i], q_ref.shape[0]))
    each_prefix(here, half, runs, lambda start, size: block(k_ref, vt, start, size))

    @pl.when(has_cross > 0)
    def _():
        def cross(j, c):
            block(kx_ref, vxt, pl.multiple_of(j * cut, cut), cut)
            return c

        lax.fori_loop(0, kx_ref.shape[0] // cut, cross, 0)

    for p in range(pairs):
        do_t = do_ref[:, 128 * p : 128 * p + 128].astype(F32).T
        parts = []
        for h in range(2):
            n = 2 * p + h
            m, l = ml[n : n + 1, :], ml[heads + n : heads + n + 1, :]
            o = acc[HD * n : HD * n + HD, :] / l
            parts.append(o)
            stat_ref[n : n + 1, :] = m + jnp.log(l)
            stat_ref[heads + n : heads + n + 1, :] = jnp.sum(o * do_t[HD * h : HD * h + HD, :], axis=0, keepdims=True)
        att_ref[:, 128 * p : 128 * p + 128] = jnp.concatenate(parts, axis=0).T.astype(BF)


def attend(info, q, do, kv, kvx):
    rows, width = q.shape
    pairs = width // 128
    cut = min(rows, 1024)
    blk = row_block(RUN, width)
    left, right = fixed((rows, width)), fixed((rows, width), (0, 1))
    return call(
        functools.partial(forward_body, pairs=pairs, cut=cut),
        "attend",
        (rows // RUN,),
        [blk, blk, left, right, left, right],
        [blk, pl.BlockSpec((4 * pairs, RUN), lambda i, s: (0, i))],
        [jax.ShapeDtypeStruct((rows, width), BF), jax.ShapeDtypeStruct((4 * pairs, rows), F32)],
        [
            pltpu.VMEM((width, rows), BF),
            pltpu.VMEM((width, rows), BF),
            pltpu.VMEM((width, RUN), F32),
            pltpu.VMEM((4 * pairs, RUN), F32),
        ],
        40e9,
        14 * rows * width,
    )(info, q, do, kv, kv, kvx, kvx)


def backward_body(info, q_ref, do_ref, stat_ref, k_ref, v_ref, kx_ref, vx_ref, dq_ref, dk_ref, dv_ref, dkvx_ref, kt, kxt, dqt, dkx, dvx, *, pairs, cut):
    i = pl.program_id(0)
    half = info[0]
    here = i ^ half
    has_cross = info[1]
    heads = 2 * pairs
    width = 128 * pairs
    scale = 1.0 / math.sqrt(HD)
    runs = k_ref.shape[0] // RUN

    @pl.when(i == 0)
    def _():
        kt[...] = k_ref[...].astype(F32).T.astype(BF)
        dk_ref[...] = jnp.zeros_like(dk_ref)
        dv_ref[...] = jnp.zeros_like(dv_ref)

    @pl.when((i == 0) & (has_cross > 0))
    def _():
        kxt[...] = kx_ref[...].astype(F32).T.astype(BF)
        dkx[...] = jnp.zeros_like(dkx)
        dvx[...] = jnp.zeros_like(dvx)

    qm = [head_masks(q_ref[:, 128 * p : 128 * p + 128], scale) for p in range(pairs)]
    dm = [head_masks(do_ref[:, 128 * p : 128 * p + 128], 1.0) for p in range(pairs)]
    dqt[...] = jnp.zeros_like(dqt)

    def block(k_r, v_r, kt_r, dk_r, dv_r, start, size, mask=None):
        def products(n):
            p, h = divmod(n, 2)
            lanes = slice(128 * p, 128 * p + 128)
            return (
                dot(k_r[pl.ds(start, size), lanes], qm[p][h], NT),
                dot(v_r[pl.ds(start, size), lanes], dm[p][h], NT),
            )

        def rest(n, s, g):
            p, h = divmod(n, 2)
            e = jnp.exp(s - stat_ref[n : n + 1, :])
            if mask is not None:
                e = jnp.where(mask, e, 0.0)
            ds = (e * (g - stat_ref[heads + n : heads + n + 1, :])).astype(BF)
            rows = slice(HD * n, HD * n + HD)
            dqt[rows, :] += dot(kt_r[rows, pl.ds(start, size)], ds)
            return dot(ds, qm[p][h]), dot(e.astype(BF), dm[p][h])

        now = products(0)
        before = None
        for n in range(heads):
            following = products(n + 1) if n + 1 < heads else None
            grads = rest(n, *now)
            now = following
            if n % 2:
                lanes = slice(HD * (n - 1), HD * (n + 1))
                dk_r[pl.ds(start, size), lanes] += before[0] + grads[0]
                dv_r[pl.ds(start, size), lanes] += before[1] + grads[1]
            before = grads

    @pl.when(has_cross > 0)
    def _():
        def cross(j, c):
            block(kx_ref, vx_ref, kxt, dkx, dvx, pl.multiple_of(j * cut, cut), cut)
            return c

        lax.fori_loop(0, kx_ref.shape[0] // cut, cross, 0)

    work = lambda start, size, mask=None: block(k_ref, v_ref, kt, dk_ref, dv_ref, start, size, mask)
    work(pl.multiple_of(i * RUN, RUN), RUN, own_mask(info[2 + i], q_ref.shape[0]))
    each_prefix(here, half, runs, work)
    dq_ref[...] = (dqt[...] * scale).T

    @pl.when(i == pl.num_programs(0) - 1)
    def _():
        @pl.when(has_cross > 0)
        def _():
            dkvx_ref[:, :width] = dkx[...].astype(BF)
            dkvx_ref[:, width:] = dvx[...].astype(BF)

        @pl.when(has_cross == 0)
        def _():
            dkvx_ref[...] = jnp.zeros_like(dkvx_ref)


def attend_back(info, q, do, stat, kv, kvx):
    rows, width = q.shape
    pairs = width // 128
    cut = min(rows, 1024)
    blk = row_block(RUN, width)
    left, right = fixed((rows, width)), fixed((rows, width), (0, 1))
    whole = pl.BlockSpec((rows, width), lambda i, s: (0, 0))
    acc = jax.ShapeDtypeStruct((rows, width), F32)
    return call(
        functools.partial(backward_body, pairs=pairs, cut=cut),
        "attend_back",
        (rows // RUN,),
        [blk, blk, pl.BlockSpec((4 * pairs, RUN), lambda i, s: (0, i)), left, right, left, right],
        [blk, whole, whole, pl.BlockSpec((rows, 2 * width), lambda i, s: (0, 0))],
        [acc, acc, acc, jax.ShapeDtypeStruct((rows, 2 * width), BF)],
        [
            pltpu.VMEM((width, rows), BF),
            pltpu.VMEM((width, rows), BF),
            pltpu.VMEM((width, RUN), F32),
            pltpu.VMEM((rows, width), F32),
            pltpu.VMEM((rows, width), F32),
        ],
        60e9,
        30 * rows * width,
    )(info, q, do, stat, kv, kv, kvx, kvx)


def collect_body(info, dq, dk, dv, other_k, other_v, cos_t, down_t, up_t, out, sums, *, width):
    c, d, u = cos_t[...], -down_t[...], -up_t[...]
    for p in range(width // 128):
        lanes = slice(128 * p, 128 * p + 128)
        out[:, lanes] = turn(dq[:, lanes], c, d, u).astype(BF)
        key = dk[:, lanes] + other_k[:, lanes].astype(F32)
        out[:, width + 128 * p : width + 128 * p + 128] = turn(key, c, d, u).astype(BF)
    out[:, 2 * width :] = (dv[...] + other_v[...].astype(F32)).astype(BF)

    @pl.when(pl.program_id(0) == 0)
    def _():
        sums[...] = jnp.zeros_like(sums)

    sums[...] += jnp.sum(out[...].astype(F32), axis=0, keepdims=True)


def collect(info, dq, dk, dv, other, tables):
    rows, width = dq.shape
    size = min(rows, 512)
    spec = row_block(size, width)
    table = row_block(size, 128)
    return call(
        functools.partial(collect_body, width=width),
        "collect",
        (rows // size,),
        [spec, spec, spec, spec, pl.BlockSpec((size, width), lambda i, s: (i, 1)), table, table, table],
        [row_block(size, 3 * width), pl.BlockSpec((1, 3 * width), lambda i, s: (0, 0))],
        [jax.ShapeDtypeStruct((rows, 3 * width), BF), jax.ShapeDtypeStruct((1, 3 * width), F32)],
        [],
        20 * rows * width,
        30 * rows * width,
    )(info, dq, dk, dv, other, other, *tables)


def input_body(info, grad, tok, cot, gain, out, *, chunk):
    xhat, inverse = norm_parts(tok[...].astype(F32))
    pieces = tok.shape[1] // chunk
    parts = [grad[:, lanes_of(info, chunk, r)] for r in range(pieces)]
    e = jnp.concatenate(parts, axis=1).astype(F32) * gain[...].astype(F32)
    mean_e = jnp.mean(e, axis=-1, keepdims=True)
    mean_ex = jnp.mean(e * xhat, axis=-1, keepdims=True)
    out[...] = (cot[...].astype(F32) + (e - mean_e - xhat * mean_ex) * inverse).astype(BF)


def input_grads(info, grad, tok, cot, gain, chunk):
    rows, width = grad.shape
    share = pl.BlockSpec((rows, width), lambda i, s: (s[1], 0))
    return call(
        functools.partial(input_body, chunk=chunk),
        "input_grad",
        (1,),
        [row_block(rows, width), share, share, fixed((1, width))],
        [row_block(rows, width)],
        [jax.ShapeDtypeStruct((rows, width), BF)],
        [],
        20 * grad.size,
        8 * grad.size,
    )(info, grad, tok, cot, gain[None])[0]


def layer_body(info, branch, tok, bias, out, *, chunk):
    for r in range(tok.shape[1] // chunk):
        at = slice(r * chunk, r * chunk + chunk)
        part = branch[:, lanes_of(info, chunk, r)].astype(F32)
        out[:, at] = (tok[:, at].astype(F32) + part + bias[:, at].astype(F32)).astype(BF)


def layer_rows(info, branch, tok, bias, chunk):
    rows, width = branch.shape
    return call(
        functools.partial(layer_body, chunk=chunk),
        "layer_out",
        (1,),
        [row_block(rows, width), pl.BlockSpec((rows, width), lambda i, s: (s[1], 0)), fixed((1, width))],
        [row_block(rows, width)],
        [jax.ShapeDtypeStruct((rows, width), BF)],
        [],
        4 * branch.size,
        6 * branch.size,
    )(info, branch, tok, bias[None])[0]


def norm_sums_body(info, grad, tok, gain_sum, shift_sum, *, chunk):
    xhat, _ = norm_parts(tok[...].astype(F32))

    @pl.when(pl.program_id(0) == 0)
    def _():
        gain_sum[...] = jnp.zeros_like(gain_sum)
        shift_sum[...] = jnp.zeros_like(shift_sum)

    for r in range(tok.shape[1] // chunk):
        at = slice(r * chunk, r * chunk + chunk)
        part = grad[:, lanes_of(info, chunk, r)].astype(F32)
        shift_sum[:, at] += jnp.sum(part, axis=0, keepdims=True)
        gain_sum[:, at] += jnp.sum(part * xhat[:, at], axis=0, keepdims=True)


def norm_sums(info, grad, tok, chunk):
    rows, width = grad.shape
    size = min(rows, 256)
    one = pl.BlockSpec((1, width), lambda i, s: (0, 0))
    return call(
        functools.partial(norm_sums_body, chunk=chunk),
        "norm_sums",
        (rows // size,),
        [row_block(size, width)] * 2,
        [one, one],
        [jax.ShapeDtypeStruct((1, width), F32)] * 2,
        [],
        20 * grad.size,
        4 * grad.size,
    )(info, grad, tok)


def body(tokens, cotangent, piece_ids, positions, norm_gain, norm_shift, in_proj, in_bias, out_proj, up_proj, up_bias, down_proj, out_bias):
    length, depth = tokens.shape
    width = in_bias.shape[1] // 2
    hidden_width = up_bias.shape[0] // 2
    f_count, z_count = lax.axis_size("fsdp"), lax.axis_size("tp")
    x_at, c_at, f_at = lax.axis_index("cx"), lax.axis_index("cc"), lax.axis_index("fsdp")
    square = f_count == 2
    chips = 2 * f_count
    chunk = depth // chips
    me = f_at * 2 + x_at if square else 0 * f_at
    info = jnp.stack([me, lax.axis_index("tp")]).astype(jnp.int32)

    other_core = lambda value: lax.ppermute(value, "cc", SWAP)
    by_x = lambda value: lax.ppermute(value, "cx", SWAP)
    by_y = lambda value: lax.ppermute(value, "fsdp", SWAP)

    def pick(value, index, size, axis):
        return lax.dynamic_slice_in_dim(value, index * size, size, axis)

    def in_order(mine, theirs, axis):
        return jnp.where(c_at == 0, jnp.concatenate([mine, theirs], axis), jnp.concatenate([theirs, mine], axis))

    def cut_attention(c):
        parts = [pick(in_proj[j], c, width, 1) for j in range(3)]
        return jnp.concatenate(parts + [pick(out_proj, c, width, 0).T], axis=1)

    def cut_hidden(c):
        return jnp.concatenate([pick(up_proj, c, hidden_width, 1), pick(down_proj, c, hidden_width, 0).T], axis=1)

    def gather(value):
        if not square:
            return lax.all_gather(value, ("fsdp", "cx"), axis=0, tiled=True)
        middle = value.shape[0] // 2
        from_x, from_y = by_x(value), by_y(value)
        far = [by_x(from_y[:middle]), by_y(from_x[middle:])]
        return jnp.concatenate([value, from_x, from_y] + far, axis=0)

    weights_a = gather(in_order(cut_attention(c_at), other_core(cut_attention(1 - c_at)), 0))
    small = jnp.stack([piece_ids, positions])
    small = jnp.concatenate([small, other_core(small)], axis=1)
    pieces, places = small[0], small[1]
    normed, cot, cot_sum = prepare(info, tokens, cotangent, norm_gain, norm_shift, chunk)
    normed = jnp.concatenate([normed, other_core(normed)], axis=0)
    cot = jnp.concatenate([cot, other_core(cot)], axis=0)
    weights_m = gather(in_order(cut_hidden(c_at), other_core(cut_hidden(1 - c_at)), 0))

    lane = jnp.arange(128, dtype=jnp.int32) % HD
    slot = (lane % (ROT // 2)).astype(F32)
    angles = places.astype(F32)[:, None] * (10000.0 ** (-2.0 * slot / ROT))[None, :]
    cos_part, sin_part = jnp.cos(angles), jnp.sin(angles)
    tables = (
        jnp.where(lane[None] < ROT, cos_part, 1.0),
        jnp.where(lane[None] < ROT // 2, -sin_part, 0.0),
        jnp.where((lane[None] >= ROT // 2) & (lane[None] < ROT), sin_part, 0.0),
    )
    bias_a = pick(in_bias, c_at, width, 1).reshape(1, 3 * width)
    bias_m = pick(up_bias, c_at, hidden_width, 0)[None]
    flags = (pieces.reshape(-1, RUN)[:, 0] > 0).astype(jnp.int32)
    scene = jnp.concatenate([jnp.stack([c_at * (length // RUN), x_at]).astype(jnp.int32), flags])

    queries, kv, grad_att = project(info, normed, cot, weights_a, bias_a, tables, width)
    kvx = lax.ppermute(kv, "cx", [(0, 1)])
    attended, stat = attend(scene, queries, grad_att, kv, kvx)
    active, grad_up, up_sum = hidden(info, normed, cot, weights_m, bias_m, hidden_width)

    def reduce_rows(left, right, x_first, name):
        if not square:
            whole = outer(info, left, right, (0, 0), chunk, name)
            return lax.psum_scatter(whole, ("fsdp", "cx"), scatter_dimension=0, tiled=True)
        near, far = (by_x, by_y) if x_first else (by_y, by_x)
        sent, kept = ((1, 2), (0, 2)) if x_first else ((2, 1), (0, 1))
        away = outer(info, left, right, sent, chunk, name)
        came = near(away)
        held = outer(info, left, right, kept, chunk, name)
        add = lambda a, b: (a.astype(F32) + b.astype(F32)).astype(BF)
        second = add(held[chunk:], came[chunk:])
        return add(add(held[:chunk], came[:chunk]), far(second))

    up_rows = reduce_rows(normed, grad_up, True, "up_grad")
    down_rows = reduce_rows(cot, active, False, "down_grad")
    out_rows = reduce_rows(cot, attended, False, "out_grad")

    ia, ib = 3, 1
    theirs = spread(info, attended, active, weights_a, weights_m, ia, ib, 1, length, None, "branch_away")
    ours = spread(info, attended, active, weights_a, weights_m, ia, ib, 0, length, other_core(theirs), "branch_here")
    branch = lax.psum_scatter(ours, "tp", scatter_dimension=0, tiled=True)
    layer_out = layer_rows(info, branch, tokens, out_bias, chunk)

    grad_q, grad_k, grad_v, away = attend_back(scene, queries, grad_att, stat, kv, kvx)
    other = lax.ppermute(away, "cx", [(1, 0)])
    grad_packed, in_sum = collect(info, grad_q, grad_k, grad_v, other, tables)
    theirs = spread(info, grad_packed, grad_up, weights_a, weights_m, 0, 0, 1, length, None, "normed_away")
    ours = spread(info, grad_packed, grad_up, weights_a, weights_m, 0, 0, 0, length, other_core(theirs), "normed_here")
    grad_normed = lax.psum_scatter(ours, "tp", scatter_dimension=0, tiled=True)
    gain_sum, shift_sum = norm_sums(info, ours, tokens, chunk)
    in_rows = reduce_rows(normed, grad_packed, True, "in_grad")
    input_grad = input_grads(info, grad_normed, tokens, cotangent, norm_gain, chunk)

    once = jnp.where(lax.axis_index("tp") == 0, cot_sum, 0.0)
    all_wide = jnp.concatenate([gain_sum, shift_sum, once], axis=1)
    narrow = jnp.concatenate([in_sum, up_sum], axis=1)
    wide_size = all_wide.shape[1]
    both = jnp.concatenate([all_wide, narrow], axis=1)
    if square:
        both = both + by_x(both)
        both = both + by_y(both)
    else:
        both = lax.psum(both, ("fsdp", "cx"))
    swapped = other_core(both)
    wide = both[:, :wide_size] + swapped[:, :wide_size]
    step = 1
    while step < z_count:
        wide = wide + lax.ppermute(wide, "tp", [(z, z ^ step) for z in range(z_count)])
        step *= 2
    gain_grad, shift_grad, outbias_grad = [wide[0, depth * j : depth * j + depth] for j in range(3)]
    narrow_pair = in_order(both[:, wide_size:], swapped[:, wide_size:], 0)
    inbias_grad = jnp.transpose(narrow_pair[:, : 3 * width].reshape(2, 3, width), (1, 0, 2)).reshape(3, 2 * width)
    upbias_grad = narrow_pair[:, 3 * width :].reshape(2 * hidden_width)

    def keep(rows):
        size = rows.shape[0] // 2
        mine, theirs = pick(rows, c_at, size, 0), pick(rows, 1 - c_at, size, 0)
        came = other_core(theirs)
        return jnp.where(c_at == 0, jnp.stack([mine, came]), jnp.stack([came, mine])).astype(F32)

    up_two, down_two, out_two, in_two = keep(up_rows), keep(down_rows), keep(out_rows), keep(in_rows)
    share = up_two.shape[1]
    upproj_grad = jnp.transpose(up_two, (1, 0, 2)).reshape(share, 2 * hidden_width)
    downproj_grad = jnp.transpose(down_two, (0, 2, 1)).reshape(2 * hidden_width, share)
    outproj_grad = jnp.transpose(out_two, (0, 2, 1)).reshape(2 * width, share)
    inproj_grad = jnp.transpose(in_two.reshape(2, share, 3, width), (2, 1, 0, 3)).reshape(3, share, 2 * width)
    return (
        layer_out,
        input_grad,
        gain_grad,
        shift_grad,
        inproj_grad,
        inbias_grad,
        outproj_grad,
        upproj_grad,
        upbias_grad,
        downproj_grad,
        outbias_grad,
    )


def solution(mesh):
    sizes = mesh.shape
    split = Mesh(
        mesh.devices.reshape(sizes["fsdp"], sizes["ctx"] // 2, 2, sizes["tp"]), ("fsdp", "cx", "cc", "tp")
    )
    group = ("fsdp", "cx", "cc")
    return jax.shard_map(
        body,
        mesh=split,
        in_specs=(
            P(group, None),
            P(group, None),
            P(group),
            P(group),
            P(),
            P(),
            P(None, group, "tp"),
            P(None, "tp"),
            P("tp", group),
            P(group, "tp"),
            P("tp"),
            P("tp", group),
            P(),
        ),
        out_specs=(
            P(group + ("tp",), None),
            P(group + ("tp",), None),
            P(),
            P(),
            P(None, group, "tp"),
            P(None, "tp"),
            P("tp", group),
            P(group, "tp"),
            P("tp"),
            P("tp", group),
            P(),
        ),
        check_vma=False,
    )
```

```python
import functools
import math

import jax
import jax.numpy as jnp
from jax import lax
from jax.experimental import pallas as pl
from jax.experimental.pallas import tpu as pltpu
from jax.sharding import Mesh
from jax.sharding import PartitionSpec as P

HD = 64
ROT = 32
RUN = 256
EPS = 1e-05
NEG = -1e30
F32 = jnp.float32
BF = jnp.bfloat16
NN = (((1,), (0,)), ((), ()))
NT = (((1,), (1,)), ((), ()))
TN = (((0,), (0,)), ((), ()))
SWAP = [(0, 1), (1, 0)]
GELU_A = math.sqrt(2.0 / math.pi)
GELU_B = 0.044715
COST = 100.0


def dot(a, b, dims=NN):
    return lax.dot_general(a, b, dims, preferred_element_type=F32)


ANY = pl.BlockSpec(memory_space=pl.ANY)


def call(body, name, grid, in_specs, out_specs, out_shape, scratch, flops, moved, prefetch=1, vmem=60, collective=None):
    return pl.pallas_call(
        body,
        out_shape=out_shape,
        grid_spec=pltpu.PrefetchScalarGridSpec(
            num_scalar_prefetch=prefetch,
            grid=grid,
            in_specs=in_specs,
            out_specs=out_specs,
            scratch_shapes=scratch,
        ),
        compiler_params=pltpu.CompilerParams(
            vmem_limit_bytes=vmem << 20,
            dimension_semantics=("arbitrary",) * len(grid),
            collective_id=collective,
            has_side_effects=collective is not None,
        ),
        cost_estimate=pl.CostEstimate(flops=int(flops * COST), bytes_accessed=int(moved * COST), transcendentals=0),
        name=name,
    )


def row_block(size, width):
    return pl.BlockSpec((size, width), lambda i, s: (i, 0))


def fixed(shape, index=None):
    place = index or (0,) * len(shape)
    return pl.BlockSpec(shape, lambda i, s: place, pipeline_mode=pl.Buffered(1))


def norm_parts(rows):
    center = rows - jnp.mean(rows, axis=-1, keepdims=True)
    inverse = lax.rsqrt(jnp.mean(center * center, axis=-1, keepdims=True) + EPS)
    return center * inverse, inverse


def lanes_of(info, chunk, piece):
    return pl.ds(pl.multiple_of((piece ^ info[0]) * chunk, chunk), chunk)


def to_neighbour(source, target, sends, receives, n, axis, at):
    return pltpu.make_async_remote_copy(
        src_ref=source,
        dst_ref=target,
        send_sem=sends.at[n],
        recv_sem=receives.at[n],
        device_id={axis: at},
        device_id_type=pl.DeviceIdType.MESH,
    )


def begin_body(tok, cot, gain, shift, in_ref, out_ref, up_any, down_any, nrm, cot_out, wa, vm, cot_sum, chip_a, away_a, chip_m, away_m, up_ref, down_ref, nbuf, cbuf, loads, locals_, sends, receives, *, chunk, square, steps):
    i = pl.program_id(0)
    core, x, y = lax.axis_index("cc"), lax.axis_index("cx"), lax.axis_index("fsdp")
    shard = in_ref.shape[1]
    size, depth = tok.shape
    width, wide = chip_a.shape[1] // 4, chip_m.shape[1] // 2
    mine = pl.ds(pl.multiple_of(core * shard, shard), shard)
    rows = 2 * shard
    peers = [("cc", 1 - core)] + ([("cx", 1 - x), ("fsdp", 1 - y)] if square else [])

    load_up = pltpu.make_async_copy(up_any, up_ref, loads.at[0])
    load_down = pltpu.make_async_copy(down_any, down_ref, loads.at[1])
    swap_a = to_neighbour(away_a, chip_a.at[mine, :], sends, receives, 0, "cc", 1 - core)
    swap_m = to_neighbour(away_m, chip_m.at[mine, :], sends, receives, 1, "cc", 1 - core)
    keep_a = pltpu.make_async_copy(chip_a, wa.at[pl.ds(0, rows), :], locals_.at[0])
    keep_m = pltpu.make_async_copy(chip_m, vm, locals_.at[1])
    if square:
        to_x = to_neighbour(chip_a, wa.at[pl.ds(rows, rows), :], sends, receives, 2, "cx", 1 - x)
        to_y = to_neighbour(chip_a, wa.at[pl.ds(2 * rows, rows), :], sends, receives, 3, "fsdp", 1 - y)
        far_x = to_neighbour(
            wa.at[pl.ds(2 * rows, shard), :], wa.at[pl.ds(3 * rows, shard), :], sends, receives, 4, "cx", 1 - x
        )
        far_y = to_neighbour(
            wa.at[pl.ds(rows + shard, shard), :],
            wa.at[pl.ds(3 * rows + shard, shard), :],
            sends,
            receives,
            5,
            "fsdp",
            1 - y,
        )

    def row_copies(j):
        here = pl.ds(pl.multiple_of(j * size, size), size)
        there = pl.ds(pl.multiple_of((j + steps) * size, size), size)
        return [
            pltpu.make_async_copy(nbuf.at[j], nrm.at[here, :], locals_.at[2 + j]),
            pltpu.make_async_copy(cbuf.at[j], cot_out.at[here, :], locals_.at[2 + steps + j]),
            to_neighbour(nbuf.at[j], nrm.at[there, :], sends, receives, 6 + j, "cc", 1 - core),
            to_neighbour(cbuf.at[j], cot_out.at[there, :], sends, receives, 6 + steps + j, "cc", 1 - core),
        ]

    @pl.when(i == 0)
    def _():
        barrier = pltpu.get_barrier_semaphore()
        for axis, at in peers:
            pl.semaphore_signal(barrier, inc=1, device_id={axis: at}, device_id_type=pl.DeviceIdType.MESH)
        load_up.start()
        load_down.start()
        for target, c, at in ((chip_a, core, mine), (away_a, 1 - core, pl.ds(0, shard))):
            cut = pl.ds(pl.multiple_of(c * width, width), width)
            for j in range(3):
                target[at, width * j : width * j + width] = in_ref[j, :, cut]
            target[at, 3 * width :] = out_ref[cut, :].astype(F32).T.astype(BF)
        pl.semaphore_wait(barrier, len(peers))
        swap_a.start()
        load_up.wait()
        load_down.wait()
        for target, c, at in ((away_m, 1 - core, pl.ds(0, shard)), (chip_m, core, mine)):
            cut = pl.ds(pl.multiple_of(c * wide, wide), wide)
            target[at, :wide] = up_ref[:, cut]
            target[at, wide:] = down_ref[cut, :].astype(F32).T.astype(BF)
            if target is away_m:
                swap_m.start()
                swap_a.wait()
                if square:
                    to_x.start()
                    to_y.start()
                keep_a.start()
        cot_sum[...] = jnp.zeros_like(cot_sum)

    center, _ = norm_parts(tok[...].astype(F32))
    full = (center * gain[...].astype(F32)[None] + shift[...].astype(F32)[None]).astype(BF)
    cot_sum[...] += jnp.sum(cot[...].astype(F32), axis=0, keepdims=True)
    for r in range(depth // chunk):
        place = ((r // 2 + y) % 2) * 2 + (r % 2 + x) % 2 if square else r
        lanes = pl.ds(pl.multiple_of(place * chunk, chunk), chunk) if square else pl.ds(r * chunk, chunk)
        nbuf[i, :, lanes] = full[:, r * chunk : r * chunk + chunk]
        cbuf[i, :, lanes] = cot[:, r * chunk : r * chunk + chunk]
    for copy in row_copies(i):
        copy.start()

    @pl.when(i == steps - 1)
    def _():
        swap_m.wait()
        keep_m.start()
        if square:
            to_y.wait()
            far_x.start()
            to_x.wait()
            far_y.start()
        keep_a.wait()
        keep_m.wait()

        def finish(j, c):
            for copy in row_copies(j):
                copy.wait()
            return c

        lax.fori_loop(0, steps, finish, 0)
        if square:
            far_x.wait()
            far_y.wait()


def begin(tokens, cot, gain, shift, in_proj, out_proj, up_proj, down_proj, chunk, square):
    length, depth = tokens.shape
    steps = 4
    size = length // steps
    shard = in_proj.shape[1]
    width, wide = in_proj.shape[2] // 2, up_proj.shape[1] // 2
    block = pl.BlockSpec((size, depth), lambda i: (i, 0))
    whole = lambda shape: pl.BlockSpec(shape, lambda i: (0,) * len(shape), pipeline_mode=pl.Buffered(1))
    rows = 8 * shard if square else 2 * shard
    return call(
        functools.partial(begin_body, chunk=chunk, square=square, steps=steps),
        "begin",
        (steps,),
        [block, block, whole((depth,)), whole((depth,)), whole(in_proj.shape), whole(out_proj.shape), ANY, ANY],
        [ANY, ANY, ANY, ANY, pl.BlockSpec((1, depth), lambda i: (0, 0))],
        [
            jax.ShapeDtypeStruct((2 * length, depth), BF),
            jax.ShapeDtypeStruct((2 * length, depth), BF),
            jax.ShapeDtypeStruct((rows, 4 * width), BF),
            jax.ShapeDtypeStruct((2 * shard, 2 * wide), BF),
            jax.ShapeDtypeStruct((1, depth), F32),
        ],
        [
            pltpu.VMEM((2 * shard, 4 * width), BF),
            pltpu.VMEM((shard, 4 * width), BF),
            pltpu.VMEM((2 * shard, 2 * wide), BF),
            pltpu.VMEM((shard, 2 * wide), BF),
            pltpu.VMEM(up_proj.shape, BF),
            pltpu.VMEM(down_proj.shape, BF),
            pltpu.VMEM((steps, size, depth), BF),
            pltpu.VMEM((steps, size, depth), BF),
            pltpu.SemaphoreType.DMA((2,)),
            pltpu.SemaphoreType.DMA((2 + 2 * steps,)),
            pltpu.SemaphoreType.DMA((6 + 2 * steps,)),
            pltpu.SemaphoreType.DMA((6 + 2 * steps,)),
        ],
        10 * tokens.size,
        16 * tokens.size,
        prefetch=0,
        collective=0,
    )(tokens, cot, gain, shift, in_proj, out_proj, up_proj, down_proj)


def rotary_tables(cos_rows, sin_rows):
    one = jnp.ones((HD - ROT, cos_rows.shape[1]), F32)
    none = jnp.zeros((HD - ROT, cos_rows.shape[1]), F32)
    few = jnp.zeros_like(cos_rows)
    return (
        jnp.concatenate([cos_rows, cos_rows, one] * 2, axis=0).T,
        jnp.concatenate([-sin_rows, few, none] * 2, axis=0).T,
        jnp.concatenate([few, sin_rows, none] * 2, axis=0).T,
    )


def turn(values, cos_part, down, up):
    return (
        values * cos_part
        + pltpu.roll(values, 128 - ROT // 2, 1) * down
        + pltpu.roll(values, ROT // 2, 1) * up
    )


def stay(shape):
    return pl.BlockSpec(shape, lambda i, s: (0,) * len(shape))


def piece_copies(pieces, columns, target, sems):
    copies, at = [], 0
    for n, piece in enumerate(pieces):
        count = piece.shape[0]
        copies.append(
            pltpu.make_async_copy(piece.at[:, columns], target.at[pl.ds(at, count), :], sems.at[n])
        )
        at += count
    return copies


def place_pieces(*jobs):
    copies = [copy for job in jobs for copy in piece_copies(*job)]
    for copy in copies:
        copy.start()
    for copy in copies:
        copy.wait()


def move_sems(pieces):
    return pltpu.SemaphoreType.DMA((len(pieces),))


def project_body(info, nrm, cot, weights, bias, cos_t, sin_t, q_out, kv_out, do_out, send, *, width):
    packed = dot(nrm[...], weights[:, : 3 * width]) + bias[...].astype(F32)
    do = dot(cot[...], weights[:, 3 * width :]).astype(BF)
    c, d, u = rotary_tables(cos_t[...], sin_t[...])
    low = []
    for p in range(2 * width // 128):
        low.append(turn(packed[:, 128 * p : 128 * p + 128], c, d, u).astype(BF))
    pairs = width // 128
    queries = jnp.concatenate(low[:pairs], axis=1)
    keys = jnp.concatenate(low[pairs:], axis=1)
    values = packed[:, 2 * width :].astype(BF)
    q_out[...] = queries
    kv_out[:, :width] = keys
    kv_out[:, width:] = values
    do_out[...] = do
    part = width // 2

    @pl.when(info[3] == 0)
    def _():
        send[:, :part] = keys[:, :part]
        send[:, part:] = values[:, :part]

    @pl.when(info[3] != 0)
    def _():
        send[:, :part] = queries[:, part:]
        send[:, part:] = do[:, part:]


def project(info, normed, cot, weights, bias, tables, width):
    rows, depth = normed.shape
    size = min(rows, 256)
    table = pl.BlockSpec((ROT // 2, size), lambda i, s: (0, i))
    return call(
        functools.partial(project_body, width=width),
        "project",
        (rows // size,),
        [row_block(size, depth)] * 2 + [fixed((depth, 4 * width)), fixed((1, 3 * width)), table, table],
        [row_block(size, width), row_block(size, 2 * width), row_block(size, width), row_block(size, width)],
        [jax.ShapeDtypeStruct((rows, n * width), BF) for n in (1, 2, 1, 1)],
        [],
        2 * rows * depth * 4 * width,
        2 * (2 * rows * depth + depth * 4 * width + 5 * rows * width),
    )(info, normed, cot, weights, bias, *tables)


def hidden_body(info, nrm, cot, bias, *rest, width, count):
    pieces, (act_out, grad_out, sum_out, weights, sems) = rest[:count], rest[count:]

    @pl.when(pl.program_id(0) == 0)
    def _():
        place_pieces((pieces, slice(0, 2 * width), weights, sems))
        sum_out[...] = jnp.zeros_like(sum_out)

    u = dot(nrm[...], weights[:, :width]) + bias[...].astype(F32)
    g = dot(cot[...], weights[:, width:])
    square = u * u
    t = jnp.tanh(GELU_A * (u + GELU_B * square * u))
    half = 0.5 * (1.0 + t)
    act_out[...] = (u * half).astype(BF)
    slope = half + 0.5 * u * (1.0 - t * t) * (GELU_A * (1.0 + 3.0 * GELU_B * square))
    low = (g * slope).astype(BF)
    grad_out[...] = low
    sum_out[...] += jnp.sum(low.astype(F32), axis=0, keepdims=True)


def hidden(info, normed, cot, pieces, bias, width):
    rows, depth = normed.shape
    size = min(rows, 256)
    return call(
        functools.partial(hidden_body, width=width, count=len(pieces)),
        "hidden",
        (rows // size,),
        [row_block(size, depth)] * 2 + [fixed((1, width))] + [ANY] * len(pieces),
        [row_block(size, width), row_block(size, width), stay((1, width))],
        [jax.ShapeDtypeStruct((rows, width), BF)] * 2 + [jax.ShapeDtypeStruct((1, width), F32)],
        [pltpu.VMEM((depth, 2 * width), BF), move_sems(pieces)],
        4 * rows * depth * width,
        2 * (2 * rows * depth + 2 * depth * width + 2 * rows * width),
    )(info, normed, cot, bias, *pieces)


def spread_body(a, b, *rest, counts, columns, sums, per):
    na, nb = counts
    wa, wb = rest[:na], rest[na : na + nb]
    rest = rest[na + nb :]
    normed = rest[:sums]
    out = rest[sums]
    totals = rest[sums + 1 : 3 * sums + 1]
    hold_a, hold_b, sem_a, sem_b, outgoing, incoming, send_sems, recv_sems = rest[3 * sums + 1 :]
    i = pl.program_id(0)
    core = lax.axis_index("cc")

    def copy(j):
        return pltpu.make_async_remote_copy(
            src_ref=outgoing.at[j],
            dst_ref=incoming.at[j],
            send_sem=send_sems.at[j],
            recv_sem=recv_sems.at[j],
            device_id={"cc": 1 - core},
            device_id_type=pl.DeviceIdType.MESH,
        )

    @pl.when(i == 0)
    def _():
        barrier = pltpu.get_barrier_semaphore()
        pl.semaphore_signal(barrier, inc=1, device_id={"cc": 1 - core}, device_id_type=pl.DeviceIdType.MESH)
        place_pieces((wa, columns[0], hold_a, sem_a), (wb, columns[1], hold_b, sem_b))
        pl.semaphore_wait(barrier, 1)
        for total in totals:
            total[...] = jnp.zeros_like(total)

    total = dot(a[...], hold_a[...], NT) + dot(b[...], hold_b[...], NT)

    @pl.when(i < per)
    def _():
        outgoing[i] = total.astype(BF)
        copy(i).start()

    @pl.when(i >= per)
    def _():
        copy(i - per).wait()
        full = total + incoming[i - per].astype(F32)
        out[...] = full.astype(BF)
        if sums:
            totals[0][...] += jnp.sum(full * normed[0][...].astype(F32), axis=0, keepdims=True)
            totals[1][...] += jnp.sum(full, axis=0, keepdims=True)


def spread(a, b, wa, wb, ca, cb, depth, name, collective, normed=()):
    rows = a.shape[0] // 2
    size = min(rows, 256)
    per = rows // size
    at = lambda width: pl.BlockSpec((size, width), lambda i: ((i + per) % (2 * per), 0))
    later = pl.BlockSpec((size, depth), lambda i: (jnp.maximum(i - per, 0), 0))
    one = pl.BlockSpec((1, depth), lambda i: (0, 0))
    wide_a, wide_b = a.shape[1], b.shape[1]
    count = len(normed)
    return call(
        functools.partial(
            spread_body,
            counts=(len(wa), len(wb)),
            columns=(slice(ca, ca + wide_a), slice(cb, cb + wide_b)),
            sums=count,
            per=per,
        ),
        name,
        (2 * per,),
        [at(wide_a), at(wide_b)] + [ANY] * (len(wa) + len(wb)) + [later] * count,
        [later] + [one] * (2 * count),
        [jax.ShapeDtypeStruct((rows, depth), BF)] + [jax.ShapeDtypeStruct((1, depth), F32)] * (2 * count),
        [
            pltpu.VMEM((depth, wide_a), BF),
            pltpu.VMEM((depth, wide_b), BF),
            move_sems(wa),
            move_sems(wb),
            pltpu.VMEM((per, size, depth), BF),
            pltpu.VMEM((per, size, depth), BF),
            pltpu.SemaphoreType.DMA((per,)),
            pltpu.SemaphoreType.DMA((per,)),
        ],
        4 * rows * depth * (wide_a + wide_b),
        2 * (2 * rows + depth) * (wide_a + wide_b) + 2 * rows * depth,
        prefetch=0,
        collective=collective,
    )(a, b, *wa, *wb, *normed)


def outer_body(info, left_n, left_c, right_n, right_c, *rest, steps, out_steps):
    i = pl.program_id(0)
    outs = rest[:-3]
    hold_n, hold_c, sems = rest[-3:]
    load_n = pltpu.make_async_copy(right_n, hold_n, sems.at[0])
    load_c = pltpu.make_async_copy(right_c, hold_c, sems.at[1])

    @pl.when(i == 0)
    def _():
        load_n.start()
        load_c.start()
        load_n.wait()

    @pl.when(i == steps)
    def _():
        load_c.wait()

    for n, (start, stop) in enumerate(out_steps):
        left, right = (left_n, hold_n) if stop <= steps else (left_c, hold_c)

        @pl.when((i >= start) & (i < stop))
        def _(left=left, right=right, out=outs[n]):
            out[...] = dot(left[...], right[...], TN).astype(BF)


def outer(info, normed, cot, right_n, right_c, groups_n, groups_c, chunk, name):
    rows = right_n.shape[0]
    wide_n, wide_c = right_n.shape[1], right_c.shape[1]
    size = min(chunk, 512)
    per = chunk // size
    order_n = [block for group in groups_n for block in group]
    order_c = [block for group in groups_c for block in group]
    steps = len(order_n) * per

    def column(order, offset):
        def place(i, s):
            at = jnp.clip(i - offset, 0, steps - 1)
            block = order[-1]
            for k in range(len(order) - 1):
                block = jnp.where(at // per == k, order[k], block)
            return (0, block * per + at % per)

        return pl.BlockSpec((rows, size), place)

    out_specs, out_shapes, out_steps = [], [], []
    start = 0
    for groups, wide in ((groups_n, wide_n), (groups_c, wide_c)):
        for group in groups:
            count = len(group) * per
            out_specs.append(
                pl.BlockSpec((size, wide), lambda i, s, start=start, count=count: (jnp.clip(i - start, 0, count - 1), 0))
            )
            out_shapes.append(jax.ShapeDtypeStruct((count * size, wide), BF))
            out_steps.append((start, start + count))
            start += count
    return call(
        functools.partial(outer_body, steps=steps, out_steps=tuple(out_steps)),
        name,
        (2 * steps,),
        [column(order_n, 0), column(order_c, steps), ANY, ANY],
        out_specs,
        out_shapes,
        [pltpu.VMEM((rows, wide_n), BF), pltpu.VMEM((rows, wide_c), BF), pltpu.SemaphoreType.DMA((2,))],
        2 * rows * steps * size * (wide_n + wide_c),
        2 * (2 * rows * steps * size + (rows + steps * size) * (wide_n + wide_c)),
    )(info, normed, cot, right_n, right_c)


def head_masks(block, scale):
    lane = lax.broadcasted_iota(jnp.int32, block.shape, 1)
    v = block.astype(F32) * scale
    return (jnp.where(lane < HD, v, 0.0).astype(BF), jnp.where(lane < HD, 0.0, v).astype(BF))


def own_mask(flag, width):
    kk = lax.broadcasted_iota(jnp.int32, (RUN, width), 0)
    qq = lax.broadcasted_iota(jnp.int32, (RUN, width), 1)
    return kk <= qq + flag * RUN


def each_prefix(here, half, runs, work):
    size = runs // 2
    while size:

        @pl.when((here & size) != 0)
        def _(size=size):
            low = here & ((runs - 1) & ~(2 * size - 1))
            work(pl.multiple_of((low ^ half) * RUN, RUN), size * RUN)

        size //= 2


def softmax_blocks(state, heads, k_r, vt_r, qm, start, size, mask=None):
    acc, ml = state

    def score(n):
        p, h = divmod(n, 2)
        s = dot(k_r[pl.ds(start, size), 128 * p : 128 * p + 128], qm[p][h], NT)
        return s if mask is None else jnp.where(mask, s, NEG)

    def rest(n, s):
        top = jnp.max(s, axis=0, keepdims=True)
        rows = slice(HD * n, HD * n + HD)
        vb = vt_r[rows, pl.ds(start, size)]
        m = ml[n : n + 1, :]
        new = jnp.maximum(m, top)
        alpha = jnp.exp(m - new)
        e = jnp.exp(s - new)
        ml[n : n + 1, :] = new
        ml[heads + n : heads + n + 1, :] = ml[heads + n : heads + n + 1, :] * alpha + jnp.sum(e, axis=0, keepdims=True)
        acc[rows, :] = acc[rows, :] * alpha + dot(vb, e.astype(BF))

    s = score(0)
    for n in range(heads):
        following = score(n + 1) if n + 1 < heads else None
        rest(n, s)
        s = following


def start_state(acc, ml, heads):
    acc[...] = jnp.zeros_like(acc)
    ml[:heads, :] = jnp.full((heads, ml.shape[1]), NEG, F32)
    ml[heads:, :] = jnp.zeros((heads, ml.shape[1]), F32)


def finish_state(acc, ml, heads, n):
    l = ml[heads + n : heads + n + 1, :]
    return acc[HD * n : HD * n + HD, :] / l, ml[n : n + 1, :] + jnp.log(l)


def query_masks(block, scale):
    return [head_masks(block[:, 128 * p : 128 * p + 128], scale) for p in range(block.shape[1] // 128)]


SCALE = 1.0 / math.sqrt(HD)


def local_body(info, q_ref, k_ref, v_ref, out_ref, lse_ref, vt, acc, ml, *, heads):
    i = pl.program_id(0)
    half = info[0]
    runs = k_ref.shape[0] // RUN

    @pl.when(i == 0)
    def _():
        vt[...] = v_ref[...].astype(F32).T.astype(BF)

    qm = query_masks(q_ref[...], SCALE)
    start_state(acc, ml, heads)
    work = lambda start, size, mask=None: softmax_blocks((acc, ml), heads, k_ref, vt, qm, start, size, mask)
    work(pl.multiple_of(i * RUN, RUN), RUN, own_mask(info[2 + i], q_ref.shape[0]))
    each_prefix(i ^ half, half, runs, work)
    for n in range(heads):
        out_ref[HD * n : HD * n + HD, :], lse_ref[n : n + 1, :] = finish_state(acc, ml, heads, n)


def attend_local(info, q, kv):
    rows, width = q.shape
    heads = width // HD
    columns = lambda count: pl.BlockSpec((count, RUN), lambda i, s: (0, i))
    return call(
        functools.partial(local_body, heads=heads),
        "attend_local",
        (rows // RUN,),
        [row_block(RUN, width), fixed((rows, width)), fixed((rows, width), (0, 1))],
        [columns(width), columns(heads)],
        [jax.ShapeDtypeStruct((width, rows), F32), jax.ShapeDtypeStruct((heads, rows), F32)],
        [pltpu.VMEM((width, rows), BF), pltpu.VMEM((width, RUN), F32), pltpu.VMEM((2 * heads, RUN), F32)],
        25e9,
        14 * rows * width,
    )(info, q, kv, kv)


def cross_body(info, q_ref, came_ref, came0, came1, k_ref, v_ref, out_ref, lse_ref, keys, vt, acc, ml, *, heads, cut):
    late = info[1] > 0

    @pl.when(pl.program_id(0) == 0)
    def _():
        keys[...] = jnp.where(late, came0[...], k_ref[...])
        vt[...] = jnp.where(late, came1[...], v_ref[...]).astype(F32).T.astype(BF)

    qm = query_masks(jnp.where(late, q_ref[...], came_ref[...]), SCALE)
    start_state(acc, ml, heads)
    for j in range(keys.shape[0] // cut):
        softmax_blocks((acc, ml), heads, keys, vt, qm, j * cut, cut)
    for n in range(heads):
        out, lse_ref[n : n + 1, :] = finish_state(acc, ml, heads, n)
        out_ref[HD * n : HD * n + HD, :] = out.astype(BF)


def cross_specs(rows, part):
    own = lambda i, s: (i, 1 - s[1])
    return (
        pl.BlockSpec((RUN, part), own),
        pl.BlockSpec((RUN, part), lambda i, s: (i, 0)),
        fixed((rows, part)),
        fixed((rows, part), (0, 1)),
        pl.BlockSpec((rows, part), lambda i, s: (0, 1 - s[1])),
        pl.BlockSpec((rows, part), lambda i, s: (0, 3 - s[1])),
    )


def attend_cross(info, q, came, kv):
    rows, part = q.shape[0], q.shape[1] // 2
    heads = part // HD
    query, came_block, came0, came1, key, value = cross_specs(rows, part)
    columns = lambda count: pl.BlockSpec((count, RUN), lambda i, s: (0, i))
    return call(
        functools.partial(cross_body, heads=heads, cut=min(rows, 1024)),
        "attend_cross",
        (rows // RUN,),
        [query, came_block, came0, came1, key, value],
        [columns(part), columns(heads)],
        [jax.ShapeDtypeStruct((part, rows), BF), jax.ShapeDtypeStruct((heads, rows), F32)],
        [
            pltpu.VMEM((rows, part), BF),
            pltpu.VMEM((part, rows), BF),
            pltpu.VMEM((part, RUN), F32),
            pltpu.VMEM((2 * heads, RUN), F32),
        ],
        15e9,
        14 * rows * part,
    )(info, q, came, came, came, kv, kv)


def merge_body(info, local, lse_local, mine, lse_mine, came, lse_came, do_ref, att_ref, stat_ref, *, heads):
    late = info[1] > 0
    part = heads // 2
    size = do_ref.shape[0]
    do_t = do_ref[...].astype(F32).T
    outs = []
    for n in range(heads):
        other, lse_other, m = (mine, lse_mine, n) if n < part else (came, lse_came, n - part)
        rows = slice(HD * n, HD * n + HD)
        ours = lse_local[n : n + 1, :]
        theirs = jnp.where(late, lse_other[m : m + 1, :], jnp.full((1, size), NEG, F32))
        top = jnp.maximum(ours, theirs)
        a, b = jnp.exp(ours - top), jnp.exp(theirs - top)
        total = a + b
        o = (local[rows, :] * a + other[HD * m : HD * m + HD, :].astype(F32) * b) / total
        outs.append(o)
        stat_ref[n : n + 1, :] = top + jnp.log(total)
        stat_ref[heads + n : heads + n + 1, :] = jnp.sum(o * do_t[rows, :], axis=0, keepdims=True)
    att_ref[...] = jnp.concatenate(outs, axis=0).T.astype(BF)


def merge(info, local, lse_local, mine, lse_mine, came, lse_came, do):
    rows, width = do.shape
    heads = width // HD
    size = min(rows, 512)
    columns = lambda count: pl.BlockSpec((count, size), lambda i, s: (0, i))
    return call(
        functools.partial(merge_body, heads=heads),
        "merge",
        (rows // size,),
        [columns(width), columns(heads)] + [columns(width // 2), columns(heads // 2)] * 2 + [row_block(size, width)],
        [row_block(size, width), columns(2 * heads)],
        [jax.ShapeDtypeStruct((rows, width), BF), jax.ShapeDtypeStruct((2 * heads, rows), F32)],
        [],
        20 * rows * width,
        10 * rows * width,
    )(info, local, lse_local, mine, lse_mine, came, lse_came, do)


def gradient_blocks(heads, k_r, v_r, kt_r, dk_r, dv_r, dqt, qm, dm, stat, start, size, mask=None):
    def products(n):
        p, h = divmod(n, 2)
        lanes = slice(128 * p, 128 * p + 128)
        return (
            dot(k_r[pl.ds(start, size), lanes], qm[p][h], NT),
            dot(v_r[pl.ds(start, size), lanes], dm[p][h], NT),
        )

    def rest(n, s, g):
        p, h = divmod(n, 2)
        e = jnp.exp(s - stat[n : n + 1, :])
        if mask is not None:
            e = jnp.where(mask, e, 0.0)
        ds = (e * (g - stat[heads + n : heads + n + 1, :])).astype(BF)
        rows = slice(HD * n, HD * n + HD)
        dqt[rows, :] += dot(kt_r[rows, pl.ds(start, size)], ds)
        return dot(ds, qm[p][h]), dot(e.astype(BF), dm[p][h])

    now = products(0)
    before = None
    for n in range(heads):
        following = products(n + 1) if n + 1 < heads else None
        grads = rest(n, *now)
        now = following
        if n % 2:
            lanes = slice(HD * (n - 1), HD * (n + 1))
            dk_r[pl.ds(start, size), lanes] += before[0] + grads[0]
            dv_r[pl.ds(start, size), lanes] += before[1] + grads[1]
        before = grads


def local_back_body(info, q_ref, do_ref, stat_ref, k_ref, v_ref, dqx, dkx, dvx, came_q, came_k, came_v, cos_t, sin_t, out, sums, kt, dqt, dk, dv, *, heads):
    i = pl.program_id(0)
    half = info[0]
    late = info[1] > 0
    runs = k_ref.shape[0] // RUN
    width = HD * heads
    part = width // 2

    @pl.when(i == 0)
    def _():
        kt[...] = k_ref[...].astype(F32).T.astype(BF)

    @pl.when((i == 0) & late)
    def _():
        dk[...] = jnp.zeros_like(dk)
        dv[...] = jnp.zeros_like(dv)

    @pl.when((i == 0) & jnp.logical_not(late))
    def _():
        dk[:, :part] = came_k[...].astype(F32)
        dk[:, part:] = dkx[...]
        dv[:, :part] = came_v[...].astype(F32)
        dv[:, part:] = dvx[...]

    qm = query_masks(q_ref[...], SCALE)
    dm = query_masks(do_ref[...], 1.0)
    dqt[...] = jnp.zeros_like(dqt)

    def work(start, size, mask=None):
        gradient_blocks(heads, k_ref, v_ref, kt, dk, dv, dqt, qm, dm, stat_ref, start, size, mask)

    work(pl.multiple_of(i * RUN, RUN), RUN, own_mask(info[2 + i], q_ref.shape[0]))
    each_prefix(i ^ half, half, runs, work)
    zero = jnp.zeros((q_ref.shape[0], part), F32)
    more = jnp.concatenate(
        [jnp.where(late, dqx[...], zero), jnp.where(late, came_q[...].astype(F32), zero)], axis=1
    )
    found = (dqt[...] * SCALE).T + more
    rows = pl.ds(pl.multiple_of(i * RUN, RUN), RUN)
    c, d, u = rotary_tables(cos_t[:, rows], -sin_t[:, rows])
    for p in range(width // 128):
        lanes = slice(128 * p, 128 * p + 128)
        out[rows, lanes] = turn(found[:, lanes], c, d, u).astype(BF)

    @pl.when(i == pl.num_programs(0) - 1)
    def _():
        def step(j, c):
            at = pl.ds(pl.multiple_of(j * RUN, RUN), RUN)
            c2, d2, u2 = rotary_tables(cos_t[:, at], -sin_t[:, at])
            for p in range(width // 128):
                lanes = slice(128 * p, 128 * p + 128)
                shifted = slice(width + 128 * p, width + 128 * p + 128)
                out[at, shifted] = turn(dk[at, lanes], c2, d2, u2).astype(BF)
            out[at, 2 * width :] = dv[at, :].astype(BF)
            return c + jnp.sum(out[at, :].astype(F32), axis=0, keepdims=True)

        sums[...] = lax.fori_loop(0, runs, step, jnp.zeros((1, 3 * width), F32))


def back_local(info, q, do, stat, kv, cross, came, tables):
    rows, width = q.shape
    heads = width // HD
    part = width // 2
    blk = row_block(RUN, width)
    few = row_block(RUN, part)
    return call(
        functools.partial(local_back_body, heads=heads),
        "back_local",
        (rows // RUN,),
        [
            blk,
            blk,
            pl.BlockSpec((2 * heads, RUN), lambda i, s: (0, i)),
            fixed((rows, width)),
            fixed((rows, width), (0, 1)),
            few,
            fixed((rows, part)),
            fixed((rows, part)),
            few,
            fixed((rows, part)),
            fixed((rows, part), (0, 1)),
            fixed((ROT // 2, rows)),
            fixed((ROT // 2, rows)),
        ],
        [stay((rows, 3 * width)), stay((1, 3 * width))],
        [jax.ShapeDtypeStruct((rows, 3 * width), BF), jax.ShapeDtypeStruct((1, 3 * width), F32)],
        [
            pltpu.VMEM((width, rows), BF),
            pltpu.VMEM((width, RUN), F32),
            pltpu.VMEM((rows, width), F32),
            pltpu.VMEM((rows, width), F32),
        ],
        40e9,
        20 * rows * width,
    )(info, q, do, stat, kv, kv, *cross, came, came, came, *tables)


def cross_back_body(info, q_ref, do_ref, came_q, came_do, came0, came1, k_ref, v_ref, stat_ref, dq_ref, dk_ref, dv_ref, send, keys, values, kt, dqt, *, heads, cut):
    late = info[1] > 0
    i = pl.program_id(0)
    part = HD * heads

    @pl.when(i == 0)
    def _():
        chosen = jnp.where(late, came0[...], k_ref[...])
        keys[...] = chosen
        kt[...] = chosen.astype(F32).T.astype(BF)
        values[...] = jnp.where(late, came1[...], v_ref[...])
        dk_ref[...] = jnp.zeros_like(dk_ref)
        dv_ref[...] = jnp.zeros_like(dv_ref)

    qm = query_masks(jnp.where(late, q_ref[...], came_q[...]), SCALE)
    dm = query_masks(jnp.where(late, do_ref[...], came_do[...]), 1.0)
    dqt[...] = jnp.zeros_like(dqt)
    for j in range(keys.shape[0] // cut):
        gradient_blocks(heads, keys, values, kt, dk_ref, dv_ref, dqt, qm, dm, stat_ref, j * cut, cut)
    found = (dqt[...] * SCALE).T
    dq_ref[...] = found
    rows = pl.ds(pl.multiple_of(i * RUN, RUN), RUN)

    @pl.when(jnp.logical_not(late))
    def _():
        send[rows, :part] = found.astype(BF)
        send[rows, part:] = found.astype(BF)

    @pl.when(late & (i == pl.num_programs(0) - 1))
    def _():
        send[:, :part] = dk_ref[...].astype(BF)
        send[:, part:] = dv_ref[...].astype(BF)


def back_cross(info, q, do, came, kv, stat):
    rows, part = q.shape[0], q.shape[1] // 2
    heads = part // HD
    query, came_block, came0, came1, key, value = cross_specs(rows, part)
    acc = jax.ShapeDtypeStruct((rows, part), F32)
    return call(
        functools.partial(cross_back_body, heads=heads, cut=min(rows, 1024)),
        "back_cross",
        (rows // RUN,),
        [
            query,
            query,
            came_block,
            pl.BlockSpec((RUN, part), lambda i, s: (i, 1)),
            came0,
            came1,
            key,
            value,
            pl.BlockSpec((2 * heads, RUN), lambda i, s: (0, i)),
        ],
        [row_block(RUN, part), stay((rows, part)), stay((rows, part)), stay((rows, 2 * part))],
        [acc, acc, acc, jax.ShapeDtypeStruct((rows, 2 * part), BF)],
        [
            pltpu.VMEM((rows, part), BF),
            pltpu.VMEM((rows, part), BF),
            pltpu.VMEM((part, rows), BF),
            pltpu.VMEM((part, RUN), F32),
        ],
        25e9,
        20 * rows * part,
    )(info, q, do, came, came, came, came, kv, kv, stat)


def input_body(info, grad, tok, cot, gain, out, *, chunk):
    xhat, inverse = norm_parts(tok[...].astype(F32))
    parts = [grad[:, lanes_of(info, chunk, r)] for r in range(tok.shape[1] // chunk)]
    e = jnp.concatenate(parts, axis=1).astype(F32) * gain[...].astype(F32)
    mean_e = jnp.mean(e, axis=-1, keepdims=True)
    mean_ex = jnp.mean(e * xhat, axis=-1, keepdims=True)
    out[...] = (cot[...].astype(F32) + (e - mean_e - xhat * mean_ex) * inverse).astype(BF)


def input_grads(info, grad, tok, cot, gain, chunk):
    rows, width = grad.shape
    steps = 4
    size = rows // steps
    share = pl.BlockSpec((size, width), lambda i, s: (s[1] * steps + i, 0))
    return call(
        functools.partial(input_body, chunk=chunk),
        "input_grad",
        (steps,),
        [row_block(size, width), share, share, fixed((1, width))],
        [row_block(size, width)],
        [jax.ShapeDtypeStruct((rows, width), BF)],
        [],
        20 * rows * width,
        8 * rows * width,
    )(info, grad, tok, cot, gain[None])[0]


def layer_body(info, branch, tok, bias, out, *, chunk):
    for r in range(tok.shape[1] // chunk):
        at = slice(r * chunk, r * chunk + chunk)
        part = branch[:, lanes_of(info, chunk, r)].astype(F32)
        out[:, at] = (tok[:, at].astype(F32) + part + bias[:, at].astype(F32)).astype(BF)


def layer_rows(info, branch, tok, bias, chunk):
    rows, width = branch.shape
    return call(
        functools.partial(layer_body, chunk=chunk),
        "layer_out",
        (1,),
        [row_block(rows, width), pl.BlockSpec((rows, width), lambda i, s: (s[1], 0)), fixed((1, width))],
        [row_block(rows, width)],
        [jax.ShapeDtypeStruct((rows, width), BF)],
        [],
        4 * branch.size,
        6 * branch.size,
    )(info, branch, tok, bias[None])[0]


def body(tokens, cotangent, piece_ids, positions, norm_gain, norm_shift, in_proj, in_bias, out_proj, up_proj, up_bias, down_proj, out_bias):
    length, depth = tokens.shape
    width = in_bias.shape[1] // 2
    hidden_width = up_bias.shape[0] // 2
    f_count, z_count = lax.axis_size("fsdp"), lax.axis_size("tp")
    x_at, c_at, f_at = lax.axis_index("cx"), lax.axis_index("cc"), lax.axis_index("fsdp")
    square = f_count == 2
    chips = 2 * f_count
    chunk = depth // chips
    me = f_at * 2 + x_at if square else 0 * f_at
    info = jnp.stack([me, lax.axis_index("tp"), c_at, x_at]).astype(jnp.int32)

    other_core = lambda value: lax.ppermute(value, "cc", SWAP)
    by_x = lambda value: lax.ppermute(value, "cx", SWAP)
    by_y = lambda value: lax.ppermute(value, "fsdp", SWAP)

    def pick(value, index, size, axis):
        return lax.dynamic_slice_in_dim(value, index * size, size, axis)

    def in_order(mine, theirs, axis):
        return jnp.where(c_at == 0, jnp.concatenate([mine, theirs], axis), jnp.concatenate([theirs, mine], axis))

    def after(value, *earlier):
        return lax.optimization_barrier((value,) + earlier)[0]

    shard = in_proj.shape[1]
    normed, cot, weights_a, value_m, cot_sum = begin(
        tokens, cotangent, norm_gain, norm_shift, in_proj, out_proj, up_proj, down_proj, chunk, square
    )
    if not square:
        weights_a = lax.all_gather(weights_a, ("fsdp", "cx"), axis=0, tiled=True)
        weights_m = [lax.all_gather(value_m, ("fsdp", "cx"), axis=0, tiled=True)]
    small = jnp.stack([piece_ids, positions])
    small = jnp.concatenate([small, other_core(small)], axis=1)
    pieces, places = small[0], small[1]

    frequency = 10000.0 ** (-2.0 * jnp.arange(ROT // 2, dtype=F32) / ROT)
    angles = frequency[:, None] * places.astype(F32)[None, :]
    tables = (jnp.cos(angles), jnp.sin(angles))
    bias_a = pick(in_bias, c_at, width, 1).reshape(1, 3 * width)
    bias_m = pick(up_bias, c_at, hidden_width, 0)[None]
    flags = (pieces.reshape(-1, RUN)[:, 0] > 0).astype(jnp.int32)
    scene = jnp.concatenate([jnp.stack([c_at * (length // RUN), x_at]).astype(jnp.int32), flags])

    if square:
        x_first, y_m = by_x(value_m[:shard]), by_y(value_m)
    queries, kv, grad_att, send = project(info, normed, cot, weights_a, bias_a, tables, width)
    came = by_x(send)
    local, lse_local = attend_local(scene, after(queries, x_first) if square else queries, kv)
    mine, lse_mine = attend_cross(scene, after(queries, local), came, kv)
    if square:
        x_second = by_x(after(value_m[shard:], local))
        y_back = by_y(x_first)
    forward_x = lambda value: lax.ppermute(value, "cx", [(0, 1)])
    attended, stat = merge(
        scene,
        after(local, x_second) if square else local,
        lse_local,
        mine,
        lse_mine,
        forward_x(mine),
        forward_x(lse_mine),
        grad_att,
    )
    heads = width // HD
    part = heads // 2
    stat_early = jnp.concatenate([stat[:part], stat[heads : heads + part]], axis=0)
    stat_late = jnp.concatenate([stat[part:heads], stat[heads + part :]], axis=0)
    stat_cross = jnp.where(x_at == 1, stat_early, lax.ppermute(stat_late, "cx", [(1, 0)]))
    if square:
        weights_m = [value_m, x_first, x_second, y_m, y_back, by_x(after(y_m[shard:], stat_cross))]
    *cross, outgoing = back_cross(
        scene, after(queries, y_back) if square else queries, grad_att, came, kv, stat_cross
    )
    returned = by_x(outgoing)
    active, grad_up, up_sum = hidden(info, normed, cot, weights_m, after(bias_m, outgoing), hidden_width)

    def scatter(value):
        return lax.psum_scatter(value, ("fsdp", "cx"), scatter_dimension=0, tiled=True)

    def grads_of(after_this, right_n, right_c, name):
        left = after(normed, after_this)
        if square:
            return outer(info, left, cot, right_n, right_c, ((1, 3), (2, 0)), ((2, 3), (1, 0)), chunk, name)
        every = (tuple(range(chips)),)
        return outer(info, left, cot, right_n, right_c, every, every, chunk, name)

    def add(*values):
        return functools.reduce(lambda a, b: a + b, [value.astype(F32) for value in values])

    columns = (3 * width, hidden_width)
    (ours,) = spread(after(attended, active), active, [weights_a], weights_m, *columns, depth, "branch", 1)
    branch = lax.psum_scatter(ours, "tp", scatter_dimension=0, tiled=True)
    hidden_grads = grads_of(ours, grad_up, active, "hidden_grads")
    last = hidden_grads[-1]
    if square:
        up_away, up_held, down_away, down_held = hidden_grads
        up_came, down_came = by_x(up_away), by_y(down_away)
    grad_packed, in_sum = back_local(scene, after(queries, last), grad_att, stat, kv, cross, returned, tables)
    ours, gain_part, shift_part = spread(
        after(grad_packed, up_came, down_came) if square else grad_packed, grad_up, [weights_a], weights_m, 0, 0, depth, "normed_grad", 2, (normed,)
    )
    grad_normed = lax.psum_scatter(ours, "tp", scatter_dimension=0, tiled=True)
    if square:
        up_pass = add(after(up_held[:chunk], ours), up_came[chunk:]).astype(BF)
        down_pass = add(after(down_held[:chunk], ours), down_came[chunk:]).astype(BF)
        up_last, down_last = by_y(up_pass), by_x(down_pass)
    packed_grads = grads_of([up_pass, down_pass] if square else ours, grad_packed, attended, "packed_grads")
    def keep(rows):
        size = rows.shape[0] // 2
        mine, theirs = pick(rows, c_at, size, 0).astype(F32), pick(rows, 1 - c_at, size, 0).astype(BF)
        came = other_core(theirs).astype(F32)
        return jnp.where(c_at == 0, jnp.stack([mine, came]), jnp.stack([came, mine]))

    def hidden_outputs(up_rows, down_rows):
        up_two, down_two = keep(up_rows), keep(down_rows)
        return (
            jnp.transpose(up_two, (1, 0, 2)).reshape(shard, 2 * hidden_width),
            jnp.transpose(down_two, (0, 2, 1)).reshape(2 * hidden_width, shard),
        )

    def packed_outputs(in_rows, out_rows):
        in_two, out_two = keep(in_rows), keep(out_rows)
        return (
            jnp.transpose(in_two.reshape(2, shard, 3, width), (2, 1, 0, 3)).reshape(3, shard, 2 * width),
            jnp.transpose(out_two, (0, 2, 1)).reshape(2 * width, shard),
        )

    if square:
        in_away, in_held, out_away, out_held = packed_grads
        in_came, out_came = by_x(in_away), by_y(out_away)
        layer_out = layer_rows(info, after(branch, in_away, up_last, down_last), tokens, out_bias, chunk)
        up_rows = add(after(up_held[chunk:], layer_out), up_came[:chunk], up_last)
        down_rows = add(after(down_held[chunk:], layer_out), down_came[:chunk], down_last)
        upproj_grad, downproj_grad = hidden_outputs(up_rows, down_rows)
        in_pass = add(after(in_held[:chunk], upproj_grad, downproj_grad), in_came[chunk:]).astype(BF)
        out_pass = add(after(out_held[:chunk], layer_out), out_came[chunk:]).astype(BF)
        in_last, out_last = by_y(in_pass), by_x(out_pass)
        in_rows = add(in_held[chunk:], in_came[:chunk], in_last)
        out_rows = add(out_held[chunk:], out_came[:chunk], out_last)
        inproj_grad, outproj_grad = packed_outputs(in_rows, out_rows)
    else:
        upproj_grad, downproj_grad = hidden_outputs(*[scatter(value) for value in hidden_grads])
        inproj_grad, outproj_grad = packed_outputs(*[scatter(value) for value in packed_grads])
        layer_out = layer_rows(info, branch, tokens, out_bias, chunk)
    input_grad = input_grads(info, grad_normed, tokens, cotangent, norm_gain, chunk)

    def to_plain(row):
        if not square:
            return row
        return jnp.concatenate([pick(row, r ^ me, chunk, 1) for r in range(chips)], axis=1)

    shift_sum = to_plain(shift_part)
    gain_sum = (to_plain(gain_part) - shift_sum * norm_shift.astype(F32)[None]) / norm_gain.astype(F32)[None]
    once = jnp.where(lax.axis_index("tp") == 0, cot_sum, 0.0)
    all_wide = jnp.concatenate([gain_sum, shift_sum, once], axis=1)
    narrow = jnp.concatenate([in_sum, up_sum], axis=1)
    wide_size = all_wide.shape[1]
    both = jnp.concatenate([all_wide, narrow], axis=1)
    if square:
        both = both + by_x(both)
        both = both + by_y(both)
    else:
        both = lax.psum(both, ("fsdp", "cx"))
    swapped = other_core(both)
    wide = both[:, :wide_size] + swapped[:, :wide_size]
    step = 1
    while step < z_count:
        wide = wide + lax.ppermute(wide, "tp", [(z, z ^ step) for z in range(z_count)])
        step *= 2
    gain_grad, shift_grad, outbias_grad = [wide[0, depth * j : depth * j + depth] for j in range(3)]
    narrow_pair = in_order(both[:, wide_size:], swapped[:, wide_size:], 0)
    inbias_grad = jnp.transpose(narrow_pair[:, : 3 * width].reshape(2, 3, width), (1, 0, 2)).reshape(3, 2 * width)
    upbias_grad = narrow_pair[:, 3 * width :].reshape(2 * hidden_width)

    return (
        layer_out,
        input_grad,
        gain_grad,
        shift_grad,
        inproj_grad,
        inbias_grad,
        outproj_grad,
        upproj_grad,
        upbias_grad,
        downproj_grad,
        outbias_grad,
    )


def solution(mesh):
    sizes = mesh.shape
    split = Mesh(
        mesh.devices.reshape(sizes["fsdp"], sizes["ctx"] // 2, 2, sizes["tp"]), ("fsdp", "cx", "cc", "tp")
    )
    group = ("fsdp", "cx", "cc")
    return jax.shard_map(
        body,
        mesh=split,
        in_specs=(
            P(group, None),
            P(group, None),
            P(group),
            P(group),
            P(),
            P(),
            P(None, group, "tp"),
            P(None, "tp"),
            P("tp", group),
            P(group, "tp"),
            P("tp"),
            P("tp", group),
            P(),
        ),
        out_specs=(
            P(group + ("tp",), None),
            P(group + ("tp",), None),
            P(),
            P(),
            P(None, group, "tp"),
            P(None, "tp"),
            P("tp", group),
            P(group, "tp"),
            P("tp"),
            P("tp", group),
            P(),
        ),
        check_vma=False,
    )
```

```python
import functools
import math

import jax
import jax.numpy as jnp
from jax import lax
from jax.experimental import pallas as pl
from jax.experimental.pallas import tpu as pltpu
from jax.sharding import Mesh
from jax.sharding import PartitionSpec as P

HD = 64
ROT = 32
RUN = 256
EPS = 1e-05
NEG = -1e30
F32 = jnp.float32
BF = jnp.bfloat16
NN = (((1,), (0,)), ((), ()))
NT = (((1,), (1,)), ((), ()))
TN = (((0,), (0,)), ((), ()))
SWAP = [(0, 1), (1, 0)]
GELU_A = math.sqrt(2.0 / math.pi)
GELU_B = 0.044715
COST = 100.0


def dot(a, b, dims=NN):
    return lax.dot_general(a, b, dims, preferred_element_type=F32)


ANY = pl.BlockSpec(memory_space=pl.ANY)


def call(body, name, grid, in_specs, out_specs, out_shape, scratch, flops, moved, prefetch=1, vmem=60, collective=None):
    return pl.pallas_call(
        body,
        out_shape=out_shape,
        grid_spec=pltpu.PrefetchScalarGridSpec(
            num_scalar_prefetch=prefetch,
            grid=grid,
            in_specs=in_specs,
            out_specs=out_specs,
            scratch_shapes=scratch,
        ),
        compiler_params=pltpu.CompilerParams(
            vmem_limit_bytes=vmem << 20,
            dimension_semantics=("arbitrary",) * len(grid),
            collective_id=collective,
            has_side_effects=collective is not None,
        ),
        cost_estimate=pl.CostEstimate(flops=int(flops * COST), bytes_accessed=int(moved * COST), transcendentals=0),
        name=name,
    )


def row_block(size, width):
    return pl.BlockSpec((size, width), lambda i, s: (i, 0))


def fixed(shape, index=None):
    place = index or (0,) * len(shape)
    return pl.BlockSpec(shape, lambda i, s: place, pipeline_mode=pl.Buffered(1))


def norm_parts(rows):
    center = rows - jnp.mean(rows, axis=-1, keepdims=True)
    inverse = lax.rsqrt(jnp.mean(center * center, axis=-1, keepdims=True) + EPS)
    return center * inverse, inverse


def lanes_of(info, chunk, piece):
    return pl.ds(pl.multiple_of((piece ^ info[0]) * chunk, chunk), chunk)


def to_neighbour(source, target, sends, receives, n, axis, at):
    return pltpu.make_async_remote_copy(
        src_ref=source,
        dst_ref=target,
        send_sem=sends.at[n],
        recv_sem=receives.at[n],
        device_id={axis: at},
        device_id_type=pl.DeviceIdType.MESH,
    )


def begin_body(tok, cot, gain, shift, in_ref, out_ref, up_any, down_any, nrm, cot_out, wa, vm_low, vm_high, cot_sum, chip_a, away_a, chip_m, away_m, up_ref, down_ref, nbuf, cbuf, loads, locals_, sends, receives, *, chunk, square, steps):
    i = pl.program_id(0)
    core, x, y = lax.axis_index("cc"), lax.axis_index("cx"), lax.axis_index("fsdp")
    shard = in_ref.shape[1]
    size, depth = tok.shape
    width, wide = chip_a.shape[1] // 4, chip_m.shape[1] // 2
    mine = pl.ds(pl.multiple_of(core * shard, shard), shard)
    rows = 2 * shard
    peers = [("cc", 1 - core)] + ([("cx", 1 - x), ("fsdp", 1 - y)] if square else [])

    load_up = pltpu.make_async_copy(up_any, up_ref, loads.at[0])
    load_down = pltpu.make_async_copy(down_any, down_ref, loads.at[1])
    swap_a = to_neighbour(away_a, chip_a.at[mine, :], sends, receives, 0, "cc", 1 - core)
    swap_m = to_neighbour(away_m, chip_m.at[mine, :], sends, receives, 1, "cc", 1 - core)
    keep_a = pltpu.make_async_copy(chip_a, wa.at[pl.ds(0, rows), :], locals_.at[0])
    keep_m = [
        pltpu.make_async_copy(chip_m.at[pl.ds(0, shard), :], vm_low, locals_.at[1]),
        pltpu.make_async_copy(chip_m.at[pl.ds(shard, shard), :], vm_high, locals_.at[2 + 2 * steps]),
    ]
    if square:
        to_x = to_neighbour(chip_a, wa.at[pl.ds(rows, rows), :], sends, receives, 2, "cx", 1 - x)
        to_y = to_neighbour(chip_a, wa.at[pl.ds(2 * rows, rows), :], sends, receives, 3, "fsdp", 1 - y)
        far_x = to_neighbour(
            wa.at[pl.ds(2 * rows, shard), :], wa.at[pl.ds(3 * rows, shard), :], sends, receives, 4, "cx", 1 - x
        )
        far_y = to_neighbour(
            wa.at[pl.ds(rows + shard, shard), :],
            wa.at[pl.ds(3 * rows + shard, shard), :],
            sends,
            receives,
            5,
            "fsdp",
            1 - y,
        )

    def row_copies(j):
        here = pl.ds(pl.multiple_of(j * size, size), size)
        there = pl.ds(pl.multiple_of((j + steps) * size, size), size)
        return [
            pltpu.make_async_copy(nbuf.at[j], nrm.at[here, :], locals_.at[2 + j]),
            pltpu.make_async_copy(cbuf.at[j], cot_out.at[here, :], locals_.at[2 + steps + j]),
            to_neighbour(nbuf.at[j], nrm.at[there, :], sends, receives, 6 + j, "cc", 1 - core),
            to_neighbour(cbuf.at[j], cot_out.at[there, :], sends, receives, 6 + steps + j, "cc", 1 - core),
        ]

    @pl.when(i == 0)
    def _():
        barrier = pltpu.get_barrier_semaphore()
        for axis, at in peers:
            pl.semaphore_signal(barrier, inc=1, device_id={axis: at}, device_id_type=pl.DeviceIdType.MESH)
        load_up.start()
        load_down.start()
        for target, c, at in ((chip_a, core, mine), (away_a, 1 - core, pl.ds(0, shard))):
            cut = pl.ds(pl.multiple_of(c * width, width), width)
            for j in range(3):
                target[at, width * j : width * j + width] = in_ref[j, :, cut]
            target[at, 3 * width :] = out_ref[cut, :].astype(F32).T.astype(BF)
        pl.semaphore_wait(barrier, len(peers))
        swap_a.start()
        load_up.wait()
        load_down.wait()
        for target, c, at in ((away_m, 1 - core, pl.ds(0, shard)), (chip_m, core, mine)):
            cut = pl.ds(pl.multiple_of(c * wide, wide), wide)
            target[at, :wide] = up_ref[:, cut]
            target[at, wide:] = down_ref[cut, :].astype(F32).T.astype(BF)
            if target is away_m:
                swap_m.start()
                swap_a.wait()
                if square:
                    to_x.start()
                    to_y.start()
                keep_a.start()
        cot_sum[...] = jnp.zeros_like(cot_sum)

    center, _ = norm_parts(tok[...].astype(F32))
    full = (center * gain[...].astype(F32)[None] + shift[...].astype(F32)[None]).astype(BF)
    cot_sum[...] += jnp.sum(cot[...].astype(F32), axis=0, keepdims=True)
    for r in range(depth // chunk):
        place = ((r // 2 + y) % 2) * 2 + (r % 2 + x) % 2 if square else r
        lanes = pl.ds(pl.multiple_of(place * chunk, chunk), chunk) if square else pl.ds(r * chunk, chunk)
        nbuf[i, :, lanes] = full[:, r * chunk : r * chunk + chunk]
        cbuf[i, :, lanes] = cot[:, r * chunk : r * chunk + chunk]
    for copy in row_copies(i):
        copy.start()

    @pl.when(i == steps - 1)
    def _():
        swap_m.wait()
        for copy in keep_m:
            copy.start()
        if square:
            to_y.wait()
            far_x.start()
            to_x.wait()
            far_y.start()
        keep_a.wait()
        for copy in keep_m:
            copy.wait()

        def finish(j, c):
            for copy in row_copies(j):
                copy.wait()
            return c

        lax.fori_loop(0, steps, finish, 0)
        if square:
            far_x.wait()
            far_y.wait()


def begin(tokens, cot, gain, shift, in_proj, out_proj, up_proj, down_proj, chunk, square):
    length, depth = tokens.shape
    steps = 4
    size = length // steps
    shard = in_proj.shape[1]
    width, wide = in_proj.shape[2] // 2, up_proj.shape[1] // 2
    block = pl.BlockSpec((size, depth), lambda i: (i, 0))
    whole = lambda shape: pl.BlockSpec(shape, lambda i: (0,) * len(shape), pipeline_mode=pl.Buffered(1))
    rows = 8 * shard if square else 2 * shard
    return call(
        functools.partial(begin_body, chunk=chunk, square=square, steps=steps),
        "begin",
        (steps,),
        [block, block, whole((depth,)), whole((depth,)), whole(in_proj.shape), whole(out_proj.shape), ANY, ANY],
        [ANY, ANY, ANY, ANY, ANY, pl.BlockSpec((1, depth), lambda i: (0, 0))],
        [
            jax.ShapeDtypeStruct((2 * length, depth), BF),
            jax.ShapeDtypeStruct((2 * length, depth), BF),
            jax.ShapeDtypeStruct((rows, 4 * width), BF),
            jax.ShapeDtypeStruct((shard, 2 * wide), BF),
            jax.ShapeDtypeStruct((shard, 2 * wide), BF),
            jax.ShapeDtypeStruct((1, depth), F32),
        ],
        [
            pltpu.VMEM((2 * shard, 4 * width), BF),
            pltpu.VMEM((shard, 4 * width), BF),
            pltpu.VMEM((2 * shard, 2 * wide), BF),
            pltpu.VMEM((shard, 2 * wide), BF),
            pltpu.VMEM(up_proj.shape, BF),
            pltpu.VMEM(down_proj.shape, BF),
            pltpu.VMEM((steps, size, depth), BF),
            pltpu.VMEM((steps, size, depth), BF),
            pltpu.SemaphoreType.DMA((2,)),
            pltpu.SemaphoreType.DMA((3 + 2 * steps,)),
            pltpu.SemaphoreType.DMA((6 + 2 * steps,)),
            pltpu.SemaphoreType.DMA((6 + 2 * steps,)),
        ],
        10 * tokens.size,
        16 * tokens.size,
        prefetch=0,
        collective=0,
    )(tokens, cot, gain, shift, in_proj, out_proj, up_proj, down_proj)


def rotary_tables(rates, positions, sign):
    angles = rates * positions
    cos_rows, sin_rows = jnp.cos(angles), sign * jnp.sin(angles)
    one = jnp.ones((HD - ROT, cos_rows.shape[1]), F32)
    none = jnp.zeros((HD - ROT, cos_rows.shape[1]), F32)
    few = jnp.zeros_like(cos_rows)
    return (
        jnp.concatenate([cos_rows, cos_rows, one] * 2, axis=0).T,
        jnp.concatenate([-sin_rows, few, none] * 2, axis=0).T,
        jnp.concatenate([few, sin_rows, none] * 2, axis=0).T,
    )


def turn(values, cos_part, down, up):
    return (
        values * cos_part
        + pltpu.roll(values, 128 - ROT // 2, 1) * down
        + pltpu.roll(values, ROT // 2, 1) * up
    )


def stay(shape):
    return pl.BlockSpec(shape, lambda i, s: (0,) * len(shape))


def piece_copies(pieces, columns, target, sems):
    copies, at = [], 0
    for n, piece in enumerate(pieces):
        count = piece.shape[0]
        copies.append(
            pltpu.make_async_copy(piece.at[:, columns], target.at[pl.ds(at, count), :], sems.at[n])
        )
        at += count
    return copies


def place_pieces(*jobs):
    copies = [copy for job in jobs for copy in piece_copies(*job)]
    for copy in copies:
        copy.start()
    for copy in copies:
        copy.wait()


def move_sems(pieces):
    return pltpu.SemaphoreType.DMA((len(pieces),))


def project_body(info, nrm, cot, weights, bias, rates, positions, q_out, kv_out, do_out, send, *, width):
    packed = dot(nrm[...], weights[:, : 3 * width]) + bias[...].astype(F32)
    do = dot(cot[...], weights[:, 3 * width :]).astype(BF)
    c, d, u = rotary_tables(rates[...], positions[...], 1.0)
    low = []
    for p in range(2 * width // 128):
        low.append(turn(packed[:, 128 * p : 128 * p + 128], c, d, u).astype(BF))
    pairs = width // 128
    queries = jnp.concatenate(low[:pairs], axis=1)
    keys = jnp.concatenate(low[pairs:], axis=1)
    values = packed[:, 2 * width :].astype(BF)
    q_out[...] = queries
    kv_out[:, :width] = keys
    kv_out[:, width:] = values
    do_out[...] = do
    part = width // 2

    @pl.when(info[3] == 0)
    def _():
        send[:, :part] = keys[:, :part]
        send[:, part:] = values[:, :part]

    @pl.when(info[3] != 0)
    def _():
        send[:, :part] = queries[:, part:]
        send[:, part:] = do[:, part:]


def project(info, normed, cot, weights, bias, tables, width):
    rows, depth = normed.shape
    size = min(rows, 256)
    return call(
        functools.partial(project_body, width=width),
        "project",
        (rows // size,),
        [row_block(size, depth)] * 2 + [fixed((depth, 4 * width)), fixed((1, 3 * width))]
        + [fixed((ROT // 2, 1)), pl.BlockSpec((1, size), lambda i, s: (0, i))],
        [row_block(size, width), row_block(size, 2 * width), row_block(size, width), row_block(size, width)],
        [jax.ShapeDtypeStruct((rows, n * width), BF) for n in (1, 2, 1, 1)],
        [],
        2 * rows * depth * 4 * width,
        2 * (2 * rows * depth + depth * 4 * width + 5 * rows * width),
    )(info, normed, cot, weights, bias, *tables)


def hidden_body(info, nrm, cot, bias, *rest, width, count):
    pieces, (act_out, grad_out, sum_out, weights, sems) = rest[:count], rest[count:]

    @pl.when(pl.program_id(0) == 0)
    def _():
        place_pieces((pieces, slice(0, 2 * width), weights, sems))
        sum_out[...] = jnp.zeros_like(sum_out)

    u = dot(nrm[...], weights[:, :width]) + bias[...].astype(F32)
    g = dot(cot[...], weights[:, width:])
    square = u * u
    t = jnp.tanh(GELU_A * (u + GELU_B * square * u))
    half = 0.5 * (1.0 + t)
    act_out[...] = (u * half).astype(BF)
    slope = half + 0.5 * u * (1.0 - t * t) * (GELU_A * (1.0 + 3.0 * GELU_B * square))
    low = (g * slope).astype(BF)
    grad_out[...] = low
    sum_out[...] += jnp.sum(low.astype(F32), axis=0, keepdims=True)


def hidden(info, normed, cot, pieces, bias, width):
    rows, depth = normed.shape
    size = min(rows, 256)
    return call(
        functools.partial(hidden_body, width=width, count=len(pieces)),
        "hidden",
        (rows // size,),
        [row_block(size, depth)] * 2 + [fixed((1, width))] + [ANY] * len(pieces),
        [row_block(size, width), row_block(size, width), stay((1, width))],
        [jax.ShapeDtypeStruct((rows, width), BF)] * 2 + [jax.ShapeDtypeStruct((1, width), F32)],
        [pltpu.VMEM((depth, 2 * width), BF), move_sems(pieces)],
        4 * rows * depth * width,
        2 * (2 * rows * depth + 2 * depth * width + 2 * rows * width),
    )(info, normed, cot, bias, *pieces)


def spread_body(a, b, *rest, counts, columns, sums, per):
    na, nb = counts
    wa, wb = rest[:na], rest[na : na + nb]
    rest = rest[na + nb :]
    normed = rest[:sums]
    out = rest[sums]
    totals = rest[sums + 1 : 3 * sums + 1]
    hold_a, hold_b, sem_a, sem_b, outgoing, incoming, send_sems, recv_sems = rest[3 * sums + 1 :]
    i = pl.program_id(0)
    core = lax.axis_index("cc")

    def copy(j):
        return pltpu.make_async_remote_copy(
            src_ref=outgoing.at[j],
            dst_ref=incoming.at[j],
            send_sem=send_sems.at[j],
            recv_sem=recv_sems.at[j],
            device_id={"cc": 1 - core},
            device_id_type=pl.DeviceIdType.MESH,
        )

    @pl.when(i == 0)
    def _():
        barrier = pltpu.get_barrier_semaphore()
        pl.semaphore_signal(barrier, inc=1, device_id={"cc": 1 - core}, device_id_type=pl.DeviceIdType.MESH)
        place_pieces((wa, columns[0], hold_a, sem_a), (wb, columns[1], hold_b, sem_b))
        pl.semaphore_wait(barrier, 1)
        for total in totals:
            total[...] = jnp.zeros_like(total)

    total = dot(a[...], hold_a[...], NT) + dot(b[...], hold_b[...], NT)

    @pl.when(i < per)
    def _():
        outgoing[i] = total.astype(BF)
        copy(i).start()

    @pl.when(i >= per)
    def _():
        copy(i - per).wait()
        full = total + incoming[i - per].astype(F32)
        out[...] = full.astype(BF)
        if sums:
            totals[0][...] += jnp.sum(full * normed[0][...].astype(F32), axis=0, keepdims=True)
            totals[1][...] += jnp.sum(full, axis=0, keepdims=True)


def spread(a, b, wa, wb, ca, cb, depth, name, collective, normed=()):
    rows = a.shape[0] // 2
    size = min(rows, 256)
    per = rows // size
    at = lambda width: pl.BlockSpec((size, width), lambda i: ((i + per) % (2 * per), 0))
    later = pl.BlockSpec((size, depth), lambda i: (jnp.maximum(i - per, 0), 0))
    one = pl.BlockSpec((1, depth), lambda i: (0, 0))
    wide_a, wide_b = a.shape[1], b.shape[1]
    count = len(normed)
    return call(
        functools.partial(
            spread_body,
            counts=(len(wa), len(wb)),
            columns=(slice(ca, ca + wide_a), slice(cb, cb + wide_b)),
            sums=count,
            per=per,
        ),
        name,
        (2 * per,),
        [at(wide_a), at(wide_b)] + [ANY] * (len(wa) + len(wb)) + [later] * count,
        [later] + [one] * (2 * count),
        [jax.ShapeDtypeStruct((rows, depth), BF)] + [jax.ShapeDtypeStruct((1, depth), F32)] * (2 * count),
        [
            pltpu.VMEM((depth, wide_a), BF),
            pltpu.VMEM((depth, wide_b), BF),
            move_sems(wa),
            move_sems(wb),
            pltpu.VMEM((per, size, depth), BF),
            pltpu.VMEM((per, size, depth), BF),
            pltpu.SemaphoreType.DMA((per,)),
            pltpu.SemaphoreType.DMA((per,)),
        ],
        4 * rows * depth * (wide_a + wide_b),
        2 * (2 * rows + depth) * (wide_a + wide_b) + 2 * rows * depth,
        prefetch=0,
        collective=collective,
    )(a, b, *wa, *wb, *normed)


def outer_body(info, left_n, left_c, right_n, right_c, *rest, order, outputs):
    i = pl.program_id(0)
    outs = rest[:-3]
    hold_n, hold_c, sems = rest[-3:]
    loads = (
        pltpu.make_async_copy(right_n, hold_n, sems.at[0]),
        pltpu.make_async_copy(right_c, hold_c, sems.at[1]),
    )
    kinds = [kind for _, kind in order]

    @pl.when(i == 0)
    def _():
        loads[kinds[0]].start()
        loads[1 - kinds[0]].start()

    for kind in (0, 1):

        @pl.when(i == kinds.index(kind))
        def _(kind=kind):
            loads[kind].wait()

    for step, (block, kind) in enumerate(order):
        left, right = ((left_n, hold_n), (left_c, hold_c))[kind]

        @pl.when(i == step)
        def _(block=block, kind=kind, left=left, right=right):
            result = dot(left[...], right[...], TN).astype(BF)
            for out, (blocks, parts) in zip(outs, outputs):
                if block in blocks and kind in parts:
                    source, target = parts[kind]
                    out[:, target] = result[:, source]


def by_step(table):
    def at(i):
        value = table[-1]
        for step in range(len(table) - 1):
            value = jnp.where(i == step, table[step], value)
        return value

    return at


def places(order, find):
    used = [find(*entry) for entry in order]
    table, upcoming = [None] * len(used), None
    for step in reversed(range(len(used))):
        upcoming = used[step] if used[step] is not None else upcoming
        table[step] = upcoming
    last = None
    for step, value in enumerate(table):
        last = value if value is not None else last
        table[step] = last
    return by_step(table)


def outer(info, normed, cot, right_n, right_c, chunk, order, outputs, name):
    rows = right_n.shape[0]
    wide = (right_n.shape[1], right_c.shape[1])

    def left(which):
        at = places(order, lambda block, kind: block if kind == which else None)
        return pl.BlockSpec((rows, chunk), lambda i, s: (0, at(i)))

    out_specs, out_shapes = [], []
    for blocks, parts in outputs:
        width = max(target.stop for _, target in parts.values())
        at = places(order, lambda block, kind: blocks.index(block) if block in blocks and kind in parts else None)
        out_specs.append(pl.BlockSpec((chunk, width), lambda i, s, at=at: (at(i), 0)))
        out_shapes.append(jax.ShapeDtypeStruct((len(blocks) * chunk, width), BF))
    return call(
        functools.partial(outer_body, order=order, outputs=outputs),
        name,
        (len(order),),
        [left(0), left(1), ANY, ANY],
        out_specs,
        out_shapes,
        [pltpu.VMEM((rows, wide[0]), BF), pltpu.VMEM((rows, wide[1]), BF), pltpu.SemaphoreType.DMA((2,))],
        rows * chunk * len(order) * sum(wide),
        2 * (rows + chunk) * len(order) * sum(wide),
    )(info, normed, cot, right_n, right_c)


def head_masks(block, scale):
    lane = lax.broadcasted_iota(jnp.int32, block.shape, 1)
    v = block.astype(F32) * scale
    return (jnp.where(lane < HD, v, 0.0).astype(BF), jnp.where(lane < HD, 0.0, v).astype(BF))


def own_mask(flag, width):
    kk = lax.broadcasted_iota(jnp.int32, (RUN, width), 0)
    qq = lax.broadcasted_iota(jnp.int32, (RUN, width), 1)
    return kk <= qq + flag * RUN


def each_prefix(here, half, runs, work):
    size = runs // 2
    while size:

        @pl.when((here & size) != 0)
        def _(size=size):
            low = here & ((runs - 1) & ~(2 * size - 1))
            work(pl.multiple_of((low ^ half) * RUN, RUN), size * RUN)

        size //= 2


def softmax_blocks(state, heads, k_r, vt_r, qm, start, size, mask=None):
    acc, ml = state

    def score(n):
        p, h = divmod(n, 2)
        s = dot(k_r[pl.ds(start, size), 128 * p : 128 * p + 128], qm[p][h], NT)
        return s if mask is None else jnp.where(mask, s, NEG)

    def rest(n, s):
        top = jnp.max(s, axis=0, keepdims=True)
        rows = slice(HD * n, HD * n + HD)
        vb = vt_r[rows, pl.ds(start, size)]
        m = ml[n : n + 1, :]
        new = jnp.maximum(m, top)
        alpha = jnp.exp(m - new)
        e = jnp.exp(s - new)
        ml[n : n + 1, :] = new
        ml[heads + n : heads + n + 1, :] = ml[heads + n : heads + n + 1, :] * alpha + jnp.sum(e, axis=0, keepdims=True)
        acc[rows, :] = acc[rows, :] * alpha + dot(vb, e.astype(BF))

    s = score(0)
    for n in range(heads):
        following = score(n + 1) if n + 1 < heads else None
        rest(n, s)
        s = following


def start_state(acc, ml, heads):
    acc[...] = jnp.zeros_like(acc)
    ml[:heads, :] = jnp.full((heads, ml.shape[1]), NEG, F32)
    ml[heads:, :] = jnp.zeros((heads, ml.shape[1]), F32)


def finish_state(acc, ml, heads, n):
    l = ml[heads + n : heads + n + 1, :]
    return acc[HD * n : HD * n + HD, :] / l, ml[n : n + 1, :] + jnp.log(l)


def query_masks(block, scale):
    return [head_masks(block[:, 128 * p : 128 * p + 128], scale) for p in range(block.shape[1] // 128)]


SCALE = 1.0 / math.sqrt(HD)


def local_body(info, q_ref, k_ref, v_ref, out_ref, lse_ref, vt, acc, ml, *, heads):
    i = pl.program_id(0)
    half = info[0]
    runs = k_ref.shape[0] // RUN

    @pl.when(i == 0)
    def _():
        vt[...] = v_ref[...].astype(F32).T.astype(BF)

    qm = query_masks(q_ref[...], SCALE)
    start_state(acc, ml, heads)
    work = lambda start, size, mask=None: softmax_blocks((acc, ml), heads, k_ref, vt, qm, start, size, mask)
    work(pl.multiple_of(i * RUN, RUN), RUN, own_mask(info[2 + i], q_ref.shape[0]))
    each_prefix(i ^ half, half, runs, work)
    for n in range(heads):
        out_ref[HD * n : HD * n + HD, :], lse_ref[n : n + 1, :] = finish_state(acc, ml, heads, n)


def attend_local(info, q, kv):
    rows, width = q.shape
    heads = width // HD
    columns = lambda count: pl.BlockSpec((count, RUN), lambda i, s: (0, i))
    return call(
        functools.partial(local_body, heads=heads),
        "attend_local",
        (rows // RUN,),
        [row_block(RUN, width), fixed((rows, width)), fixed((rows, width), (0, 1))],
        [columns(width), columns(heads)],
        [jax.ShapeDtypeStruct((width, rows), F32), jax.ShapeDtypeStruct((heads, rows), F32)],
        [pltpu.VMEM((width, rows), BF), pltpu.VMEM((width, RUN), F32), pltpu.VMEM((2 * heads, RUN), F32)],
        25e9,
        14 * rows * width,
    )(info, q, kv, kv)


def cross_body(info, q_ref, came_ref, came0, came1, k_ref, v_ref, out_ref, lse_ref, keys, vt, acc, ml, *, heads, cut):
    late = info[1] > 0

    @pl.when(pl.program_id(0) == 0)
    def _():
        keys[...] = jnp.where(late, came0[...], k_ref[...])
        vt[...] = jnp.where(late, came1[...], v_ref[...]).astype(F32).T.astype(BF)

    qm = query_masks(jnp.where(late, q_ref[...], came_ref[...]), SCALE)
    start_state(acc, ml, heads)
    for j in range(keys.shape[0] // cut):
        softmax_blocks((acc, ml), heads, keys, vt, qm, j * cut, cut)
    for n in range(heads):
        out, lse_ref[n : n + 1, :] = finish_state(acc, ml, heads, n)
        out_ref[HD * n : HD * n + HD, :] = out.astype(BF)


def cross_specs(rows, part):
    own = lambda i, s: (i, 1 - s[1])
    return (
        pl.BlockSpec((RUN, part), own),
        pl.BlockSpec((RUN, part), lambda i, s: (i, 0)),
        fixed((rows, part)),
        fixed((rows, part), (0, 1)),
        pl.BlockSpec((rows, part), lambda i, s: (0, 1 - s[1])),
        pl.BlockSpec((rows, part), lambda i, s: (0, 3 - s[1])),
    )


def attend_cross(info, q, came, kv):
    rows, part = q.shape[0], q.shape[1] // 2
    heads = part // HD
    query, came_block, came0, came1, key, value = cross_specs(rows, part)
    columns = lambda count: pl.BlockSpec((count, RUN), lambda i, s: (0, i))
    return call(
        functools.partial(cross_body, heads=heads, cut=min(rows, 1024)),
        "attend_cross",
        (rows // RUN,),
        [query, came_block, came0, came1, key, value],
        [columns(part), columns(heads)],
        [jax.ShapeDtypeStruct((part, rows), BF), jax.ShapeDtypeStruct((heads, rows), F32)],
        [
            pltpu.VMEM((rows, part), BF),
            pltpu.VMEM((part, rows), BF),
            pltpu.VMEM((part, RUN), F32),
            pltpu.VMEM((2 * heads, RUN), F32),
        ],
        15e9,
        14 * rows * part,
    )(info, q, came, came, came, kv, kv)


def merge_body(info, local, lse_local, mine, lse_mine, came, lse_came, do_ref, att_ref, stat_ref, early_ref, late_ref, *, heads):
    late = info[1] > 0
    part = heads // 2
    size = do_ref.shape[0]
    do_t = do_ref[...].astype(F32).T
    outs = []
    for n in range(heads):
        other, lse_other, m = (mine, lse_mine, n) if n < part else (came, lse_came, n - part)
        rows = slice(HD * n, HD * n + HD)
        ours = lse_local[n : n + 1, :]
        theirs = jnp.where(late, lse_other[m : m + 1, :], jnp.full((1, size), NEG, F32))
        top = jnp.maximum(ours, theirs)
        a, b = jnp.exp(ours - top), jnp.exp(theirs - top)
        total = a + b
        o = (local[rows, :] * a + other[HD * m : HD * m + HD, :].astype(F32) * b) / total
        outs.append(o)
        lse = top + jnp.log(total)
        delta = jnp.sum(o * do_t[rows, :], axis=0, keepdims=True)
        stat_ref[n : n + 1, :] = lse
        stat_ref[heads + n : heads + n + 1, :] = delta
        for ref, base in ((early_ref, 0), (late_ref, part)):
            if base <= n < base + part:
                ref[n - base : n - base + 1, :] = lse
                ref[part + n - base : part + n - base + 1, :] = delta
    att_ref[...] = jnp.concatenate(outs, axis=0).T.astype(BF)


def merge(info, local, lse_local, mine, lse_mine, came, lse_came, do):
    rows, width = do.shape
    heads = width // HD
    size = min(rows, 512)
    columns = lambda count: pl.BlockSpec((count, size), lambda i, s: (0, i))
    return call(
        functools.partial(merge_body, heads=heads),
        "merge",
        (rows // size,),
        [columns(width), columns(heads)] + [columns(width // 2), columns(heads // 2)] * 2 + [row_block(size, width)],
        [row_block(size, width), columns(2 * heads), columns(heads), columns(heads)],
        [jax.ShapeDtypeStruct((rows, width), BF)]
        + [jax.ShapeDtypeStruct((count, rows), F32) for count in (2 * heads, heads, heads)],
        [],
        20 * rows * width,
        10 * rows * width,
    )(info, local, lse_local, mine, lse_mine, came, lse_came, do)


def gradient_blocks(heads, k_r, v_r, kt_r, dk_r, dv_r, dqt, qm, dm, stat, start, size, mask=None):
    def products(n):
        p, h = divmod(n, 2)
        lanes = slice(128 * p, 128 * p + 128)
        return (
            dot(k_r[pl.ds(start, size), lanes], qm[p][h], NT),
            dot(v_r[pl.ds(start, size), lanes], dm[p][h], NT),
        )

    def rest(n, s, g):
        p, h = divmod(n, 2)
        e = jnp.exp(s - stat[n : n + 1, :])
        if mask is not None:
            e = jnp.where(mask, e, 0.0)
        ds = (e * (g - stat[heads + n : heads + n + 1, :])).astype(BF)
        rows = slice(HD * n, HD * n + HD)
        dqt[rows, :] += dot(kt_r[rows, pl.ds(start, size)], ds)
        return dot(ds, qm[p][h]), dot(e.astype(BF), dm[p][h])

    now = products(0)
    before = None
    for n in range(heads):
        following = products(n + 1) if n + 1 < heads else None
        grads = rest(n, *now)
        now = following
        if n % 2:
            lanes = slice(HD * (n - 1), HD * (n + 1))
            dk_r[pl.ds(start, size), lanes] += before[0] + grads[0]
            dv_r[pl.ds(start, size), lanes] += before[1] + grads[1]
        before = grads


def local_back_body(info, q_ref, do_ref, stat_ref, k_ref, v_ref, dqx, dkx, dvx, came_q, came_k, came_v, rates, positions, out, sums, kt, dqt, dk, dv, *, heads):
    i = pl.program_id(0)
    half = info[0]
    late = info[1] > 0
    runs = k_ref.shape[0] // RUN
    width = HD * heads
    part = width // 2

    @pl.when(i == 0)
    def _():
        kt[...] = k_ref[...].astype(F32).T.astype(BF)

    @pl.when((i == 0) & late)
    def _():
        dk[...] = jnp.zeros_like(dk)
        dv[...] = jnp.zeros_like(dv)

    @pl.when((i == 0) & jnp.logical_not(late))
    def _():
        dk[:, :part] = came_k[...].astype(F32)
        dk[:, part:] = dkx[...]
        dv[:, :part] = came_v[...].astype(F32)
        dv[:, part:] = dvx[...]

    qm = query_masks(q_ref[...], SCALE)
    dm = query_masks(do_ref[...], 1.0)
    dqt[...] = jnp.zeros_like(dqt)

    def work(start, size, mask=None):
        gradient_blocks(heads, k_ref, v_ref, kt, dk, dv, dqt, qm, dm, stat_ref, start, size, mask)

    work(pl.multiple_of(i * RUN, RUN), RUN, own_mask(info[2 + i], q_ref.shape[0]))
    each_prefix(i ^ half, half, runs, work)
    zero = jnp.zeros((q_ref.shape[0], part), F32)
    more = jnp.concatenate(
        [jnp.where(late, dqx[...], zero), jnp.where(late, came_q[...].astype(F32), zero)], axis=1
    )
    found = (dqt[...] * SCALE).T + more
    rows = pl.ds(pl.multiple_of(i * RUN, RUN), RUN)
    c, d, u = rotary_tables(rates[...], positions[:, rows], -1.0)
    for p in range(width // 128):
        lanes = slice(128 * p, 128 * p + 128)
        out[rows, lanes] = turn(found[:, lanes], c, d, u).astype(BF)

    @pl.when(i == pl.num_programs(0) - 1)
    def _():
        def step(j, c):
            at = pl.ds(pl.multiple_of(j * RUN, RUN), RUN)
            c2, d2, u2 = rotary_tables(rates[...], positions[:, at], -1.0)
            for p in range(width // 128):
                lanes = slice(128 * p, 128 * p + 128)
                shifted = slice(width + 128 * p, width + 128 * p + 128)
                out[at, shifted] = turn(dk[at, lanes], c2, d2, u2).astype(BF)
            out[at, 2 * width :] = dv[at, :].astype(BF)
            return c + jnp.sum(out[at, :].astype(F32), axis=0, keepdims=True)

        sums[...] = lax.fori_loop(0, runs, step, jnp.zeros((1, 3 * width), F32))


def back_local(info, q, do, stat, kv, cross, came, tables):
    rows, width = q.shape
    heads = width // HD
    part = width // 2
    blk = row_block(RUN, width)
    few = row_block(RUN, part)
    return call(
        functools.partial(local_back_body, heads=heads),
        "back_local",
        (rows // RUN,),
        [
            blk,
            blk,
            pl.BlockSpec((2 * heads, RUN), lambda i, s: (0, i)),
            fixed((rows, width)),
            fixed((rows, width), (0, 1)),
            few,
            fixed((rows, part)),
            fixed((rows, part)),
            few,
            fixed((rows, part)),
            fixed((rows, part), (0, 1)),
            fixed((ROT // 2, 1)),
            fixed((1, rows)),
        ],
        [stay((rows, 3 * width)), stay((1, 3 * width))],
        [jax.ShapeDtypeStruct((rows, 3 * width), BF), jax.ShapeDtypeStruct((1, 3 * width), F32)],
        [
            pltpu.VMEM((width, rows), BF),
            pltpu.VMEM((width, RUN), F32),
            pltpu.VMEM((rows, width), F32),
            pltpu.VMEM((rows, width), F32),
        ],
        40e9,
        20 * rows * width,
    )(info, q, do, stat, kv, kv, *cross, came, came, came, *tables)


def cross_back_body(info, q_ref, do_ref, came_q, came_do, came0, came1, k_ref, v_ref, early, came_stat, dq_ref, dk_ref, dv_ref, send, keys, values, kt, dqt, *, heads, cut):
    late = info[1] > 0
    i = pl.program_id(0)
    part = HD * heads

    @pl.when(i == 0)
    def _():
        chosen = jnp.where(late, came0[...], k_ref[...])
        keys[...] = chosen
        kt[...] = chosen.astype(F32).T.astype(BF)
        values[...] = jnp.where(late, came1[...], v_ref[...])
        dk_ref[...] = jnp.zeros_like(dk_ref)
        dv_ref[...] = jnp.zeros_like(dv_ref)

    qm = query_masks(jnp.where(late, q_ref[...], came_q[...]), SCALE)
    dm = query_masks(jnp.where(late, do_ref[...], came_do[...]), 1.0)
    dqt[...] = jnp.zeros_like(dqt)
    stat = jnp.where(late, early[...], came_stat[...])
    for j in range(keys.shape[0] // cut):
        gradient_blocks(heads, keys, values, kt, dk_ref, dv_ref, dqt, qm, dm, stat, j * cut, cut)
    found = (dqt[...] * SCALE).T
    dq_ref[...] = found
    rows = pl.ds(pl.multiple_of(i * RUN, RUN), RUN)

    @pl.when(jnp.logical_not(late))
    def _():
        send[rows, :part] = found.astype(BF)
        send[rows, part:] = found.astype(BF)

    @pl.when(late & (i == pl.num_programs(0) - 1))
    def _():
        send[:, :part] = dk_ref[...].astype(BF)
        send[:, part:] = dv_ref[...].astype(BF)


def back_cross(info, q, do, came, kv, early, came_stat):
    rows, part = q.shape[0], q.shape[1] // 2
    heads = part // HD
    query, came_block, came0, came1, key, value = cross_specs(rows, part)
    acc = jax.ShapeDtypeStruct((rows, part), F32)
    return call(
        functools.partial(cross_back_body, heads=heads, cut=min(rows, 1024)),
        "back_cross",
        (rows // RUN,),
        [
            query,
            query,
            came_block,
            pl.BlockSpec((RUN, part), lambda i, s: (i, 1)),
            came0,
            came1,
            key,
            value,
            pl.BlockSpec((2 * heads, RUN), lambda i, s: (0, i)),
            pl.BlockSpec((2 * heads, RUN), lambda i, s: (0, i)),
        ],
        [row_block(RUN, part), stay((rows, part)), stay((rows, part)), stay((rows, 2 * part))],
        [acc, acc, acc, jax.ShapeDtypeStruct((rows, 2 * part), BF)],
        [
            pltpu.VMEM((rows, part), BF),
            pltpu.VMEM((rows, part), BF),
            pltpu.VMEM((part, rows), BF),
            pltpu.VMEM((part, RUN), F32),
        ],
        25e9,
        20 * rows * part,
    )(info, q, do, came, came, came, came, kv, kv, early, came_stat)


def input_body(info, grad, tok, cot, gain, out, *, chunk):
    xhat, inverse = norm_parts(tok[...].astype(F32))
    parts = [grad[:, lanes_of(info, chunk, r)] for r in range(tok.shape[1] // chunk)]
    e = jnp.concatenate(parts, axis=1).astype(F32) * gain[...].astype(F32)
    mean_e = jnp.mean(e, axis=-1, keepdims=True)
    mean_ex = jnp.mean(e * xhat, axis=-1, keepdims=True)
    out[...] = (cot[...].astype(F32) + (e - mean_e - xhat * mean_ex) * inverse).astype(BF)


def input_grads(info, grad, tok, cot, gain, chunk):
    rows, width = grad.shape
    steps = 4
    size = rows // steps
    share = pl.BlockSpec((size, width), lambda i, s: (s[1] * steps + i, 0))
    return call(
        functools.partial(input_body, chunk=chunk),
        "input_grad",
        (steps,),
        [row_block(size, width), share, share, fixed((1, width))],
        [row_block(size, width)],
        [jax.ShapeDtypeStruct((rows, width), BF)],
        [],
        20 * rows * width,
        8 * rows * width,
    )(info, grad, tok, cot, gain[None])[0]


def layer_body(info, branch, tok, bias, out, *, chunk):
    for r in range(tok.shape[1] // chunk):
        at = slice(r * chunk, r * chunk + chunk)
        part = branch[:, lanes_of(info, chunk, r)].astype(F32)
        out[:, at] = (tok[:, at].astype(F32) + part + bias[:, at].astype(F32)).astype(BF)


def layer_rows(info, branch, tok, bias, chunk):
    rows, width = branch.shape
    return call(
        functools.partial(layer_body, chunk=chunk),
        "layer_out",
        (1,),
        [row_block(rows, width), pl.BlockSpec((rows, width), lambda i, s: (s[1], 0)), fixed((1, width))],
        [row_block(rows, width)],
        [jax.ShapeDtypeStruct((rows, width), BF)],
        [],
        4 * branch.size,
        6 * branch.size,
    )(info, branch, tok, bias[None])[0]


def body(tokens, cotangent, piece_ids, positions, norm_gain, norm_shift, in_proj, in_bias, out_proj, up_proj, up_bias, down_proj, out_bias):
    length, depth = tokens.shape
    width = in_bias.shape[1] // 2
    hidden_width = up_bias.shape[0] // 2
    f_count, z_count = lax.axis_size("fsdp"), lax.axis_size("tp")
    x_at, c_at, f_at = lax.axis_index("cx"), lax.axis_index("cc"), lax.axis_index("fsdp")
    square = f_count == 2
    chips = 2 * f_count
    chunk = depth // chips
    me = f_at * 2 + x_at if square else 0 * f_at
    info = jnp.stack([me, lax.axis_index("tp"), c_at, x_at]).astype(jnp.int32)

    other_core = lambda value: lax.ppermute(value, "cc", SWAP)
    by_x = lambda value: lax.ppermute(value, "cx", SWAP)
    by_y = lambda value: lax.ppermute(value, "fsdp", SWAP)

    def pick(value, index, size, axis):
        return lax.dynamic_slice_in_dim(value, index * size, size, axis)

    def in_order(mine, theirs, axis):
        return jnp.where(c_at == 0, jnp.concatenate([mine, theirs], axis), jnp.concatenate([theirs, mine], axis))

    def after(value, *earlier):
        return lax.optimization_barrier((value,) + earlier)[0]

    shard = in_proj.shape[1]
    normed, cot, weights_a, low_m, high_m, cot_sum = begin(
        tokens, cotangent, norm_gain, norm_shift, in_proj, out_proj, up_proj, down_proj, chunk, square
    )
    if not square:
        weights_a = lax.all_gather(weights_a, ("fsdp", "cx"), axis=0, tiled=True)
        both_m = jnp.concatenate([low_m, high_m], axis=0)
        weights_m = [lax.all_gather(both_m, ("fsdp", "cx"), axis=0, tiled=True)]
    small = jnp.stack([piece_ids, positions])
    small = jnp.concatenate([small, other_core(small)], axis=1)
    pieces, rows_at = small[0], small[1]

    frequency = 10000.0 ** (-2.0 * jnp.arange(ROT // 2, dtype=F32) / ROT)
    tables = (frequency[:, None], rows_at.astype(F32)[None, :])
    bias_a = pick(in_bias, c_at, width, 1).reshape(1, 3 * width)
    bias_m = pick(up_bias, c_at, hidden_width, 0)[None]
    flags = (pieces.reshape(-1, RUN)[:, 0] > 0).astype(jnp.int32)
    scene = jnp.concatenate([jnp.stack([c_at * (length // RUN), x_at]).astype(jnp.int32), flags])

    if square:
        x_first, y_first, y_second = by_x(low_m), by_y(low_m), by_y(high_m)
    queries, kv, grad_att, send = project(info, normed, cot, weights_a, bias_a, tables, width)
    came = by_x(send)
    local, lse_local = attend_local(scene, after(queries, x_first) if square else queries, kv)
    mine, lse_mine = attend_cross(scene, after(queries, local), came, kv)
    if square:
        x_second = by_x(after(high_m, local))
        y_back = by_y(x_first)
    forward_x = lambda value: lax.ppermute(value, "cx", [(0, 1)])
    attended, stat, stat_early, stat_late = merge(
        scene,
        after(local, x_second) if square else local,
        lse_local,
        mine,
        lse_mine,
        forward_x(mine),
        forward_x(lse_mine),
        grad_att,
    )
    stat_came = lax.ppermute(stat_late, "cx", [(1, 0)])
    if square:
        weights_m = [low_m, high_m, x_first, x_second, y_first, y_second, y_back, by_x(after(y_second, stat_came))]
    *cross, outgoing = back_cross(
        scene, after(queries, y_back) if square else queries, grad_att, came, kv, stat_early, stat_came
    )
    returned = by_x(outgoing)
    active, grad_up, up_sum = hidden(info, normed, cot, weights_m, after(bias_m, outgoing), hidden_width)

    def scatter(value):
        return lax.psum_scatter(value, ("fsdp", "cx"), scatter_dimension=0, tiled=True)

    every = tuple(range(chips))
    every_step = tuple((block, kind) for kind in (0, 1) for block in every)

    def columns_of(*parts):
        return {kind: (slice(*source), slice(*target)) for kind, source, target in parts}

    def hidden_weight_grads(last):
        up = columns_of((0, (0, hidden_width), (0, hidden_width)))
        down = columns_of((1, (0, hidden_width), (0, hidden_width)))
        order, outputs = every_step, ((every, up), (every, down))
        if square:
            order = tuple((block, 0) for block in (1, 3, 2, 0)) + tuple((block, 1) for block in (2, 3, 1, 0))
            outputs = (((1, 3), up), ((2,), up), ((0,), up), ((2, 3), down), ((1,), down), ((0,), down))
        return outer(info, after(normed, last), cot, grad_up, active, chunk, order, outputs, "hidden_grads")

    def packed_weight_grads(last):
        wide = 3 * width
        two = 2 * width
        all_in = columns_of((0, (0, wide), (0, wide)))
        all_out = columns_of((1, (0, width), (0, width)))
        order, outputs = every_step, ((every, all_in), (every, all_out))
        if square:
            first = columns_of((0, (0, two), (0, two)))
            second = columns_of((0, (two, wide), (0, width)), (1, (0, width), (width, two)))
            order = tuple((block, kind) for block in (3, 1, 2, 0) for kind in (0, 1))
            outputs = (((1, 3), first), ((2,), first), ((0,), first), ((2, 3), second), ((1,), second), ((0,), second))
        return outer(info, after(normed, *last), cot, grad_packed, attended, chunk, order, outputs, "packed_grads")

    def add(*values):
        return functools.reduce(lambda a, b: a + b, [value.astype(F32) for value in values])

    columns = (3 * width, hidden_width)
    (ours,) = spread(attended, active, [weights_a], weights_m, *columns, depth, "branch", 1)
    branch = lax.psum_scatter(ours, "tp", scatter_dimension=0, tiled=True)
    hidden_grads = hidden_weight_grads(ours)
    if square:
        up_away, up_second, up_own, down_away, down_second, down_own = hidden_grads
        up_came, down_came = by_x(up_away), by_y(down_away)
    grad_packed, in_sum = back_local(
        scene, after(queries, hidden_grads[-1]), grad_att, stat, kv, cross, returned, tables
    )
    if square:
        up_pass = add(up_second, up_came[chunk:]).astype(BF)
        down_pass = add(down_second, down_came[chunk:]).astype(BF)
        up_last, down_last = by_y(up_pass), by_x(down_pass)
        left = after(grad_packed, up_pass, down_pass)
    else:
        left = grad_packed
    ours, gain_part, shift_part = spread(
        left, grad_up, [weights_a], weights_m, 0, 0, depth, "normed_grad", 2, (normed,)
    )
    grad_normed = lax.psum_scatter(ours, "tp", scatter_dimension=0, tiled=True)

    def to_plain(row):
        if not square:
            return row
        return jnp.concatenate([pick(row, r ^ me, chunk, 1) for r in range(chips)], axis=1)

    shift_sum = to_plain(shift_part)
    gain_sum = (to_plain(gain_part) - shift_sum * norm_shift.astype(F32)[None]) / norm_gain.astype(F32)[None]
    once = jnp.where(lax.axis_index("tp") == 0, cot_sum, 0.0)
    both = jnp.concatenate([gain_sum, shift_sum, once, in_sum, up_sum], axis=1)
    wide_size = 3 * depth

    def keep(rows):
        size = rows.shape[0] // 2
        mine, theirs = pick(rows, c_at, size, 0).astype(F32), pick(rows, 1 - c_at, size, 0).astype(BF)
        came = other_core(theirs).astype(F32)
        return jnp.where(c_at == 0, jnp.stack([mine, came]), jnp.stack([came, mine]))

    def side_by_side(two):
        return jnp.transpose(two, (1, 0, 2)).reshape(two.shape[1], 2 * two.shape[2])

    def one_below_other(two):
        return jnp.transpose(two, (0, 2, 1)).reshape(2 * two.shape[2], two.shape[1])

    if square:
        qk_away, qk_second, qk_own, vo_away, vo_second, vo_own = packed_weight_grads((both, up_last, down_last))
        both = both + by_x(both)
        hop = by_y(after(both, qk_away))
        qk_came, vo_came = by_x(qk_away), by_y(vo_away)
        layer_out = layer_rows(info, after(branch, vo_own), tokens, out_bias, chunk)
        both = both + hop
        up_two = keep(add(after(up_own, layer_out, both), up_came[:chunk], up_last))
        down_two = keep(add(after(down_own, layer_out, both), down_came[:chunk], down_last))
        qk_pass = add(after(qk_second, up_two, down_two), qk_came[chunk:]).astype(BF)
        vo_pass = add(after(vo_second, up_two, down_two), vo_came[chunk:]).astype(BF)
        qk_far, vo_far = by_y(qk_pass), by_x(vo_pass)
        upproj_grad, downproj_grad = side_by_side(after(up_two, qk_pass)), one_below_other(after(down_two, vo_pass))
        qk_two = keep(add(after(qk_own, upproj_grad), qk_came[:chunk], qk_far))
        vo_two = keep(add(after(vo_own, downproj_grad), vo_came[:chunk], vo_far))
        in_parts = [qk_two[..., :width], qk_two[..., width:], vo_two[..., :width]]
        out_two = vo_two[..., width:]
    else:
        layer_out = layer_rows(info, branch, tokens, out_bias, chunk)
        both = lax.psum(both, ("fsdp", "cx"))
        up_two, down_two = [keep(scatter(value)) for value in hidden_grads]
        upproj_grad, downproj_grad = side_by_side(up_two), one_below_other(down_two)
        in_two, out_two = [keep(scatter(value)) for value in packed_weight_grads((both,))]
        in_parts = [in_two[..., j * width : j * width + width] for j in range(3)]
    inproj_grad = jnp.stack([side_by_side(part) for part in in_parts])
    outproj_grad = one_below_other(out_two)
    swapped = other_core(both)
    wide = both[:, :wide_size] + swapped[:, :wide_size]
    step = 1
    while step < z_count:
        wide = wide + lax.ppermute(wide, "tp", [(z, z ^ step) for z in range(z_count)])
        step *= 2
    gain_grad, shift_grad, outbias_grad = [wide[0, depth * j : depth * j + depth] for j in range(3)]
    narrow_pair = in_order(both[:, wide_size:], swapped[:, wide_size:], 0)
    inbias_grad = jnp.transpose(narrow_pair[:, : 3 * width].reshape(2, 3, width), (1, 0, 2)).reshape(3, 2 * width)
    upbias_grad = narrow_pair[:, 3 * width :].reshape(2 * hidden_width)
    input_grad = input_grads(info, after(grad_normed, inproj_grad), tokens, cotangent, norm_gain, chunk)
    return (
        layer_out,
        input_grad,
        gain_grad,
        shift_grad,
        inproj_grad,
        inbias_grad,
        outproj_grad,
        upproj_grad,
        upbias_grad,
        downproj_grad,
        outbias_grad,
    )


def solution(mesh):
    sizes = mesh.shape
    split = Mesh(
        mesh.devices.reshape(sizes["fsdp"], sizes["ctx"] // 2, 2, sizes["tp"]), ("fsdp", "cx", "cc", "tp")
    )
    group = ("fsdp", "cx", "cc")
    return jax.shard_map(
        body,
        mesh=split,
        in_specs=(
            P(group, None),
            P(group, None),
            P(group),
            P(group),
            P(),
            P(),
            P(None, group, "tp"),
            P(None, "tp"),
            P("tp", group),
            P(group, "tp"),
            P("tp"),
            P("tp", group),
            P(),
        ),
        out_specs=(
            P(group + ("tp",), None),
            P(group + ("tp",), None),
            P(),
            P(),
            P(None, group, "tp"),
            P(None, "tp"),
            P("tp", group),
            P(group, "tp"),
            P("tp"),
            P("tp", group),
            P(),
        ),
        check_vma=False,
    )
```

```python
import functools
import math

import jax
import jax.numpy as jnp
from jax import lax
from jax.experimental import pallas as pl
from jax.experimental.pallas import tpu as pltpu
from jax.sharding import Mesh
from jax.sharding import PartitionSpec as P

HD = 64
ROT = 32
RUN = 256
EPS = 1e-05
NEG = -1e30
F32 = jnp.float32
BF = jnp.bfloat16
NN = (((1,), (0,)), ((), ()))
NT = (((1,), (1,)), ((), ()))
TN = (((0,), (0,)), ((), ()))
SWAP = [(0, 1), (1, 0)]
GELU_A = math.sqrt(2.0 / math.pi)
GELU_B = 0.044715
COST = 100.0


def dot(a, b, dims=NN):
    return lax.dot_general(a, b, dims, preferred_element_type=F32)


ANY = pl.BlockSpec(memory_space=pl.ANY)


def call(body, name, grid, in_specs, out_specs, out_shape, scratch, flops, moved, prefetch=1, vmem=60, collective=None):
    return pl.pallas_call(
        body,
        out_shape=out_shape,
        grid_spec=pltpu.PrefetchScalarGridSpec(
            num_scalar_prefetch=prefetch,
            grid=grid,
            in_specs=in_specs,
            out_specs=out_specs,
            scratch_shapes=scratch,
        ),
        compiler_params=pltpu.CompilerParams(
            vmem_limit_bytes=vmem << 20,
            dimension_semantics=("arbitrary",) * len(grid),
            collective_id=collective,
            has_side_effects=collective is not None,
        ),
        cost_estimate=pl.CostEstimate(flops=int(flops * COST), bytes_accessed=int(moved * COST), transcendentals=0),
        name=name,
    )


def row_block(size, width):
    return pl.BlockSpec((size, width), lambda i, s: (i, 0))


def fixed(shape, index=None):
    place = index or (0,) * len(shape)
    return pl.BlockSpec(shape, lambda i, s: place, pipeline_mode=pl.Buffered(1))


def norm_parts(rows):
    center = rows - jnp.mean(rows, axis=-1, keepdims=True)
    inverse = lax.rsqrt(jnp.mean(center * center, axis=-1, keepdims=True) + EPS)
    return center * inverse, inverse


def lanes_of(info, chunk, piece):
    return pl.ds(pl.multiple_of((piece ^ info[0]) * chunk, chunk), chunk)


def to_neighbour(source, target, sends, receives, n, axis, at):
    return pltpu.make_async_remote_copy(
        src_ref=source,
        dst_ref=target,
        send_sem=sends.at[n],
        recv_sem=receives.at[n],
        device_id={axis: at},
        device_id_type=pl.DeviceIdType.MESH,
    )


def begin_body(tok, cot, gain, shift, in_ref, out_ref, up_any, down_any, nrm, cot_out, wa, vm_low, vm_high, cot_sum, chip_a, away_a, chip_m, away_m, up_ref, down_ref, nbuf, cbuf, loads, locals_, sends, receives, *, chunk, square, steps):
    i = pl.program_id(0)
    core, x, y = lax.axis_index("cc"), lax.axis_index("cx"), lax.axis_index("fsdp")
    shard = in_ref.shape[1]
    size, depth = tok.shape
    width, wide = chip_a.shape[1] // 4, chip_m.shape[1] // 2
    mine = pl.ds(pl.multiple_of(core * shard, shard), shard)
    rows = 2 * shard
    peers = [("cc", 1 - core)] + ([("cx", 1 - x), ("fsdp", 1 - y)] if square else [])

    load_up = pltpu.make_async_copy(up_any, up_ref, loads.at[0])
    load_down = pltpu.make_async_copy(down_any, down_ref, loads.at[1])
    swap_a = to_neighbour(away_a, chip_a.at[mine, :], sends, receives, 0, "cc", 1 - core)
    swap_m = to_neighbour(away_m, chip_m.at[mine, :], sends, receives, 1, "cc", 1 - core)
    keep_a = pltpu.make_async_copy(chip_a, wa.at[pl.ds(0, rows), :], locals_.at[0])
    keep_m = [
        pltpu.make_async_copy(chip_m.at[pl.ds(0, shard), :], vm_low, locals_.at[1]),
        pltpu.make_async_copy(chip_m.at[pl.ds(shard, shard), :], vm_high, locals_.at[2 + 2 * steps]),
    ]
    if square:
        to_x = to_neighbour(chip_a, wa.at[pl.ds(rows, rows), :], sends, receives, 2, "cx", 1 - x)
        to_y = to_neighbour(chip_a, wa.at[pl.ds(2 * rows, rows), :], sends, receives, 3, "fsdp", 1 - y)
        far_x = to_neighbour(
            wa.at[pl.ds(2 * rows, shard), :], wa.at[pl.ds(3 * rows, shard), :], sends, receives, 4, "cx", 1 - x
        )
        far_y = to_neighbour(
            wa.at[pl.ds(rows + shard, shard), :],
            wa.at[pl.ds(3 * rows + shard, shard), :],
            sends,
            receives,
            5,
            "fsdp",
            1 - y,
        )

    def row_copies(j):
        here = pl.ds(pl.multiple_of(j * size, size), size)
        there = pl.ds(pl.multiple_of((j + steps) * size, size), size)
        return [
            pltpu.make_async_copy(nbuf.at[j], nrm.at[here, :], locals_.at[2 + j]),
            pltpu.make_async_copy(cbuf.at[j], cot_out.at[here, :], locals_.at[2 + steps + j]),
            to_neighbour(nbuf.at[j], nrm.at[there, :], sends, receives, 6 + j, "cc", 1 - core),
            to_neighbour(cbuf.at[j], cot_out.at[there, :], sends, receives, 6 + steps + j, "cc", 1 - core),
        ]

    @pl.when(i == 0)
    def _():
        barrier = pltpu.get_barrier_semaphore()
        for axis, at in peers:
            pl.semaphore_signal(barrier, inc=1, device_id={axis: at}, device_id_type=pl.DeviceIdType.MESH)
        load_up.start()
        load_down.start()
        for target, c, at in ((chip_a, core, mine), (away_a, 1 - core, pl.ds(0, shard))):
            cut = pl.ds(pl.multiple_of(c * width, width), width)
            for j in range(3):
                target[at, width * j : width * j + width] = in_ref[j, :, cut]
            target[at, 3 * width :] = out_ref[cut, :].astype(F32).T.astype(BF)
        pl.semaphore_wait(barrier, len(peers))
        swap_a.start()
        load_up.wait()
        load_down.wait()
        for target, c, at in ((away_m, 1 - core, pl.ds(0, shard)), (chip_m, core, mine)):
            cut = pl.ds(pl.multiple_of(c * wide, wide), wide)
            target[at, :wide] = up_ref[:, cut]
            target[at, wide:] = down_ref[cut, :].astype(F32).T.astype(BF)
            if target is away_m:
                swap_m.start()
                swap_a.wait()
                if square:
                    to_x.start()
                    to_y.start()
                keep_a.start()
        cot_sum[...] = jnp.zeros_like(cot_sum)

    center, _ = norm_parts(tok[...].astype(F32))
    full = (center * gain[...].astype(F32)[None] + shift[...].astype(F32)[None]).astype(BF)
    cot_sum[...] += jnp.sum(cot[...].astype(F32), axis=0, keepdims=True)
    for r in range(depth // chunk):
        place = ((r // 2 + y) % 2) * 2 + (r % 2 + x) % 2 if square else r
        lanes = pl.ds(pl.multiple_of(place * chunk, chunk), chunk) if square else pl.ds(r * chunk, chunk)
        nbuf[i, :, lanes] = full[:, r * chunk : r * chunk + chunk]
        cbuf[i, :, lanes] = cot[:, r * chunk : r * chunk + chunk]
    for copy in row_copies(i):
        copy.start()

    @pl.when(i == steps - 1)
    def _():
        swap_m.wait()
        for copy in keep_m:
            copy.start()
        if square:
            to_y.wait()
            far_x.start()
            to_x.wait()
            far_y.start()
        keep_a.wait()
        for copy in keep_m:
            copy.wait()

        def finish(j, c):
            for copy in row_copies(j):
                copy.wait()
            return c

        lax.fori_loop(0, steps, finish, 0)
        if square:
            far_x.wait()
            far_y.wait()


def begin(tokens, cot, gain, shift, in_proj, out_proj, up_proj, down_proj, chunk, square):
    length, depth = tokens.shape
    steps = 4
    size = length // steps
    shard = in_proj.shape[1]
    width, wide = in_proj.shape[2] // 2, up_proj.shape[1] // 2
    block = pl.BlockSpec((size, depth), lambda i: (i, 0))
    whole = lambda shape: pl.BlockSpec(shape, lambda i: (0,) * len(shape), pipeline_mode=pl.Buffered(1))
    rows = 8 * shard if square else 2 * shard
    return call(
        functools.partial(begin_body, chunk=chunk, square=square, steps=steps),
        "begin",
        (steps,),
        [block, block, whole((depth,)), whole((depth,)), whole(in_proj.shape), whole(out_proj.shape), ANY, ANY],
        [ANY, ANY, ANY, ANY, ANY, pl.BlockSpec((1, depth), lambda i: (0, 0))],
        [
            jax.ShapeDtypeStruct((2 * length, depth), BF),
            jax.ShapeDtypeStruct((2 * length, depth), BF),
            jax.ShapeDtypeStruct((rows, 4 * width), BF),
            jax.ShapeDtypeStruct((shard, 2 * wide), BF),
            jax.ShapeDtypeStruct((shard, 2 * wide), BF),
            jax.ShapeDtypeStruct((1, depth), F32),
        ],
        [
            pltpu.VMEM((2 * shard, 4 * width), BF),
            pltpu.VMEM((shard, 4 * width), BF),
            pltpu.VMEM((2 * shard, 2 * wide), BF),
            pltpu.VMEM((shard, 2 * wide), BF),
            pltpu.VMEM(up_proj.shape, BF),
            pltpu.VMEM(down_proj.shape, BF),
            pltpu.VMEM((steps, size, depth), BF),
            pltpu.VMEM((steps, size, depth), BF),
            pltpu.SemaphoreType.DMA((2,)),
            pltpu.SemaphoreType.DMA((3 + 2 * steps,)),
            pltpu.SemaphoreType.DMA((6 + 2 * steps,)),
            pltpu.SemaphoreType.DMA((6 + 2 * steps,)),
        ],
        10 * tokens.size,
        16 * tokens.size,
        prefetch=0,
        collective=0,
    )(tokens, cot, gain, shift, in_proj, out_proj, up_proj, down_proj)


def rotary_tables(rates, positions, sign):
    angles = rates * positions
    cos_rows, sin_rows = jnp.cos(angles), sign * jnp.sin(angles)
    one = jnp.ones((HD - ROT, cos_rows.shape[1]), F32)
    none = jnp.zeros((HD - ROT, cos_rows.shape[1]), F32)
    few = jnp.zeros_like(cos_rows)
    return (
        jnp.concatenate([cos_rows, cos_rows, one] * 2, axis=0).T,
        jnp.concatenate([-sin_rows, few, none] * 2, axis=0).T,
        jnp.concatenate([few, sin_rows, none] * 2, axis=0).T,
    )


def turn(values, cos_part, down, up):
    return (
        values * cos_part
        + pltpu.roll(values, 128 - ROT // 2, 1) * down
        + pltpu.roll(values, ROT // 2, 1) * up
    )


def stay(shape):
    return pl.BlockSpec(shape, lambda i, s: (0,) * len(shape))


def start_body(tok, cot, gain, shift, in_ref, out_ref, up_any, down_any, bias, own_at, rates, nrm_out, cot_out, wa_out, vm_low, vm_high, q_out, kv_out, do_out, came_out, cot_sum, away_a, chip_m, away_m, up_ref, down_ref, full_n, full_c, wa, acc, positions, q_hold, kv_hold, do_hold, send_hold, loads, locals_, sends, receives, *, chunk, steps, size):
    i = pl.program_id(0)
    core, x, y = lax.axis_index("cc"), lax.axis_index("cx"), lax.axis_index("fsdp")
    shard = in_ref.shape[1]
    length, depth = steps * tok.shape[0], tok.shape[1]
    block = tok.shape[0]
    width, wide = away_a.shape[1] // 4, chip_m.shape[1] // 2
    rows = 2 * shard
    mine = pl.ds(pl.multiple_of(core * shard, shard), shard)
    peers = [("cc", 1 - core), ("cx", 1 - x), ("fsdp", 1 - y)]

    load_up = pltpu.make_async_copy(up_any, up_ref, loads.at[0])
    load_down = pltpu.make_async_copy(down_any, down_ref, loads.at[1])
    swap_a = to_neighbour(away_a, wa.at[mine, :], sends, receives, 0, "cc", 1 - core)
    swap_m = to_neighbour(away_m, chip_m.at[mine, :], sends, receives, 1, "cc", 1 - core)
    home = wa.at[pl.ds(0, rows), :]
    to_x = to_neighbour(home, wa.at[pl.ds(rows, rows), :], sends, receives, 2, "cx", 1 - x)
    to_y = to_neighbour(home, wa.at[pl.ds(2 * rows, rows), :], sends, receives, 3, "fsdp", 1 - y)
    part = wa.at[pl.ds(3 * rows, shard), :]
    far_x = to_neighbour(wa.at[pl.ds(2 * rows, shard), :], part, sends, receives, 4, "cx", 1 - x)
    part = wa.at[pl.ds(3 * rows + shard, shard), :]
    far_y = to_neighbour(wa.at[pl.ds(rows + shard, shard), :], part, sends, receives, 5, "fsdp", 1 - y)
    swap_at = to_neighbour(own_at, positions.at[:, pl.ds(length, length)], sends, receives, 6, "cc", 1 - core)
    halves = [pl.ds(0, length), pl.ds(length, length)]
    stores = [
        [pltpu.make_async_copy(held.at[half, :], out.at[half, :], locals_.at[2 * k + n]) for k, half in enumerate(halves)]
        for n, (held, out) in enumerate(((full_n, nrm_out), (full_c, cot_out)))
    ]
    keep = [
        pltpu.make_async_copy(wa, wa_out, locals_.at[4]),
        pltpu.make_async_copy(chip_m.at[pl.ds(0, shard), :], vm_low, locals_.at[5]),
        pltpu.make_async_copy(chip_m.at[pl.ds(shard, shard), :], vm_high, locals_.at[6]),
    ]

    def row_copies(j):
        here = pl.ds(pl.multiple_of(j * block, block), block)
        there = pl.ds(pl.multiple_of((j + steps) * block, block), block)
        return [
            to_neighbour(full_n.at[here, :], full_n.at[there, :], sends, receives, 7 + j, "cc", 1 - core),
            to_neighbour(full_c.at[here, :], full_c.at[there, :], sends, receives, 7 + steps + j, "cc", 1 - core),
        ]

    @pl.when(i == 0)
    def _():
        barrier = pltpu.get_barrier_semaphore()
        for axis, at in peers:
            pl.semaphore_signal(barrier, inc=1, device_id={axis: at}, device_id_type=pl.DeviceIdType.MESH)
        load_up.start()
        load_down.start()
        for target, c, at in ((wa, core, mine), (away_a, 1 - core, pl.ds(0, shard))):
            cut = pl.ds(pl.multiple_of(c * width, width), width)
            for j in range(3):
                target[at, width * j : width * j + width] = in_ref[j, :, cut]
            target[at, 3 * width :] = out_ref[cut, :].astype(F32).T.astype(BF)
        pl.semaphore_wait(barrier, len(peers))
        swap_a.start()
        swap_at.start()
        positions[:, :length] = own_at[...]
        load_up.wait()
        load_down.wait()
        for target, c, at in ((away_m, 1 - core, pl.ds(0, shard)), (chip_m, core, mine)):
            cut = pl.ds(pl.multiple_of(c * wide, wide), wide)
            target[at, :wide] = up_ref[:, cut]
            target[at, wide:] = down_ref[cut, :].astype(F32).T.astype(BF)
            if target is away_m:
                swap_m.start()
                swap_a.wait()
                to_x.start()
                to_y.start()
        cot_sum[...] = jnp.zeros_like(cot_sum)

    center, _ = norm_parts(tok[...].astype(F32))
    full = (center * gain[...].astype(F32)[None] + shift[...].astype(F32)[None]).astype(BF)
    cot_sum[...] += jnp.sum(cot[...].astype(F32), axis=0, keepdims=True)
    here = pl.ds(pl.multiple_of(i * block, block), block)
    for r in range(depth // chunk):
        place = ((r // 2 + y) % 2) * 2 + (r % 2 + x) % 2
        lanes = pl.ds(pl.multiple_of(place * chunk, chunk), chunk)
        full_n[here, lanes] = full[:, r * chunk : r * chunk + chunk]
        full_c[here, lanes] = cot[:, r * chunk : r * chunk + chunk]
    for copy in row_copies(i):
        copy.start()

    def products(at, low, high):
        return (
            dot(full_n[at, low:high], wa[low:high, : 3 * width]),
            dot(full_c[at, low:high], wa[low:high, 3 * width :]),
        )

    def outputs(r):
        at = pl.ds(pl.multiple_of(r * size, size), size)
        pairs = ((q_hold, q_out), (kv_hold, kv_out), (do_hold, do_out))
        return [
            pltpu.make_async_copy(held.at[at, :], out.at[at, :], locals_.at[7 + 3 * r + n])
            for n, (held, out) in enumerate(pairs)
        ]

    def across(r):
        at = pl.ds(pl.multiple_of(r * size, size), size)
        return to_neighbour(
            send_hold.at[at, :], came_out.at[at, :], sends, receives, 7 + 2 * steps + r, "cx", 1 - x
        )

    @pl.when(i == steps - 1)
    def _():
        count = 2 * length // size
        for pair in stores:
            pair[0].start()
        swap_m.wait()
        keep[1].start()
        keep[2].start()
        swap_at.wait()

        def arrive(j, c):
            for copy in row_copies(j):
                copy.wait()
            return c

        lax.fori_loop(0, steps, arrive, 0)
        for pair in stores:
            pair[1].start()

        def first(r, c):
            at = pl.ds(pl.multiple_of(r * size, size), size)
            acc[at, : 3 * width], acc[at, 3 * width :] = products(at, 0, chunk)
            return c

        lax.fori_loop(0, count, first, 0)
        to_y.wait()
        far_x.start()
        to_x.wait()
        far_y.start()

        def second(r, c):
            at = pl.ds(pl.multiple_of(r * size, size), size)
            packed, do = products(at, chunk, 3 * chunk)
            acc[at, : 3 * width] += packed
            acc[at, 3 * width :] += do
            return c

        lax.fori_loop(0, count, second, 0)
        far_x.wait()
        far_y.wait()
        keep[0].start()
        mine_w = pl.ds(pl.multiple_of(core * width, width), width)
        half = width // 2

        def biases(j, low, high):
            return bias[j : j + 1, mine_w][:, low:high].astype(F32)

        def third(r, carry):
            at = pl.ds(pl.multiple_of(r * size, size), size)
            packed, do = products(at, 3 * chunk, 4 * chunk)
            packed = packed + acc[at, : 3 * width]
            do = do + acc[at, 3 * width :]
            acc[at, : 3 * width] = packed
            acc[at, 3 * width :] = do
            c, d, u = rotary_tables(rates[...], positions[:, at], 1.0)
            query = packed[:, half:width] + biases(0, half, width)
            key = packed[:, width : width + half] + biases(1, 0, half)
            value = packed[:, 2 * width : 2 * width + half] + biases(2, 0, half)
            first_part = jnp.where(x == 0, key, query)
            for k in range(0, half, 128):
                send_hold[at, k : k + 128] = turn(first_part[:, k : k + 128], c, d, u).astype(BF)
            send_hold[at, half:] = jnp.where(x == 0, value, do[:, half:]).astype(BF)
            across(r).start()
            return carry

        lax.fori_loop(0, count, third, 0)

        def fourth(r, carry):
            at = pl.ds(pl.multiple_of(r * size, size), size)
            c, d, u = rotary_tables(rates[...], positions[:, at], 1.0)
            for j, hold in ((0, q_hold), (1, kv_hold)):
                rows_j = acc[at, width * j : width * j + width] + biases(j, 0, width)
                for k in range(0, width, 128):
                    hold[at, k : k + 128] = turn(rows_j[:, k : k + 128], c, d, u).astype(BF)
            kv_hold[at, width:] = (acc[at, 2 * width : 3 * width] + biases(2, 0, width)).astype(BF)
            do_hold[at, :] = acc[at, 3 * width :].astype(BF)
            for copy in outputs(r):
                copy.start()
            return carry

        lax.fori_loop(0, count, fourth, 0)
        for copy in keep + stores[0] + stores[1]:
            copy.wait()

        def finish(r, c):
            for copy in outputs(r):
                copy.wait()
            across(r).wait()
            return c

        lax.fori_loop(0, count, finish, 0)


def start(tokens, cot, gain, shift, in_proj, out_proj, up_proj, down_proj, in_bias, own_at, rates, chunk):
    length, depth = tokens.shape
    steps = 4
    block = length // steps
    size = 256
    count = 2 * length // size
    shard = in_proj.shape[1]
    width, wide = in_proj.shape[2] // 2, up_proj.shape[1] // 2
    spec = pl.BlockSpec((block, depth), lambda i: (i, 0))
    whole = lambda array: pl.BlockSpec(array.shape, lambda i: (0,) * array.ndim, pipeline_mode=pl.Buffered(1))
    both = jax.ShapeDtypeStruct((2 * length, depth), BF)
    heads = [jax.ShapeDtypeStruct((2 * length, n * width), BF) for n in (1, 2, 1, 1)]
    return call(
        functools.partial(start_body, chunk=chunk, steps=steps, size=size),
        "start",
        (steps,),
        [spec, spec, whole(gain), whole(shift), whole(in_proj), whole(out_proj), ANY, ANY]
        + [whole(in_bias), whole(own_at), whole(rates)],
        [ANY] * 9 + [pl.BlockSpec((1, depth), lambda i: (0, 0))],
        [both, both, jax.ShapeDtypeStruct((depth, 4 * width), BF)]
        + [jax.ShapeDtypeStruct((shard, 2 * wide), BF)] * 2
        + heads
        + [jax.ShapeDtypeStruct((1, depth), F32)],
        [
            pltpu.VMEM((shard, 4 * width), BF),
            pltpu.VMEM((2 * shard, 2 * wide), BF),
            pltpu.VMEM((shard, 2 * wide), BF),
            pltpu.VMEM(up_proj.shape, BF),
            pltpu.VMEM(down_proj.shape, BF),
            pltpu.VMEM((2 * length, depth), BF),
            pltpu.VMEM((2 * length, depth), BF),
            pltpu.VMEM((depth, 4 * width), BF),
            pltpu.VMEM((2 * length, 4 * width), F32),
            pltpu.VMEM((1, 2 * length), F32),
        ]
        + [pltpu.VMEM(head.shape, BF) for head in heads]
        + [
            pltpu.SemaphoreType.DMA((2,)),
            pltpu.SemaphoreType.DMA((7 + 3 * count,)),
            pltpu.SemaphoreType.DMA((7 + 2 * steps + count,)),
            pltpu.SemaphoreType.DMA((7 + 2 * steps + count,)),
        ],
        20 * tokens.size,
        16 * tokens.size,
        prefetch=0,
        collective=0,
    )(tokens, cot, gain, shift, in_proj, out_proj, up_proj, down_proj, in_bias, own_at, rates)


def piece_copies(pieces, columns, target, sems):
    copies, at = [], 0
    for n, piece in enumerate(pieces):
        count = piece.shape[0]
        copies.append(
            pltpu.make_async_copy(piece.at[:, columns], target.at[pl.ds(at, count), :], sems.at[n])
        )
        at += count
    return copies


def place_pieces(*jobs):
    copies = [copy for job in jobs for copy in piece_copies(*job)]
    for copy in copies:
        copy.start()
    for copy in copies:
        copy.wait()


def move_sems(pieces):
    return pltpu.SemaphoreType.DMA((len(pieces),))


def project_body(info, nrm, cot, weights, bias, rates, positions, q_out, kv_out, do_out, send, *, width):
    packed = dot(nrm[...], weights[:, : 3 * width]) + bias[...].astype(F32)
    do = dot(cot[...], weights[:, 3 * width :]).astype(BF)
    c, d, u = rotary_tables(rates[...], positions[...], 1.0)
    low = []
    for p in range(2 * width // 128):
        low.append(turn(packed[:, 128 * p : 128 * p + 128], c, d, u).astype(BF))
    pairs = width // 128
    queries = jnp.concatenate(low[:pairs], axis=1)
    keys = jnp.concatenate(low[pairs:], axis=1)
    values = packed[:, 2 * width :].astype(BF)
    q_out[...] = queries
    kv_out[:, :width] = keys
    kv_out[:, width:] = values
    do_out[...] = do
    part = width // 2

    @pl.when(info[3] == 0)
    def _():
        send[:, :part] = keys[:, :part]
        send[:, part:] = values[:, :part]

    @pl.when(info[3] != 0)
    def _():
        send[:, :part] = queries[:, part:]
        send[:, part:] = do[:, part:]


def project(info, normed, cot, weights, bias, tables, width):
    rows, depth = normed.shape
    size = min(rows, 256)
    return call(
        functools.partial(project_body, width=width),
        "project",
        (rows // size,),
        [row_block(size, depth)] * 2 + [fixed((depth, 4 * width)), fixed((1, 3 * width))]
        + [fixed((ROT // 2, 1)), pl.BlockSpec((1, size), lambda i, s: (0, i))],
        [row_block(size, width), row_block(size, 2 * width), row_block(size, width), row_block(size, width)],
        [jax.ShapeDtypeStruct((rows, n * width), BF) for n in (1, 2, 1, 1)],
        [],
        2 * rows * depth * 4 * width,
        2 * (2 * rows * depth + depth * 4 * width + 5 * rows * width),
    )(info, normed, cot, weights, bias, *tables)


def spread_body(a, b, *rest, counts, columns, sums, per):
    na, nb = counts
    wa, wb = rest[:na], rest[na : na + nb]
    rest = rest[na + nb :]
    normed = rest[:sums]
    out = rest[sums]
    totals = rest[sums + 1 : 3 * sums + 1]
    hold_a, hold_b, sem_a, sem_b, outgoing, incoming, send_sems, recv_sems = rest[3 * sums + 1 :]
    i = pl.program_id(0)
    core = lax.axis_index("cc")

    def copy(j):
        return pltpu.make_async_remote_copy(
            src_ref=outgoing.at[j],
            dst_ref=incoming.at[j],
            send_sem=send_sems.at[j],
            recv_sem=recv_sems.at[j],
            device_id={"cc": 1 - core},
            device_id_type=pl.DeviceIdType.MESH,
        )

    @pl.when(i == 0)
    def _():
        barrier = pltpu.get_barrier_semaphore()
        pl.semaphore_signal(barrier, inc=1, device_id={"cc": 1 - core}, device_id_type=pl.DeviceIdType.MESH)
        place_pieces((wa, columns[0], hold_a, sem_a), (wb, columns[1], hold_b, sem_b))
        pl.semaphore_wait(barrier, 1)
        for total in totals:
            total[...] = jnp.zeros_like(total)

    total = dot(a[...], hold_a[...], NT) + dot(b[...], hold_b[...], NT)

    @pl.when(i < per)
    def _():
        outgoing[i] = total.astype(BF)
        copy(i).start()

    @pl.when(i >= per)
    def _():
        copy(i - per).wait()
        full = total + incoming[i - per].astype(F32)
        out[...] = full.astype(BF)
        if sums:
            totals[0][...] += jnp.sum(full * normed[0][...].astype(F32), axis=0, keepdims=True)
            totals[1][...] += jnp.sum(full, axis=0, keepdims=True)


def spread(a, b, wa, wb, ca, cb, depth, name, collective, normed=()):
    rows = a.shape[0] // 2
    size = min(rows, 256)
    per = rows // size
    at = lambda width: pl.BlockSpec((size, width), lambda i: ((i + per) % (2 * per), 0))
    later = pl.BlockSpec((size, depth), lambda i: (jnp.maximum(i - per, 0), 0))
    one = pl.BlockSpec((1, depth), lambda i: (0, 0))
    wide_a, wide_b = a.shape[1], b.shape[1]
    count = len(normed)
    return call(
        functools.partial(
            spread_body,
            counts=(len(wa), len(wb)),
            columns=(slice(ca, ca + wide_a), slice(cb, cb + wide_b)),
            sums=count,
            per=per,
        ),
        name,
        (2 * per,),
        [at(wide_a), at(wide_b)] + [ANY] * (len(wa) + len(wb)) + [later] * count,
        [later] + [one] * (2 * count),
        [jax.ShapeDtypeStruct((rows, depth), BF)] + [jax.ShapeDtypeStruct((1, depth), F32)] * (2 * count),
        [
            pltpu.VMEM((depth, wide_a), BF),
            pltpu.VMEM((depth, wide_b), BF),
            move_sems(wa),
            move_sems(wb),
            pltpu.VMEM((per, size, depth), BF),
            pltpu.VMEM((per, size, depth), BF),
            pltpu.SemaphoreType.DMA((per,)),
            pltpu.SemaphoreType.DMA((per,)),
        ],
        4 * rows * depth * (wide_a + wide_b),
        2 * (2 * rows + depth) * (wide_a + wide_b) + 2 * rows * depth,
        prefetch=0,
        collective=collective,
    )(a, b, *wa, *wb, *normed)


def branch_body(nrm, cot, att, bias, wa, *rest, count, column):
    pieces = rest[:count]
    act_out, grad_out, sum_out, out, hold, hold_a, sem, sem_a, outgoing, incoming, send_sems, recv_sems = rest[count:]
    i = pl.program_id(0)
    per = outgoing.shape[0]
    width = act_out.shape[1]
    core = lax.axis_index("cc")

    def copy(j):
        return to_neighbour(outgoing.at[j], incoming.at[j], send_sems, recv_sems, j, "cc", 1 - core)

    @pl.when(i == 0)
    def _():
        barrier = pltpu.get_barrier_semaphore()
        pl.semaphore_signal(barrier, inc=1, device_id={"cc": 1 - core}, device_id_type=pl.DeviceIdType.MESH)
        place_pieces((pieces, slice(0, 2 * width), hold, sem), ([wa], slice(column, column + att.shape[1]), hold_a, sem_a))
        sum_out[...] = jnp.zeros_like(sum_out)
        pl.semaphore_wait(barrier, 1)

    u = dot(nrm[...], hold[:, :width]) + bias[...].astype(F32)
    g = dot(cot[...], hold[:, width:])
    square = u * u
    t = jnp.tanh(GELU_A * (u + GELU_B * square * u))
    half = 0.5 * (1.0 + t)
    act = (u * half).astype(BF)
    act_out[...] = act
    total = dot(att[...], hold_a[...], NT) + dot(act, hold[:, width:], NT)
    slope = half + 0.5 * u * (1.0 - t * t) * (GELU_A * (1.0 + 3.0 * GELU_B * square))
    low = (g * slope).astype(BF)
    grad_out[...] = low
    sum_out[...] += jnp.sum(low.astype(F32), axis=0, keepdims=True)

    @pl.when(i < per)
    def _():
        outgoing[i] = total.astype(BF)
        copy(i).start()

    @pl.when(i >= per)
    def _():
        copy(i - per).wait()
        out[...] = (total + incoming[i - per].astype(F32)).astype(BF)


def branch_rows(normed, cot, attended, bias, wa, pieces, column):
    rows, depth = normed.shape
    width = bias.shape[1]
    wide_a = attended.shape[1]
    size = min(rows // 2, 256)
    per = rows // 2 // size
    at = lambda wide: pl.BlockSpec((size, wide), lambda i: ((i + per) % (2 * per), 0))
    one = lambda wide: pl.BlockSpec((1, wide), lambda i: (0, 0))
    return call(
        functools.partial(branch_body, count=len(pieces), column=column),
        "branch",
        (2 * per,),
        [at(depth), at(depth), at(wide_a), one(width)] + [ANY] * (1 + len(pieces)),
        [at(width), at(width), one(width), pl.BlockSpec((size, depth), lambda i: (jnp.maximum(i - per, 0), 0))],
        [jax.ShapeDtypeStruct((rows, width), BF)] * 2
        + [jax.ShapeDtypeStruct((1, width), F32), jax.ShapeDtypeStruct((rows // 2, depth), BF)],
        [
            pltpu.VMEM((depth, 2 * width), BF),
            pltpu.VMEM((depth, wide_a), BF),
            move_sems(pieces),
            move_sems([wa]),
            pltpu.VMEM((per, size, depth), BF),
            pltpu.VMEM((per, size, depth), BF),
            pltpu.SemaphoreType.DMA((per,)),
            pltpu.SemaphoreType.DMA((per,)),
        ],
        2 * rows * depth * (3 * width + wide_a),
        2 * (3 * rows * depth + depth * (2 * width + wide_a) + 2 * rows * width),
        prefetch=0,
        collective=1,
    )(normed, cot, attended, bias, wa, *pieces)


def outer_body(info, left_n, left_c, right_n, right_c, *rest, order, outputs):
    i = pl.program_id(0)
    outs = rest[:-3]
    hold_n, hold_c, sems = rest[-3:]
    loads = (
        pltpu.make_async_copy(right_n, hold_n, sems.at[0]),
        pltpu.make_async_copy(right_c, hold_c, sems.at[1]),
    )
    kinds = [kind for _, kind in order]

    @pl.when(i == 0)
    def _():
        loads[kinds[0]].start()
        loads[1 - kinds[0]].start()

    for kind in (0, 1):

        @pl.when(i == kinds.index(kind))
        def _(kind=kind):
            loads[kind].wait()

    for step, (block, kind) in enumerate(order):
        left, right = ((left_n, hold_n), (left_c, hold_c))[kind]

        @pl.when(i == step)
        def _(block=block, kind=kind, left=left, right=right):
            result = dot(left[...], right[...], TN).astype(BF)
            for out, (blocks, parts) in zip(outs, outputs):
                if block in blocks and kind in parts:
                    source, target = parts[kind]
                    out[:, target] = result[:, source]


def by_step(table):
    def at(i):
        value = table[-1]
        for step in range(len(table) - 1):
            value = jnp.where(i == step, table[step], value)
        return value

    return at


def places(order, find):
    used = [find(*entry) for entry in order]
    table, upcoming = [None] * len(used), None
    for step in reversed(range(len(used))):
        upcoming = used[step] if used[step] is not None else upcoming
        table[step] = upcoming
    last = None
    for step, value in enumerate(table):
        last = value if value is not None else last
        table[step] = last
    return by_step(table)


def outer(info, normed, cot, right_n, right_c, chunk, order, outputs, name):
    rows = right_n.shape[0]
    wide = (right_n.shape[1], right_c.shape[1])

    def left(which):
        at = places(order, lambda block, kind: block if kind == which else None)
        return pl.BlockSpec((rows, chunk), lambda i, s: (0, at(i)))

    out_specs, out_shapes = [], []
    for blocks, parts in outputs:
        width = max(target.stop for _, target in parts.values())
        at = places(order, lambda block, kind: blocks.index(block) if block in blocks and kind in parts else None)
        out_specs.append(pl.BlockSpec((chunk, width), lambda i, s, at=at: (at(i), 0)))
        out_shapes.append(jax.ShapeDtypeStruct((len(blocks) * chunk, width), BF))
    return call(
        functools.partial(outer_body, order=order, outputs=outputs),
        name,
        (len(order),),
        [left(0), left(1), ANY, ANY],
        out_specs,
        out_shapes,
        [pltpu.VMEM((rows, wide[0]), BF), pltpu.VMEM((rows, wide[1]), BF), pltpu.SemaphoreType.DMA((2,))],
        rows * chunk * len(order) * sum(wide),
        2 * (rows + chunk) * len(order) * sum(wide),
    )(info, normed, cot, right_n, right_c)


def head_masks(block, scale):
    lane = lax.broadcasted_iota(jnp.int32, block.shape, 1)
    v = block.astype(F32) * scale
    return (jnp.where(lane < HD, v, 0.0).astype(BF), jnp.where(lane < HD, 0.0, v).astype(BF))


def own_mask(flag, width):
    kk = lax.broadcasted_iota(jnp.int32, (RUN, width), 0)
    qq = lax.broadcasted_iota(jnp.int32, (RUN, width), 1)
    return kk <= qq + flag * RUN


def each_prefix(here, half, runs, work):
    size = runs // 2
    while size:

        @pl.when((here & size) != 0)
        def _(size=size):
            low = here & ((runs - 1) & ~(2 * size - 1))
            work(pl.multiple_of((low ^ half) * RUN, RUN), size * RUN)

        size //= 2


def softmax_blocks(state, heads, k_r, vt_r, qm, start, size, mask=None):
    acc, ml = state

    def score(n):
        p, h = divmod(n, 2)
        s = dot(k_r[pl.ds(start, size), 128 * p : 128 * p + 128], qm[p][h], NT)
        return s if mask is None else jnp.where(mask, s, NEG)

    def rest(n, s):
        top = jnp.max(s, axis=0, keepdims=True)
        rows = slice(HD * n, HD * n + HD)
        vb = vt_r[rows, pl.ds(start, size)]
        m = ml[n : n + 1, :]
        new = jnp.maximum(m, top)
        alpha = jnp.exp(m - new)
        e = jnp.exp(s - new)
        ml[n : n + 1, :] = new
        ml[heads + n : heads + n + 1, :] = ml[heads + n : heads + n + 1, :] * alpha + jnp.sum(e, axis=0, keepdims=True)
        acc[rows, :] = acc[rows, :] * alpha + dot(vb, e.astype(BF))

    s = score(0)
    for n in range(heads):
        following = score(n + 1) if n + 1 < heads else None
        rest(n, s)
        s = following


def start_state(acc, ml, heads):
    acc[...] = jnp.zeros_like(acc)
    ml[:heads, :] = jnp.full((heads, ml.shape[1]), NEG, F32)
    ml[heads:, :] = jnp.zeros((heads, ml.shape[1]), F32)


def finish_state(acc, ml, heads, n):
    l = ml[heads + n : heads + n + 1, :]
    return acc[HD * n : HD * n + HD, :] / l, ml[n : n + 1, :] + jnp.log(l)


def query_masks(block, scale):
    return [head_masks(block[:, 128 * p : 128 * p + 128], scale) for p in range(block.shape[1] // 128)]


SCALE = 1.0 / math.sqrt(HD)


def local_body(info, q_ref, k_ref, v_ref, out_ref, lse_ref, vt, acc, ml, *, heads):
    i = pl.program_id(0)
    half = info[0]
    runs = k_ref.shape[0] // RUN

    @pl.when(i == 0)
    def _():
        vt[...] = v_ref[...].astype(F32).T.astype(BF)

    qm = query_masks(q_ref[...], SCALE)
    start_state(acc, ml, heads)
    work = lambda start, size, mask=None: softmax_blocks((acc, ml), heads, k_ref, vt, qm, start, size, mask)
    work(pl.multiple_of(i * RUN, RUN), RUN, own_mask(info[2 + i], q_ref.shape[0]))
    each_prefix(i ^ half, half, runs, work)
    for n in range(heads):
        out_ref[HD * n : HD * n + HD, :], lse_ref[n : n + 1, :] = finish_state(acc, ml, heads, n)


def attend_local(info, q, kv):
    rows, width = q.shape
    heads = width // HD
    columns = lambda count: pl.BlockSpec((count, RUN), lambda i, s: (0, i))
    return call(
        functools.partial(local_body, heads=heads),
        "attend_local",
        (rows // RUN,),
        [row_block(RUN, width), fixed((rows, width)), fixed((rows, width), (0, 1))],
        [columns(width), columns(heads)],
        [jax.ShapeDtypeStruct((width, rows), F32), jax.ShapeDtypeStruct((heads, rows), F32)],
        [pltpu.VMEM((width, rows), BF), pltpu.VMEM((width, RUN), F32), pltpu.VMEM((2 * heads, RUN), F32)],
        25e9,
        14 * rows * width,
    )(info, q, kv, kv)


def cross_body(info, q_ref, came_ref, came0, came1, k_ref, v_ref, out_ref, lse_ref, keys, vt, acc, ml, *, heads, cut):
    late = info[1] > 0

    @pl.when(pl.program_id(0) == 0)
    def _():
        keys[...] = jnp.where(late, came0[...], k_ref[...])
        vt[...] = jnp.where(late, came1[...], v_ref[...]).astype(F32).T.astype(BF)

    qm = query_masks(jnp.where(late, q_ref[...], came_ref[...]), SCALE)
    start_state(acc, ml, heads)
    for j in range(keys.shape[0] // cut):
        softmax_blocks((acc, ml), heads, keys, vt, qm, j * cut, cut)
    for n in range(heads):
        out, lse_ref[n : n + 1, :] = finish_state(acc, ml, heads, n)
        out_ref[HD * n : HD * n + HD, :] = out.astype(BF)


def cross_specs(rows, part):
    own = lambda i, s: (i, 1 - s[1])
    return (
        pl.BlockSpec((RUN, part), own),
        pl.BlockSpec((RUN, part), lambda i, s: (i, 0)),
        fixed((rows, part)),
        fixed((rows, part), (0, 1)),
        pl.BlockSpec((rows, part), lambda i, s: (0, 1 - s[1])),
        pl.BlockSpec((rows, part), lambda i, s: (0, 3 - s[1])),
    )


def attend_cross(info, q, came, kv):
    rows, part = q.shape[0], q.shape[1] // 2
    heads = part // HD
    query, came_block, came0, came1, key, value = cross_specs(rows, part)
    columns = lambda count: pl.BlockSpec((count, RUN), lambda i, s: (0, i))
    return call(
        functools.partial(cross_body, heads=heads, cut=min(rows, 2048)),
        "attend_cross",
        (rows // RUN,),
        [query, came_block, came0, came1, key, value],
        [columns(part), columns(heads)],
        [jax.ShapeDtypeStruct((part, rows), BF), jax.ShapeDtypeStruct((heads, rows), F32)],
        [
            pltpu.VMEM((rows, part), BF),
            pltpu.VMEM((part, rows), BF),
            pltpu.VMEM((part, RUN), F32),
            pltpu.VMEM((2 * heads, RUN), F32),
        ],
        15e9,
        14 * rows * part,
    )(info, q, came, came, came, kv, kv)


def merge_body(info, local, lse_local, mine, lse_mine, came, lse_came, do_ref, att_ref, stat_ref, early_ref, late_ref, *, heads):
    late = info[1] > 0
    part = heads // 2
    size = do_ref.shape[0]
    do_t = do_ref[...].astype(F32).T
    outs = []
    for n in range(heads):
        other, lse_other, m = (mine, lse_mine, n) if n < part else (came, lse_came, n - part)
        rows = slice(HD * n, HD * n + HD)
        ours = lse_local[n : n + 1, :]
        theirs = jnp.where(late, lse_other[m : m + 1, :], jnp.full((1, size), NEG, F32))
        top = jnp.maximum(ours, theirs)
        a, b = jnp.exp(ours - top), jnp.exp(theirs - top)
        total = a + b
        o = (local[rows, :] * a + other[HD * m : HD * m + HD, :].astype(F32) * b) / total
        outs.append(o)
        lse = top + jnp.log(total)
        delta = jnp.sum(o * do_t[rows, :], axis=0, keepdims=True)
        stat_ref[n : n + 1, :] = lse
        stat_ref[heads + n : heads + n + 1, :] = delta
        for ref, base in ((early_ref, 0), (late_ref, part)):
            if base <= n < base + part:
                ref[n - base : n - base + 1, :] = lse
                ref[part + n - base : part + n - base + 1, :] = delta
    att_ref[...] = jnp.concatenate(outs, axis=0).T.astype(BF)


def merge(info, local, lse_local, mine, lse_mine, came, lse_came, do):
    rows, width = do.shape
    heads = width // HD
    size = min(rows, 512)
    columns = lambda count: pl.BlockSpec((count, size), lambda i, s: (0, i))
    return call(
        functools.partial(merge_body, heads=heads),
        "merge",
        (rows // size,),
        [columns(width), columns(heads)] + [columns(width // 2), columns(heads // 2)] * 2 + [row_block(size, width)],
        [row_block(size, width), columns(2 * heads), columns(heads), columns(heads)],
        [jax.ShapeDtypeStruct((rows, width), BF)]
        + [jax.ShapeDtypeStruct((count, rows), F32) for count in (2 * heads, heads, heads)],
        [],
        20 * rows * width,
        10 * rows * width,
    )(info, local, lse_local, mine, lse_mine, came, lse_came, do)


def gradient_blocks(heads, k_r, v_r, kt_r, dk_r, dv_r, dqt, qm, dm, stat, start, size, mask=None):
    def products(n):
        p, h = divmod(n, 2)
        lanes = slice(128 * p, 128 * p + 128)
        return (
            dot(k_r[pl.ds(start, size), lanes], qm[p][h], NT),
            dot(v_r[pl.ds(start, size), lanes], dm[p][h], NT),
        )

    def rest(n, s, g):
        p, h = divmod(n, 2)
        e = jnp.exp(s - stat[n : n + 1, :])
        if mask is not None:
            e = jnp.where(mask, e, 0.0)
        ds = (e * (g - stat[heads + n : heads + n + 1, :])).astype(BF)
        rows = slice(HD * n, HD * n + HD)
        dqt[rows, :] += dot(kt_r[rows, pl.ds(start, size)], ds)
        return dot(ds, qm[p][h]), dot(e.astype(BF), dm[p][h])

    now = products(0)
    before = None
    for n in range(heads):
        following = products(n + 1) if n + 1 < heads else None
        grads = rest(n, *now)
        now = following
        if n % 2:
            lanes = slice(HD * (n - 1), HD * (n + 1))
            dk_r[pl.ds(start, size), lanes] += before[0] + grads[0]
            dv_r[pl.ds(start, size), lanes] += before[1] + grads[1]
        before = grads


def local_back_body(info, q_ref, do_ref, stat_ref, k_ref, v_ref, dqx, dkx, dvx, came_q, came_k, came_v, rates, positions, out, sums, kt, dqt, dk, dv, *, heads):
    i = pl.program_id(0)
    half = info[0]
    late = info[1] > 0
    runs = k_ref.shape[0] // RUN
    width = HD * heads
    part = width // 2

    @pl.when(i == 0)
    def _():
        kt[...] = k_ref[...].astype(F32).T.astype(BF)

    @pl.when((i == 0) & late)
    def _():
        dk[...] = jnp.zeros_like(dk)
        dv[...] = jnp.zeros_like(dv)

    @pl.when((i == 0) & jnp.logical_not(late))
    def _():
        dk[:, :part] = came_k[...].astype(F32)
        dk[:, part:] = dkx[...]
        dv[:, :part] = came_v[...].astype(F32)
        dv[:, part:] = dvx[...]

    qm = query_masks(q_ref[...], SCALE)
    dm = query_masks(do_ref[...], 1.0)
    dqt[...] = jnp.zeros_like(dqt)

    def work(start, size, mask=None):
        gradient_blocks(heads, k_ref, v_ref, kt, dk, dv, dqt, qm, dm, stat_ref, start, size, mask)

    work(pl.multiple_of(i * RUN, RUN), RUN, own_mask(info[2 + i], q_ref.shape[0]))
    each_prefix(i ^ half, half, runs, work)
    zero = jnp.zeros((q_ref.shape[0], part), F32)
    more = jnp.concatenate(
        [jnp.where(late, dqx[...], zero), jnp.where(late, came_q[...].astype(F32), zero)], axis=1
    )
    found = (dqt[...] * SCALE).T + more
    rows = pl.ds(pl.multiple_of(i * RUN, RUN), RUN)
    c, d, u = rotary_tables(rates[...], positions[:, rows], -1.0)
    for p in range(width // 128):
        lanes = slice(128 * p, 128 * p + 128)
        out[rows, lanes] = turn(found[:, lanes], c, d, u).astype(BF)

    @pl.when(i == pl.num_programs(0) - 1)
    def _():
        def step(j, c):
            at = pl.ds(pl.multiple_of(j * RUN, RUN), RUN)
            c2, d2, u2 = rotary_tables(rates[...], positions[:, at], -1.0)
            for p in range(width // 128):
                lanes = slice(128 * p, 128 * p + 128)
                shifted = slice(width + 128 * p, width + 128 * p + 128)
                out[at, shifted] = turn(dk[at, lanes], c2, d2, u2).astype(BF)
            out[at, 2 * width :] = dv[at, :].astype(BF)
            return c + jnp.sum(out[at, :].astype(F32), axis=0, keepdims=True)

        sums[...] = lax.fori_loop(0, runs, step, jnp.zeros((1, 3 * width), F32))


def back_local(info, q, do, stat, kv, cross, came, tables):
    rows, width = q.shape
    heads = width // HD
    part = width // 2
    blk = row_block(RUN, width)
    few = row_block(RUN, part)
    return call(
        functools.partial(local_back_body, heads=heads),
        "back_local",
        (rows // RUN,),
        [
            blk,
            blk,
            pl.BlockSpec((2 * heads, RUN), lambda i, s: (0, i)),
            fixed((rows, width)),
            fixed((rows, width), (0, 1)),
            few,
            fixed((rows, part)),
            fixed((rows, part)),
            few,
            fixed((rows, part)),
            fixed((rows, part), (0, 1)),
            fixed((ROT // 2, 1)),
            fixed((1, rows)),
        ],
        [stay((rows, 3 * width)), stay((1, 3 * width))],
        [jax.ShapeDtypeStruct((rows, 3 * width), BF), jax.ShapeDtypeStruct((1, 3 * width), F32)],
        [
            pltpu.VMEM((width, rows), BF),
            pltpu.VMEM((width, RUN), F32),
            pltpu.VMEM((rows, width), F32),
            pltpu.VMEM((rows, width), F32),
        ],
        40e9,
        20 * rows * width,
    )(info, q, do, stat, kv, kv, *cross, came, came, came, *tables)


def cross_back_body(info, q_ref, do_ref, came_q, came_do, came0, came1, k_ref, v_ref, early, came_stat, dq_ref, dk_ref, dv_ref, send, keys, values, kt, dqt, *, heads, cut):
    late = info[1] > 0
    i = pl.program_id(0)
    part = HD * heads

    @pl.when(i == 0)
    def _():
        chosen = jnp.where(late, came0[...], k_ref[...])
        keys[...] = chosen
        kt[...] = chosen.astype(F32).T.astype(BF)
        values[...] = jnp.where(late, came1[...], v_ref[...])
        dk_ref[...] = jnp.zeros_like(dk_ref)
        dv_ref[...] = jnp.zeros_like(dv_ref)

    qm = query_masks(jnp.where(late, q_ref[...], came_q[...]), SCALE)
    dm = query_masks(jnp.where(late, do_ref[...], came_do[...]), 1.0)
    dqt[...] = jnp.zeros_like(dqt)
    stat = jnp.where(late, early[...], came_stat[...])
    for j in range(keys.shape[0] // cut):
        gradient_blocks(heads, keys, values, kt, dk_ref, dv_ref, dqt, qm, dm, stat, j * cut, cut)
    found = (dqt[...] * SCALE).T
    dq_ref[...] = found
    rows = pl.ds(pl.multiple_of(i * RUN, RUN), RUN)

    @pl.when(jnp.logical_not(late))
    def _():
        send[rows, :part] = found.astype(BF)
        send[rows, part:] = found.astype(BF)

    @pl.when(late & (i == pl.num_programs(0) - 1))
    def _():
        send[:, :part] = dk_ref[...].astype(BF)
        send[:, part:] = dv_ref[...].astype(BF)


def back_cross(info, q, do, came, kv, early, came_stat):
    rows, part = q.shape[0], q.shape[1] // 2
    heads = part // HD
    query, came_block, came0, came1, key, value = cross_specs(rows, part)
    acc = jax.ShapeDtypeStruct((rows, part), F32)
    return call(
        functools.partial(cross_back_body, heads=heads, cut=min(rows, 1024)),
        "back_cross",
        (rows // RUN,),
        [
            query,
            query,
            came_block,
            pl.BlockSpec((RUN, part), lambda i, s: (i, 1)),
            came0,
            came1,
            key,
            value,
            pl.BlockSpec((2 * heads, RUN), lambda i, s: (0, i)),
            pl.BlockSpec((2 * heads, RUN), lambda i, s: (0, i)),
        ],
        [row_block(RUN, part), stay((rows, part)), stay((rows, part)), stay((rows, 2 * part))],
        [acc, acc, acc, jax.ShapeDtypeStruct((rows, 2 * part), BF)],
        [
            pltpu.VMEM((rows, part), BF),
            pltpu.VMEM((rows, part), BF),
            pltpu.VMEM((part, rows), BF),
            pltpu.VMEM((part, RUN), F32),
        ],
        25e9,
        20 * rows * part,
    )(info, q, do, came, came, came, came, kv, kv, early, came_stat)


def input_body(info, grad, tok, cot, gain, out, *, chunk):
    xhat, inverse = norm_parts(tok[...].astype(F32))
    parts = [grad[:, lanes_of(info, chunk, r)] for r in range(tok.shape[1] // chunk)]
    e = jnp.concatenate(parts, axis=1).astype(F32) * gain[...].astype(F32)
    mean_e = jnp.mean(e, axis=-1, keepdims=True)
    mean_ex = jnp.mean(e * xhat, axis=-1, keepdims=True)
    out[...] = (cot[...].astype(F32) + (e - mean_e - xhat * mean_ex) * inverse).astype(BF)


def input_grads(info, grad, tok, cot, gain, chunk):
    rows, width = grad.shape
    steps = 4
    size = rows // steps
    share = pl.BlockSpec((size, width), lambda i, s: (s[1] * steps + i, 0))
    return call(
        functools.partial(input_body, chunk=chunk),
        "input_grad",
        (steps,),
        [row_block(size, width), share, share, fixed((1, width))],
        [row_block(size, width)],
        [jax.ShapeDtypeStruct((rows, width), BF)],
        [],
        20 * rows * width,
        8 * rows * width,
    )(info, grad, tok, cot, gain[None])[0]


def layer_body(info, branch, tok, bias, out, *, chunk):
    for r in range(tok.shape[1] // chunk):
        at = slice(r * chunk, r * chunk + chunk)
        part = branch[:, lanes_of(info, chunk, r)].astype(F32)
        out[:, at] = (tok[:, at].astype(F32) + part + bias[:, at].astype(F32)).astype(BF)


def layer_rows(info, branch, tok, bias, chunk):
    rows, width = branch.shape
    return call(
        functools.partial(layer_body, chunk=chunk),
        "layer_out",
        (1,),
        [row_block(rows, width), pl.BlockSpec((rows, width), lambda i, s: (s[1], 0)), fixed((1, width))],
        [row_block(rows, width)],
        [jax.ShapeDtypeStruct((rows, width), BF)],
        [],
        4 * branch.size,
        6 * branch.size,
    )(info, branch, tok, bias[None])[0]


def body(tokens, cotangent, piece_ids, positions, norm_gain, norm_shift, in_proj, in_bias, out_proj, up_proj, up_bias, down_proj, out_bias):
    length, depth = tokens.shape
    width = in_bias.shape[1] // 2
    hidden_width = up_bias.shape[0] // 2
    f_count, z_count = lax.axis_size("fsdp"), lax.axis_size("tp")
    x_at, c_at, f_at = lax.axis_index("cx"), lax.axis_index("cc"), lax.axis_index("fsdp")
    square = f_count == 2
    chips = 2 * f_count
    chunk = depth // chips
    me = f_at * 2 + x_at if square else 0 * f_at
    info = jnp.stack([me, lax.axis_index("tp"), c_at, x_at]).astype(jnp.int32)

    other_core = lambda value: lax.ppermute(value, "cc", SWAP)
    by_x = lambda value: lax.ppermute(value, "cx", SWAP)
    by_y = lambda value: lax.ppermute(value, "fsdp", SWAP)

    def pick(value, index, size, axis):
        return lax.dynamic_slice_in_dim(value, index * size, size, axis)

    def in_order(mine, theirs, axis):
        return jnp.where(c_at == 0, jnp.concatenate([mine, theirs], axis), jnp.concatenate([theirs, mine], axis))

    def after(value, *earlier):
        return lax.optimization_barrier((value,) + earlier)[0]

    shard = in_proj.shape[1]
    frequency = 10000.0 ** (-2.0 * jnp.arange(ROT // 2, dtype=F32) / ROT)
    rates = frequency[:, None]
    if square:
        own_at = positions.astype(F32)[None, :]
        normed, cot, weights_a, low_m, high_m, queries, kv, grad_att, came, cot_sum = start(
            tokens, cotangent, norm_gain, norm_shift, in_proj, out_proj, up_proj, down_proj, in_bias, own_at, rates, chunk
        )
    else:
        normed, cot, weights_a, low_m, high_m, cot_sum = begin(
            tokens, cotangent, norm_gain, norm_shift, in_proj, out_proj, up_proj, down_proj, chunk, square
        )
        weights_a = lax.all_gather(weights_a, ("fsdp", "cx"), axis=0, tiled=True)
        both_m = jnp.concatenate([low_m, high_m], axis=0)
        weights_m = [lax.all_gather(both_m, ("fsdp", "cx"), axis=0, tiled=True)]
    small = jnp.stack([piece_ids, positions])
    small = jnp.concatenate([small, other_core(small)], axis=1)
    pieces, rows_at = small[0], small[1]

    tables = (rates, rows_at.astype(F32)[None, :])
    bias_a = pick(in_bias, c_at, width, 1).reshape(1, 3 * width)
    bias_m = pick(up_bias, c_at, hidden_width, 0)[None]
    flags = (pieces.reshape(-1, RUN)[:, 0] > 0).astype(jnp.int32)
    scene = jnp.concatenate([jnp.stack([c_at * (length // RUN), x_at]).astype(jnp.int32), flags])

    if square:
        x_first, y_first, y_second = by_x(low_m), by_y(low_m), by_y(high_m)
    else:
        queries, kv, grad_att, send = project(info, normed, cot, weights_a, bias_a, tables, width)
        came = by_x(send)
    mine, lse_mine = attend_cross(scene, queries, came, kv)
    local, lse_local = attend_local(scene, after(queries, mine, *([x_first, y_first] if square else [])), kv)
    forward_x = lambda value: lax.ppermute(value, "cx", [(0, 1)])
    if square:
        x_second, y_back = by_x(after(high_m, mine)), by_y(x_first)
    attended, stat, stat_early, stat_late = merge(
        scene,
        after(local, x_second, y_second) if square else local,
        lse_local,
        mine,
        lse_mine,
        forward_x(mine),
        forward_x(lse_mine),
        grad_att,
    )
    stat_came = lax.ppermute(stat_late, "cx", [(1, 0)])
    if square:
        weights_m = [low_m, high_m, x_first, x_second, y_first, y_second, y_back, by_x(after(y_second, stat_came))]
    *cross, outgoing = back_cross(scene, queries, grad_att, came, kv, stat_early, stat_came)
    returned = by_x(outgoing)
    active, grad_up, up_sum, ours = branch_rows(
        normed, cot, after(attended, outgoing), bias_m, weights_a, weights_m, 3 * width
    )
    branch = lax.psum_scatter(ours, "tp", scatter_dimension=0, tiled=True)

    def scatter(value):
        return lax.psum_scatter(value, ("fsdp", "cx"), scatter_dimension=0, tiled=True)

    every = tuple(range(chips))
    every_step = tuple((block, kind) for kind in (0, 1) for block in every)

    def columns_of(*parts):
        return {kind: (slice(*source), slice(*target)) for kind, source, target in parts}

    def hidden_weight_grads(last):
        up = columns_of((0, (0, hidden_width), (0, hidden_width)))
        down = columns_of((1, (0, hidden_width), (0, hidden_width)))
        order, outputs = every_step, ((every, up), (every, down))
        if square:
            order = tuple((block, 0) for block in (1, 3, 2, 0)) + tuple((block, 1) for block in (2, 3, 1, 0))
            outputs = (((1, 3), up), ((2,), up), ((0,), up), ((2, 3), down), ((1,), down), ((0,), down))
        return outer(info, after(normed, last), cot, grad_up, active, chunk, order, outputs, "hidden_grads")

    def packed_weight_grads(last):
        wide = 3 * width
        two = 2 * width
        all_in = columns_of((0, (0, wide), (0, wide)))
        all_out = columns_of((1, (0, width), (0, width)))
        order, outputs = every_step, ((every, all_in), (every, all_out))
        if square:
            first = columns_of((0, (0, two), (0, two)))
            second = columns_of((0, (two, wide), (0, width)), (1, (0, width), (width, two)))
            order = tuple((block, kind) for block in (3, 1, 2, 0) for kind in (0, 1))
            outputs = (((1, 3), first), ((2,), first), ((0,), first), ((2, 3), second), ((1,), second), ((0,), second))
        return outer(info, after(normed, *last), cot, grad_packed, attended, chunk, order, outputs, "packed_grads")

    def add(*values):
        return functools.reduce(lambda a, b: a + b, [value.astype(F32) for value in values])

    hidden_grads = hidden_weight_grads(ours)
    if square:
        up_away, up_second, up_own, down_away, down_second, down_own = hidden_grads
        up_came, down_came = by_x(up_away), by_y(down_away)
    grad_packed, in_sum = back_local(
        scene, after(queries, hidden_grads[-1]), grad_att, stat, kv, cross, returned, tables
    )
    if square:
        up_pass = add(up_second, up_came[chunk:]).astype(BF)
        down_pass = add(down_second, down_came[chunk:]).astype(BF)
        up_last, down_last = by_y(up_pass), by_x(down_pass)
        left = after(grad_packed, up_pass, down_pass)
    else:
        left = grad_packed
    ours, gain_part, shift_part = spread(
        left, grad_up, [weights_a], weights_m, 0, 0, depth, "normed_grad", 2, (normed,)
    )
    grad_normed = lax.psum_scatter(ours, "tp", scatter_dimension=0, tiled=True)

    def to_plain(row):
        if not square:
            return row
        return jnp.concatenate([pick(row, r ^ me, chunk, 1) for r in range(chips)], axis=1)

    shift_sum = to_plain(shift_part)
    gain_sum = (to_plain(gain_part) - shift_sum * norm_shift.astype(F32)[None]) / norm_gain.astype(F32)[None]
    once = jnp.where(lax.axis_index("tp") == 0, cot_sum, 0.0)
    both = jnp.concatenate([gain_sum, shift_sum, once, in_sum, up_sum], axis=1)
    wide_size = 3 * depth

    def keep(rows):
        size = rows.shape[0] // 2
        mine, theirs = pick(rows, c_at, size, 0).astype(F32), pick(rows, 1 - c_at, size, 0).astype(BF)
        came = other_core(theirs).astype(F32)
        return jnp.where(c_at == 0, jnp.stack([mine, came]), jnp.stack([came, mine]))

    def side_by_side(two):
        return jnp.transpose(two, (1, 0, 2)).reshape(two.shape[1], 2 * two.shape[2])

    def one_below_other(two):
        return jnp.transpose(two, (0, 2, 1)).reshape(2 * two.shape[2], two.shape[1])

    if square:
        qk_away, qk_second, qk_own, vo_away, vo_second, vo_own = packed_weight_grads((both, up_last, down_last))
        both = both + by_x(both)
        hop = by_y(after(both, qk_away))
        qk_came, vo_came = by_x(qk_away), by_y(vo_away)
        layer_out = layer_rows(info, after(branch, vo_own), tokens, out_bias, chunk)
        both = both + hop
        up_two = keep(add(after(up_own, layer_out, both), up_came[:chunk], up_last))
        down_two = keep(add(after(down_own, layer_out, both), down_came[:chunk], down_last))
        qk_pass = add(after(qk_second, up_two, down_two), qk_came[chunk:]).astype(BF)
        vo_pass = add(after(vo_second, up_two, down_two), vo_came[chunk:]).astype(BF)
        qk_far, vo_far = by_y(qk_pass), by_x(vo_pass)
        upproj_grad, downproj_grad = side_by_side(after(up_two, qk_pass)), one_below_other(after(down_two, vo_pass))
        qk_two = keep(add(after(qk_own, upproj_grad), qk_came[:chunk], qk_far))
        vo_two = keep(add(after(vo_own, downproj_grad), vo_came[:chunk], vo_far))
        in_parts = [qk_two[..., :width], qk_two[..., width:], vo_two[..., :width]]
        out_two = vo_two[..., width:]
    else:
        layer_out = layer_rows(info, branch, tokens, out_bias, chunk)
        both = lax.psum(both, ("fsdp", "cx"))
        up_two, down_two = [keep(scatter(value)) for value in hidden_grads]
        upproj_grad, downproj_grad = side_by_side(up_two), one_below_other(down_two)
        in_two, out_two = [keep(scatter(value)) for value in packed_weight_grads((both,))]
        in_parts = [in_two[..., j * width : j * width + width] for j in range(3)]
    inproj_grad = jnp.stack([side_by_side(part) for part in in_parts])
    outproj_grad = one_below_other(out_two)
    swapped = other_core(both)
    wide = both[:, :wide_size] + swapped[:, :wide_size]
    step = 1
    while step < z_count:
        wide = wide + lax.ppermute(wide, "tp", [(z, z ^ step) for z in range(z_count)])
        step *= 2
    gain_grad, shift_grad, outbias_grad = [wide[0, depth * j : depth * j + depth] for j in range(3)]
    narrow_pair = in_order(both[:, wide_size:], swapped[:, wide_size:], 0)
    inbias_grad = jnp.transpose(narrow_pair[:, : 3 * width].reshape(2, 3, width), (1, 0, 2)).reshape(3, 2 * width)
    upbias_grad = narrow_pair[:, 3 * width :].reshape(2 * hidden_width)
    input_grad = input_grads(info, after(grad_normed, inproj_grad), tokens, cotangent, norm_gain, chunk)
    return (
        layer_out,
        input_grad,
        gain_grad,
        shift_grad,
        inproj_grad,
        inbias_grad,
        outproj_grad,
        upproj_grad,
        upbias_grad,
        downproj_grad,
        outbias_grad,
    )


def solution(mesh):
    sizes = mesh.shape
    split = Mesh(
        mesh.devices.reshape(sizes["fsdp"], sizes["ctx"] // 2, 2, sizes["tp"]), ("fsdp", "cx", "cc", "tp")
    )
    group = ("fsdp", "cx", "cc")
    return jax.shard_map(
        body,
        mesh=split,
        in_specs=(
            P(group, None),
            P(group, None),
            P(group),
            P(group),
            P(),
            P(),
            P(None, group, "tp"),
            P(None, "tp"),
            P("tp", group),
            P(group, "tp"),
            P("tp"),
            P("tp", group),
            P(),
        ),
        out_specs=(
            P(group + ("tp",), None),
            P(group + ("tp",), None),
            P(),
            P(),
            P(None, group, "tp"),
            P(None, "tp"),
            P("tp", group),
            P(group, "tp"),
            P("tp"),
            P("tp", group),
            P(),
        ),
        check_vma=False,
    )
```

```python
import functools
import math

import jax
import jax.numpy as jnp
from jax import lax
from jax.experimental import pallas as pl
from jax.experimental.pallas import tpu as pltpu
from jax.sharding import Mesh
from jax.sharding import PartitionSpec as P

HD = 64
ROT = 32
RUN = 256
EPS = 1e-05
NEG = -1e30
F32 = jnp.float32
BF = jnp.bfloat16
NN = (((1,), (0,)), ((), ()))
NT = (((1,), (1,)), ((), ()))
TN = (((0,), (0,)), ((), ()))
SWAP = [(0, 1), (1, 0)]
GELU_A = math.sqrt(2.0 / math.pi)
GELU_B = 0.044715
COST = 100.0


def dot(a, b, dims=NN):
    return lax.dot_general(a, b, dims, preferred_element_type=F32)


ANY = pl.BlockSpec(memory_space=pl.ANY)


def call(body, name, grid, in_specs, out_specs, out_shape, scratch, flops, moved, prefetch=1, vmem=60, collective=None):
    return pl.pallas_call(
        body,
        out_shape=out_shape,
        grid_spec=pltpu.PrefetchScalarGridSpec(
            num_scalar_prefetch=prefetch,
            grid=grid,
            in_specs=in_specs,
            out_specs=out_specs,
            scratch_shapes=scratch,
        ),
        compiler_params=pltpu.CompilerParams(
            vmem_limit_bytes=vmem << 20,
            dimension_semantics=("arbitrary",) * len(grid),
            collective_id=collective,
            has_side_effects=collective is not None,
        ),
        cost_estimate=pl.CostEstimate(flops=int(flops * COST), bytes_accessed=int(moved * COST), transcendentals=0),
        name=name,
    )


def row_block(size, width):
    return pl.BlockSpec((size, width), lambda i, s: (i, 0))


def fixed(shape, index=None):
    place = index or (0,) * len(shape)
    return pl.BlockSpec(shape, lambda i, s: place, pipeline_mode=pl.Buffered(1))


def norm_parts(rows):
    center = rows - jnp.mean(rows, axis=-1, keepdims=True)
    inverse = lax.rsqrt(jnp.mean(center * center, axis=-1, keepdims=True) + EPS)
    return center * inverse, inverse


def lanes_of(info, chunk, piece):
    return pl.ds(pl.multiple_of((piece ^ info[0]) * chunk, chunk), chunk)


def to_neighbour(source, target, sends, receives, n, axis, at):
    return pltpu.make_async_remote_copy(
        src_ref=source,
        dst_ref=target,
        send_sem=sends.at[n],
        recv_sem=receives.at[n],
        device_id={axis: at},
        device_id_type=pl.DeviceIdType.MESH,
    )


def begin_body(tok, cot, gain, shift, in_ref, out_ref, up_any, down_any, nrm, cot_out, wa, vm_low, vm_high, cot_sum, chip_a, away_a, chip_m, away_m, up_ref, down_ref, nbuf, cbuf, loads, locals_, sends, receives, *, chunk, square, steps):
    i = pl.program_id(0)
    core, x, y = lax.axis_index("cc"), lax.axis_index("cx"), lax.axis_index("fsdp")
    shard = in_ref.shape[1]
    size, depth = tok.shape
    width, wide = chip_a.shape[1] // 4, chip_m.shape[1] // 2
    mine = pl.ds(pl.multiple_of(core * shard, shard), shard)
    rows = 2 * shard
    peers = [("cc", 1 - core)] + ([("cx", 1 - x), ("fsdp", 1 - y)] if square else [])

    load_up = pltpu.make_async_copy(up_any, up_ref, loads.at[0])
    load_down = pltpu.make_async_copy(down_any, down_ref, loads.at[1])
    swap_a = to_neighbour(away_a, chip_a.at[mine, :], sends, receives, 0, "cc", 1 - core)
    swap_m = to_neighbour(away_m, chip_m.at[mine, :], sends, receives, 1, "cc", 1 - core)
    keep_a = pltpu.make_async_copy(chip_a, wa.at[pl.ds(0, rows), :], locals_.at[0])
    keep_m = [
        pltpu.make_async_copy(chip_m.at[pl.ds(0, shard), :], vm_low, locals_.at[1]),
        pltpu.make_async_copy(chip_m.at[pl.ds(shard, shard), :], vm_high, locals_.at[2 + 2 * steps]),
    ]
    if square:
        to_x = to_neighbour(chip_a, wa.at[pl.ds(rows, rows), :], sends, receives, 2, "cx", 1 - x)
        to_y = to_neighbour(chip_a, wa.at[pl.ds(2 * rows, rows), :], sends, receives, 3, "fsdp", 1 - y)
        far_x = to_neighbour(
            wa.at[pl.ds(2 * rows, shard), :], wa.at[pl.ds(3 * rows, shard), :], sends, receives, 4, "cx", 1 - x
        )
        far_y = to_neighbour(
            wa.at[pl.ds(rows + shard, shard), :],
            wa.at[pl.ds(3 * rows + shard, shard), :],
            sends,
            receives,
            5,
            "fsdp",
            1 - y,
        )

    def row_copies(j):
        here = pl.ds(pl.multiple_of(j * size, size), size)
        there = pl.ds(pl.multiple_of((j + steps) * size, size), size)
        return [
            pltpu.make_async_copy(nbuf.at[j], nrm.at[here, :], locals_.at[2 + j]),
            pltpu.make_async_copy(cbuf.at[j], cot_out.at[here, :], locals_.at[2 + steps + j]),
            to_neighbour(nbuf.at[j], nrm.at[there, :], sends, receives, 6 + j, "cc", 1 - core),
            to_neighbour(cbuf.at[j], cot_out.at[there, :], sends, receives, 6 + steps + j, "cc", 1 - core),
        ]

    @pl.when(i == 0)
    def _():
        barrier = pltpu.get_barrier_semaphore()
        for axis, at in peers:
            pl.semaphore_signal(barrier, inc=1, device_id={axis: at}, device_id_type=pl.DeviceIdType.MESH)
        load_up.start()
        load_down.start()
        for target, c, at in ((chip_a, core, mine), (away_a, 1 - core, pl.ds(0, shard))):
            cut = pl.ds(pl.multiple_of(c * width, width), width)
            for j in range(3):
                target[at, width * j : width * j + width] = in_ref[j, :, cut]
            target[at, 3 * width :] = out_ref[cut, :].astype(F32).T.astype(BF)
        pl.semaphore_wait(barrier, len(peers))
        swap_a.start()
        load_up.wait()
        load_down.wait()
        for target, c, at in ((away_m, 1 - core, pl.ds(0, shard)), (chip_m, core, mine)):
            cut = pl.ds(pl.multiple_of(c * wide, wide), wide)
            target[at, :wide] = up_ref[:, cut]
            target[at, wide:] = down_ref[cut, :].astype(F32).T.astype(BF)
            if target is away_m:
                swap_m.start()
                swap_a.wait()
                if square:
                    to_x.start()
                    to_y.start()
                keep_a.start()
        cot_sum[...] = jnp.zeros_like(cot_sum)

    center, _ = norm_parts(tok[...].astype(F32))
    full = (center * gain[...].astype(F32)[None] + shift[...].astype(F32)[None]).astype(BF)
    cot_sum[...] += jnp.sum(cot[...].astype(F32), axis=0, keepdims=True)
    for r in range(depth // chunk):
        place = ((r // 2 + y) % 2) * 2 + (r % 2 + x) % 2 if square else r
        lanes = pl.ds(pl.multiple_of(place * chunk, chunk), chunk) if square else pl.ds(r * chunk, chunk)
        nbuf[i, :, lanes] = full[:, r * chunk : r * chunk + chunk]
        cbuf[i, :, lanes] = cot[:, r * chunk : r * chunk + chunk]
    for copy in row_copies(i):
        copy.start()

    @pl.when(i == steps - 1)
    def _():
        swap_m.wait()
        for copy in keep_m:
            copy.start()
        if square:
            to_y.wait()
            far_x.start()
            to_x.wait()
            far_y.start()
        keep_a.wait()
        for copy in keep_m:
            copy.wait()

        def finish(j, c):
            for copy in row_copies(j):
                copy.wait()
            return c

        lax.fori_loop(0, steps, finish, 0)
        if square:
            far_x.wait()
            far_y.wait()


def begin(tokens, cot, gain, shift, in_proj, out_proj, up_proj, down_proj, chunk, square):
    length, depth = tokens.shape
    steps = 4
    size = length // steps
    shard = in_proj.shape[1]
    width, wide = in_proj.shape[2] // 2, up_proj.shape[1] // 2
    block = pl.BlockSpec((size, depth), lambda i: (i, 0))
    whole = lambda shape: pl.BlockSpec(shape, lambda i: (0,) * len(shape), pipeline_mode=pl.Buffered(1))
    rows = 8 * shard if square else 2 * shard
    return call(
        functools.partial(begin_body, chunk=chunk, square=square, steps=steps),
        "begin",
        (steps,),
        [block, block, whole((depth,)), whole((depth,)), whole(in_proj.shape), whole(out_proj.shape), ANY, ANY],
        [ANY, ANY, ANY, ANY, ANY, pl.BlockSpec((1, depth), lambda i: (0, 0))],
        [
            jax.ShapeDtypeStruct((2 * length, depth), BF),
            jax.ShapeDtypeStruct((2 * length, depth), BF),
            jax.ShapeDtypeStruct((rows, 4 * width), BF),
            jax.ShapeDtypeStruct((shard, 2 * wide), BF),
            jax.ShapeDtypeStruct((shard, 2 * wide), BF),
            jax.ShapeDtypeStruct((1, depth), F32),
        ],
        [
            pltpu.VMEM((2 * shard, 4 * width), BF),
            pltpu.VMEM((shard, 4 * width), BF),
            pltpu.VMEM((2 * shard, 2 * wide), BF),
            pltpu.VMEM((shard, 2 * wide), BF),
            pltpu.VMEM(up_proj.shape, BF),
            pltpu.VMEM(down_proj.shape, BF),
            pltpu.VMEM((steps, size, depth), BF),
            pltpu.VMEM((steps, size, depth), BF),
            pltpu.SemaphoreType.DMA((2,)),
            pltpu.SemaphoreType.DMA((3 + 2 * steps,)),
            pltpu.SemaphoreType.DMA((6 + 2 * steps,)),
            pltpu.SemaphoreType.DMA((6 + 2 * steps,)),
        ],
        10 * tokens.size,
        16 * tokens.size,
        prefetch=0,
        collective=0,
    )(tokens, cot, gain, shift, in_proj, out_proj, up_proj, down_proj)


def rotary_tables(rates, positions, sign):
    angles = rates * positions
    cos_rows, sin_rows = jnp.cos(angles), sign * jnp.sin(angles)
    one = jnp.ones((HD - ROT, cos_rows.shape[1]), F32)
    none = jnp.zeros((HD - ROT, cos_rows.shape[1]), F32)
    few = jnp.zeros_like(cos_rows)
    return (
        jnp.concatenate([cos_rows, cos_rows, one] * 2, axis=0).T,
        jnp.concatenate([-sin_rows, few, none] * 2, axis=0).T,
        jnp.concatenate([few, sin_rows, none] * 2, axis=0).T,
    )


def turn(values, cos_part, down, up):
    return (
        values * cos_part
        + pltpu.roll(values, 128 - ROT // 2, 1) * down
        + pltpu.roll(values, ROT // 2, 1) * up
    )


def stay(shape):
    return pl.BlockSpec(shape, lambda i, s: (0,) * len(shape))


def start_body(tok, cot, gain, shift, in_ref, out_ref, up_any, down_any, bias, own_at, rates, nrm_out, cot_out, wa_out, vm_low, vm_high, q_out, kv_out, do_out, came_out, cot_sum, away_a, chip_m, away_m, up_ref, down_ref, full_n, full_c, wa, acc, positions, q_hold, kv_hold, do_hold, send_hold, loads, locals_, sends, receives, *, chunk, steps, size):
    i = pl.program_id(0)
    core, x, y = lax.axis_index("cc"), lax.axis_index("cx"), lax.axis_index("fsdp")
    shard = in_ref.shape[1]
    length, depth = steps * tok.shape[0], tok.shape[1]
    block = tok.shape[0]
    width, wide = away_a.shape[1] // 4, chip_m.shape[1] // 2
    rows = 2 * shard
    mine = pl.ds(pl.multiple_of(core * shard, shard), shard)
    peers = [("cc", 1 - core), ("cx", 1 - x), ("fsdp", 1 - y)]

    load_up = pltpu.make_async_copy(up_any, up_ref, loads.at[0])
    load_down = pltpu.make_async_copy(down_any, down_ref, loads.at[1])
    swap_a = to_neighbour(away_a, wa.at[mine, :], sends, receives, 0, "cc", 1 - core)
    swap_m = to_neighbour(away_m, chip_m.at[mine, :], sends, receives, 1, "cc", 1 - core)
    home = wa.at[pl.ds(0, rows), :]
    to_x = to_neighbour(home, wa.at[pl.ds(rows, rows), :], sends, receives, 2, "cx", 1 - x)
    to_y = to_neighbour(home, wa.at[pl.ds(2 * rows, rows), :], sends, receives, 3, "fsdp", 1 - y)
    part = wa.at[pl.ds(3 * rows, shard), :]
    far_x = to_neighbour(wa.at[pl.ds(2 * rows, shard), :], part, sends, receives, 4, "cx", 1 - x)
    part = wa.at[pl.ds(3 * rows + shard, shard), :]
    far_y = to_neighbour(wa.at[pl.ds(rows + shard, shard), :], part, sends, receives, 5, "fsdp", 1 - y)
    swap_at = to_neighbour(own_at, positions.at[:, pl.ds(length, length)], sends, receives, 6, "cc", 1 - core)
    halves = [pl.ds(0, length), pl.ds(length, length)]
    stores = [
        [pltpu.make_async_copy(held.at[half, :], out.at[half, :], locals_.at[2 * k + n]) for k, half in enumerate(halves)]
        for n, (held, out) in enumerate(((full_n, nrm_out), (full_c, cot_out)))
    ]
    keep = [
        pltpu.make_async_copy(wa, wa_out, locals_.at[4]),
        pltpu.make_async_copy(chip_m.at[pl.ds(0, shard), :], vm_low, locals_.at[5]),
        pltpu.make_async_copy(chip_m.at[pl.ds(shard, shard), :], vm_high, locals_.at[6]),
    ]

    def row_copies(j):
        here = pl.ds(pl.multiple_of(j * block, block), block)
        there = pl.ds(pl.multiple_of((j + steps) * block, block), block)
        return [
            to_neighbour(full_n.at[here, :], full_n.at[there, :], sends, receives, 7 + j, "cc", 1 - core),
            to_neighbour(full_c.at[here, :], full_c.at[there, :], sends, receives, 7 + steps + j, "cc", 1 - core),
        ]

    @pl.when(i == 0)
    def _():
        barrier = pltpu.get_barrier_semaphore()
        for axis, at in peers:
            pl.semaphore_signal(barrier, inc=1, device_id={axis: at}, device_id_type=pl.DeviceIdType.MESH)
        load_up.start()
        load_down.start()
        for target, c, at in ((wa, core, mine), (away_a, 1 - core, pl.ds(0, shard))):
            cut = pl.ds(pl.multiple_of(c * width, width), width)
            for j in range(3):
                target[at, width * j : width * j + width] = in_ref[j, :, cut]
            target[at, 3 * width :] = out_ref[cut, :].astype(F32).T.astype(BF)
        pl.semaphore_wait(barrier, len(peers))
        swap_a.start()
        swap_at.start()
        positions[:, :length] = own_at[...]
        load_up.wait()
        load_down.wait()
        for target, c, at in ((away_m, 1 - core, pl.ds(0, shard)), (chip_m, core, mine)):
            cut = pl.ds(pl.multiple_of(c * wide, wide), wide)
            target[at, :wide] = up_ref[:, cut]
            target[at, wide:] = down_ref[cut, :].astype(F32).T.astype(BF)
            if target is away_m:
                swap_m.start()
                swap_a.wait()
                to_x.start()
                to_y.start()
        cot_sum[...] = jnp.zeros_like(cot_sum)

    center, _ = norm_parts(tok[...].astype(F32))
    full = (center * gain[...].astype(F32)[None] + shift[...].astype(F32)[None]).astype(BF)
    cot_sum[...] += jnp.sum(cot[...].astype(F32), axis=0, keepdims=True)
    here = pl.ds(pl.multiple_of(i * block, block), block)
    for r in range(depth // chunk):
        place = ((r // 2 + y) % 2) * 2 + (r % 2 + x) % 2
        lanes = pl.ds(pl.multiple_of(place * chunk, chunk), chunk)
        full_n[here, lanes] = full[:, r * chunk : r * chunk + chunk]
        full_c[here, lanes] = cot[:, r * chunk : r * chunk + chunk]
    for copy in row_copies(i):
        copy.start()

    def products(at, low, high):
        return (
            dot(full_n[at, low:high], wa[low:high, : 3 * width]),
            dot(full_c[at, low:high], wa[low:high, 3 * width :]),
        )

    def outputs(r):
        at = pl.ds(pl.multiple_of(r * size, size), size)
        pairs = ((q_hold, q_out), (kv_hold, kv_out), (do_hold, do_out))
        return [
            pltpu.make_async_copy(held.at[at, :], out.at[at, :], locals_.at[7 + 3 * r + n])
            for n, (held, out) in enumerate(pairs)
        ]

    def across(r):
        at = pl.ds(pl.multiple_of(r * size, size), size)
        return to_neighbour(
            send_hold.at[at, :], came_out.at[at, :], sends, receives, 7 + 2 * steps + r, "cx", 1 - x
        )

    @pl.when(i == steps - 1)
    def _():
        count = 2 * length // size
        for pair in stores:
            pair[0].start()
        swap_m.wait()
        keep[1].start()
        keep[2].start()
        swap_at.wait()

        def arrive(j, c):
            for copy in row_copies(j):
                copy.wait()
            return c

        lax.fori_loop(0, steps, arrive, 0)
        for pair in stores:
            pair[1].start()

        def first(r, c):
            at = pl.ds(pl.multiple_of(r * size, size), size)
            acc[at, : 3 * width], acc[at, 3 * width :] = products(at, 0, chunk)
            return c

        lax.fori_loop(0, count, first, 0)
        to_y.wait()
        far_x.start()
        to_x.wait()
        far_y.start()

        def second(r, c):
            at = pl.ds(pl.multiple_of(r * size, size), size)
            packed, do = products(at, chunk, 3 * chunk)
            acc[at, : 3 * width] += packed
            acc[at, 3 * width :] += do
            return c

        lax.fori_loop(0, count, second, 0)
        far_x.wait()
        far_y.wait()
        keep[0].start()
        mine_w = pl.ds(pl.multiple_of(core * width, width), width)
        half = width // 2

        def biases(j, low, high):
            return bias[j : j + 1, mine_w][:, low:high].astype(F32)

        def third(r, carry):
            at = pl.ds(pl.multiple_of(r * size, size), size)
            packed, do = products(at, 3 * chunk, 4 * chunk)
            packed = packed + acc[at, : 3 * width]
            do = do + acc[at, 3 * width :]
            acc[at, : 3 * width] = packed
            acc[at, 3 * width :] = do
            c, d, u = rotary_tables(rates[...], positions[:, at], 1.0)
            query = packed[:, half:width] + biases(0, half, width)
            key = packed[:, width : width + half] + biases(1, 0, half)
            value = packed[:, 2 * width : 2 * width + half] + biases(2, 0, half)
            first_part = jnp.where(x == 0, key, query)
            for k in range(0, half, 128):
                send_hold[at, k : k + 128] = turn(first_part[:, k : k + 128], c, d, u).astype(BF)
            send_hold[at, half:] = jnp.where(x == 0, value, do[:, half:]).astype(BF)
            across(r).start()
            return carry

        lax.fori_loop(0, count, third, 0)

        def fourth(r, carry):
            at = pl.ds(pl.multiple_of(r * size, size), size)
            c, d, u = rotary_tables(rates[...], positions[:, at], 1.0)
            for j, hold in ((0, q_hold), (1, kv_hold)):
                rows_j = acc[at, width * j : width * j + width] + biases(j, 0, width)
                for k in range(0, width, 128):
                    hold[at, k : k + 128] = turn(rows_j[:, k : k + 128], c, d, u).astype(BF)
            kv_hold[at, width:] = (acc[at, 2 * width : 3 * width] + biases(2, 0, width)).astype(BF)
            do_hold[at, :] = acc[at, 3 * width :].astype(BF)
            for copy in outputs(r):
                copy.start()
            return carry

        lax.fori_loop(0, count, fourth, 0)
        for copy in keep + stores[0] + stores[1]:
            copy.wait()

        def finish(r, c):
            for copy in outputs(r):
                copy.wait()
            across(r).wait()
            return c

        lax.fori_loop(0, count, finish, 0)


def start(tokens, cot, gain, shift, in_proj, out_proj, up_proj, down_proj, in_bias, own_at, rates, chunk):
    length, depth = tokens.shape
    steps = 4
    block = length // steps
    size = 256
    count = 2 * length // size
    shard = in_proj.shape[1]
    width, wide = in_proj.shape[2] // 2, up_proj.shape[1] // 2
    spec = pl.BlockSpec((block, depth), lambda i: (i, 0))
    whole = lambda array: pl.BlockSpec(array.shape, lambda i: (0,) * array.ndim, pipeline_mode=pl.Buffered(1))
    both = jax.ShapeDtypeStruct((2 * length, depth), BF)
    heads = [jax.ShapeDtypeStruct((2 * length, n * width), BF) for n in (1, 2, 1, 1)]
    return call(
        functools.partial(start_body, chunk=chunk, steps=steps, size=size),
        "start",
        (steps,),
        [spec, spec, whole(gain), whole(shift), whole(in_proj), whole(out_proj), ANY, ANY]
        + [whole(in_bias), whole(own_at), whole(rates)],
        [ANY] * 9 + [pl.BlockSpec((1, depth), lambda i: (0, 0))],
        [both, both, jax.ShapeDtypeStruct((depth, 4 * width), BF)]
        + [jax.ShapeDtypeStruct((shard, 2 * wide), BF)] * 2
        + heads
        + [jax.ShapeDtypeStruct((1, depth), F32)],
        [
            pltpu.VMEM((shard, 4 * width), BF),
            pltpu.VMEM((2 * shard, 2 * wide), BF),
            pltpu.VMEM((shard, 2 * wide), BF),
            pltpu.VMEM(up_proj.shape, BF),
            pltpu.VMEM(down_proj.shape, BF),
            pltpu.VMEM((2 * length, depth), BF),
            pltpu.VMEM((2 * length, depth), BF),
            pltpu.VMEM((depth, 4 * width), BF),
            pltpu.VMEM((2 * length, 4 * width), F32),
            pltpu.VMEM((1, 2 * length), F32),
        ]
        + [pltpu.VMEM(head.shape, BF) for head in heads]
        + [
            pltpu.SemaphoreType.DMA((2,)),
            pltpu.SemaphoreType.DMA((7 + 3 * count,)),
            pltpu.SemaphoreType.DMA((7 + 2 * steps + count,)),
            pltpu.SemaphoreType.DMA((7 + 2 * steps + count,)),
        ],
        20 * tokens.size,
        16 * tokens.size,
        prefetch=0,
        collective=0,
    )(tokens, cot, gain, shift, in_proj, out_proj, up_proj, down_proj, in_bias, own_at, rates)


def piece_copies(pieces, columns, target, sems):
    copies, at = [], 0
    for n, piece in enumerate(pieces):
        count = piece.shape[0]
        copies.append(
            pltpu.make_async_copy(piece.at[:, columns], target.at[pl.ds(at, count), :], sems.at[n])
        )
        at += count
    return copies


def place_pieces(*jobs):
    copies = [copy for job in jobs for copy in piece_copies(*job)]
    for copy in copies:
        copy.start()
    for copy in copies:
        copy.wait()


def move_sems(pieces):
    return pltpu.SemaphoreType.DMA((len(pieces),))


def project_body(info, nrm, cot, weights, bias, rates, positions, q_out, kv_out, do_out, send, *, width):
    packed = dot(nrm[...], weights[:, : 3 * width]) + bias[...].astype(F32)
    do = dot(cot[...], weights[:, 3 * width :]).astype(BF)
    c, d, u = rotary_tables(rates[...], positions[...], 1.0)
    low = []
    for p in range(2 * width // 128):
        low.append(turn(packed[:, 128 * p : 128 * p + 128], c, d, u).astype(BF))
    pairs = width // 128
    queries = jnp.concatenate(low[:pairs], axis=1)
    keys = jnp.concatenate(low[pairs:], axis=1)
    values = packed[:, 2 * width :].astype(BF)
    q_out[...] = queries
    kv_out[:, :width] = keys
    kv_out[:, width:] = values
    do_out[...] = do
    part = width // 2

    @pl.when(info[3] == 0)
    def _():
        send[:, :part] = keys[:, :part]
        send[:, part:] = values[:, :part]

    @pl.when(info[3] != 0)
    def _():
        send[:, :part] = queries[:, part:]
        send[:, part:] = do[:, part:]


def project(info, normed, cot, weights, bias, tables, width):
    rows, depth = normed.shape
    size = min(rows, 256)
    return call(
        functools.partial(project_body, width=width),
        "project",
        (rows // size,),
        [row_block(size, depth)] * 2 + [fixed((depth, 4 * width)), fixed((1, 3 * width))]
        + [fixed((ROT // 2, 1)), pl.BlockSpec((1, size), lambda i, s: (0, i))],
        [row_block(size, width), row_block(size, 2 * width), row_block(size, width), row_block(size, width)],
        [jax.ShapeDtypeStruct((rows, n * width), BF) for n in (1, 2, 1, 1)],
        [],
        2 * rows * depth * 4 * width,
        2 * (2 * rows * depth + depth * 4 * width + 5 * rows * width),
    )(info, normed, cot, weights, bias, *tables)


def spread_body(a, b, *rest, counts, columns, sums, per):
    na, nb = counts
    wa, wb = rest[:na], rest[na : na + nb]
    rest = rest[na + nb :]
    normed = rest[:sums]
    out = rest[sums]
    totals = rest[sums + 1 : 3 * sums + 1]
    hold_a, hold_b, sem_a, sem_b, outgoing, incoming, send_sems, recv_sems = rest[3 * sums + 1 :]
    i = pl.program_id(0)
    core = lax.axis_index("cc")

    def copy(j):
        return pltpu.make_async_remote_copy(
            src_ref=outgoing.at[j],
            dst_ref=incoming.at[j],
            send_sem=send_sems.at[j],
            recv_sem=recv_sems.at[j],
            device_id={"cc": 1 - core},
            device_id_type=pl.DeviceIdType.MESH,
        )

    @pl.when(i == 0)
    def _():
        barrier = pltpu.get_barrier_semaphore()
        pl.semaphore_signal(barrier, inc=1, device_id={"cc": 1 - core}, device_id_type=pl.DeviceIdType.MESH)
        place_pieces((wa, columns[0], hold_a, sem_a), (wb, columns[1], hold_b, sem_b))
        pl.semaphore_wait(barrier, 1)
        for total in totals:
            total[...] = jnp.zeros_like(total)

    total = dot(a[...], hold_a[...], NT) + dot(b[...], hold_b[...], NT)

    @pl.when(i < per)
    def _():
        outgoing[i] = total.astype(BF)
        copy(i).start()

    @pl.when(i >= per)
    def _():
        copy(i - per).wait()
        full = total + incoming[i - per].astype(F32)
        out[...] = full.astype(BF)
        if sums:
            totals[0][...] += jnp.sum(full * normed[0][...].astype(F32), axis=0, keepdims=True)
            totals[1][...] += jnp.sum(full, axis=0, keepdims=True)


def spread(a, b, wa, wb, ca, cb, depth, name, collective, normed=()):
    rows = a.shape[0] // 2
    size = min(rows, 256)
    per = rows // size
    at = lambda width: pl.BlockSpec((size, width), lambda i: ((i + per) % (2 * per), 0))
    later = pl.BlockSpec((size, depth), lambda i: (jnp.maximum(i - per, 0), 0))
    one = pl.BlockSpec((1, depth), lambda i: (0, 0))
    wide_a, wide_b = a.shape[1], b.shape[1]
    count = len(normed)
    return call(
        functools.partial(
            spread_body,
            counts=(len(wa), len(wb)),
            columns=(slice(ca, ca + wide_a), slice(cb, cb + wide_b)),
            sums=count,
            per=per,
        ),
        name,
        (2 * per,),
        [at(wide_a), at(wide_b)] + [ANY] * (len(wa) + len(wb)) + [later] * count,
        [later] + [one] * (2 * count),
        [jax.ShapeDtypeStruct((rows, depth), BF)] + [jax.ShapeDtypeStruct((1, depth), F32)] * (2 * count),
        [
            pltpu.VMEM((depth, wide_a), BF),
            pltpu.VMEM((depth, wide_b), BF),
            move_sems(wa),
            move_sems(wb),
            pltpu.VMEM((per, size, depth), BF),
            pltpu.VMEM((per, size, depth), BF),
            pltpu.SemaphoreType.DMA((per,)),
            pltpu.SemaphoreType.DMA((per,)),
        ],
        4 * rows * depth * (wide_a + wide_b),
        2 * (2 * rows + depth) * (wide_a + wide_b) + 2 * rows * depth,
        prefetch=0,
        collective=collective,
    )(a, b, *wa, *wb, *normed)


def branch_body(nrm, cot, att, bias, wa, *rest, count, column):
    pieces = rest[:count]
    act_out, grad_out, sum_out, out, hold, hold_a, sem, sem_a, outgoing, incoming, send_sems, recv_sems = rest[count:]
    i = pl.program_id(0)
    per = outgoing.shape[0]
    width = act_out.shape[1]
    core = lax.axis_index("cc")

    def copy(j):
        return to_neighbour(outgoing.at[j], incoming.at[j], send_sems, recv_sems, j, "cc", 1 - core)

    @pl.when(i == 0)
    def _():
        barrier = pltpu.get_barrier_semaphore()
        pl.semaphore_signal(barrier, inc=1, device_id={"cc": 1 - core}, device_id_type=pl.DeviceIdType.MESH)
        place_pieces((pieces, slice(0, 2 * width), hold, sem), ([wa], slice(column, column + att.shape[1]), hold_a, sem_a))
        sum_out[...] = jnp.zeros_like(sum_out)
        pl.semaphore_wait(barrier, 1)

    u = dot(nrm[...], hold[:, :width]) + bias[...].astype(F32)
    g = dot(cot[...], hold[:, width:])
    square = u * u
    t = jnp.tanh(GELU_A * (u + GELU_B * square * u))
    half = 0.5 * (1.0 + t)
    act = (u * half).astype(BF)
    act_out[...] = act
    total = dot(att[...], hold_a[...], NT) + dot(act, hold[:, width:], NT)
    slope = half + 0.5 * u * (1.0 - t * t) * (GELU_A * (1.0 + 3.0 * GELU_B * square))
    low = (g * slope).astype(BF)
    grad_out[...] = low
    sum_out[...] += jnp.sum(low.astype(F32), axis=0, keepdims=True)

    @pl.when(i < per)
    def _():
        outgoing[i] = total.astype(BF)
        copy(i).start()

    @pl.when(i >= per)
    def _():
        copy(i - per).wait()
        out[...] = (total + incoming[i - per].astype(F32)).astype(BF)


def branch_rows(normed, cot, attended, bias, wa, pieces, column):
    rows, depth = normed.shape
    width = bias.shape[1]
    wide_a = attended.shape[1]
    size = min(rows // 2, 256)
    per = rows // 2 // size
    at = lambda wide: pl.BlockSpec((size, wide), lambda i: ((i + per) % (2 * per), 0))
    one = lambda wide: pl.BlockSpec((1, wide), lambda i: (0, 0))
    return call(
        functools.partial(branch_body, count=len(pieces), column=column),
        "branch",
        (2 * per,),
        [at(depth), at(depth), at(wide_a), one(width)] + [ANY] * (1 + len(pieces)),
        [at(width), at(width), one(width), pl.BlockSpec((size, depth), lambda i: (jnp.maximum(i - per, 0), 0))],
        [jax.ShapeDtypeStruct((rows, width), BF)] * 2
        + [jax.ShapeDtypeStruct((1, width), F32), jax.ShapeDtypeStruct((rows // 2, depth), BF)],
        [
            pltpu.VMEM((depth, 2 * width), BF),
            pltpu.VMEM((depth, wide_a), BF),
            move_sems(pieces),
            move_sems([wa]),
            pltpu.VMEM((per, size, depth), BF),
            pltpu.VMEM((per, size, depth), BF),
            pltpu.SemaphoreType.DMA((per,)),
            pltpu.SemaphoreType.DMA((per,)),
        ],
        2 * rows * depth * (3 * width + wide_a),
        2 * (3 * rows * depth + depth * (2 * width + wide_a) + 2 * rows * width),
        prefetch=0,
        collective=1,
    )(normed, cot, attended, bias, wa, *pieces)


def outer_body(info, left_n, left_c, right_n, right_c, *rest, order, outputs):
    i = pl.program_id(0)
    outs = rest[:-3]
    hold_n, hold_c, sems = rest[-3:]
    loads = (
        pltpu.make_async_copy(right_n, hold_n, sems.at[0]),
        pltpu.make_async_copy(right_c, hold_c, sems.at[1]),
    )
    kinds = [kind for _, kind in order]

    @pl.when(i == 0)
    def _():
        loads[kinds[0]].start()
        loads[1 - kinds[0]].start()

    for kind in (0, 1):

        @pl.when(i == kinds.index(kind))
        def _(kind=kind):
            loads[kind].wait()

    for step, (block, kind) in enumerate(order):
        left, right = ((left_n, hold_n), (left_c, hold_c))[kind]

        @pl.when(i == step)
        def _(block=block, kind=kind, left=left, right=right):
            result = dot(left[...], right[...], TN).astype(BF)
            for out, (blocks, parts) in zip(outs, outputs):
                if block in blocks and kind in parts:
                    source, target = parts[kind]
                    out[:, target] = result[:, source]


def by_step(table):
    def at(i):
        value = table[-1]
        for step in range(len(table) - 1):
            value = jnp.where(i == step, table[step], value)
        return value

    return at


def places(order, find):
    used = [find(*entry) for entry in order]
    table, upcoming = [None] * len(used), None
    for step in reversed(range(len(used))):
        upcoming = used[step] if used[step] is not None else upcoming
        table[step] = upcoming
    last = None
    for step, value in enumerate(table):
        last = value if value is not None else last
        table[step] = last
    return by_step(table)


def outer(info, normed, cot, right_n, right_c, chunk, order, outputs, name):
    rows = right_n.shape[0]
    wide = (right_n.shape[1], right_c.shape[1])

    def left(which):
        at = places(order, lambda block, kind: block if kind == which else None)
        return pl.BlockSpec((rows, chunk), lambda i, s: (0, at(i)))

    out_specs, out_shapes = [], []
    for blocks, parts in outputs:
        width = max(target.stop for _, target in parts.values())
        at = places(order, lambda block, kind: blocks.index(block) if block in blocks and kind in parts else None)
        out_specs.append(pl.BlockSpec((chunk, width), lambda i, s, at=at: (at(i), 0)))
        out_shapes.append(jax.ShapeDtypeStruct((len(blocks) * chunk, width), BF))
    return call(
        functools.partial(outer_body, order=order, outputs=outputs),
        name,
        (len(order),),
        [left(0), left(1), ANY, ANY],
        out_specs,
        out_shapes,
        [pltpu.VMEM((rows, wide[0]), BF), pltpu.VMEM((rows, wide[1]), BF), pltpu.SemaphoreType.DMA((2,))],
        rows * chunk * len(order) * sum(wide),
        2 * (rows + chunk) * len(order) * sum(wide),
    )(info, normed, cot, right_n, right_c)


def head_masks(block, scale):
    lane = lax.broadcasted_iota(jnp.int32, block.shape, 1)
    v = block.astype(F32) * scale
    return (jnp.where(lane < HD, v, 0.0).astype(BF), jnp.where(lane < HD, 0.0, v).astype(BF))


def own_mask(flag, width):
    kk = lax.broadcasted_iota(jnp.int32, (RUN, width), 0)
    qq = lax.broadcasted_iota(jnp.int32, (RUN, width), 1)
    return kk <= qq + flag * RUN


def each_prefix(here, half, runs, work):
    size = runs // 2
    while size:

        @pl.when((here & size) != 0)
        def _(size=size):
            low = here & ((runs - 1) & ~(2 * size - 1))
            work(pl.multiple_of((low ^ half) * RUN, RUN), size * RUN)

        size //= 2


def softmax_blocks(state, heads, k_r, vt_r, qm, start, size, mask=None):
    acc, ml = state

    def score(n):
        p, h = divmod(n, 2)
        s = dot(k_r[pl.ds(start, size), 128 * p : 128 * p + 128], qm[p][h], NT)
        return s if mask is None else jnp.where(mask, s, NEG)

    def rest(n, s):
        top = jnp.max(s, axis=0, keepdims=True)
        rows = slice(HD * n, HD * n + HD)
        vb = vt_r[rows, pl.ds(start, size)]
        m = ml[n : n + 1, :]
        new = jnp.maximum(m, top)
        alpha = jnp.exp(m - new)
        e = jnp.exp(s - new)
        ml[n : n + 1, :] = new
        ml[heads + n : heads + n + 1, :] = ml[heads + n : heads + n + 1, :] * alpha + jnp.sum(e, axis=0, keepdims=True)
        acc[rows, :] = acc[rows, :] * alpha + dot(vb, e.astype(BF))

    s = score(0)
    for n in range(heads):
        following = score(n + 1) if n + 1 < heads else None
        rest(n, s)
        s = following


def start_state(acc, ml, heads):
    acc[...] = jnp.zeros_like(acc)
    ml[:heads, :] = jnp.full((heads, ml.shape[1]), NEG, F32)
    ml[heads:, :] = jnp.zeros((heads, ml.shape[1]), F32)


def finish_state(acc, ml, heads, n):
    l = ml[heads + n : heads + n + 1, :]
    return acc[HD * n : HD * n + HD, :] / l, ml[n : n + 1, :] + jnp.log(l)


def query_masks(block, scale):
    return [head_masks(block[:, 128 * p : 128 * p + 128], scale) for p in range(block.shape[1] // 128)]


SCALE = 1.0 / math.sqrt(HD)


def local_body(info, q_ref, k_ref, v_ref, out_ref, lse_ref, vt, acc, ml, *, heads):
    i = pl.program_id(0)
    half = info[0]
    runs = k_ref.shape[0] // RUN

    @pl.when(i == 0)
    def _():
        vt[...] = v_ref[...].astype(F32).T.astype(BF)

    qm = query_masks(q_ref[...], SCALE)
    start_state(acc, ml, heads)
    work = lambda start, size, mask=None: softmax_blocks((acc, ml), heads, k_ref, vt, qm, start, size, mask)
    work(pl.multiple_of(i * RUN, RUN), RUN, own_mask(info[2 + i], q_ref.shape[0]))
    each_prefix(i ^ half, half, runs, work)
    for n in range(heads):
        out_ref[HD * n : HD * n + HD, :], lse_ref[n : n + 1, :] = finish_state(acc, ml, heads, n)


def attend_local(info, q, kv):
    rows, width = q.shape
    heads = width // HD
    columns = lambda count: pl.BlockSpec((count, RUN), lambda i, s: (0, i))
    return call(
        functools.partial(local_body, heads=heads),
        "attend_local",
        (rows // RUN,),
        [row_block(RUN, width), fixed((rows, width)), fixed((rows, width), (0, 1))],
        [columns(width), columns(heads)],
        [jax.ShapeDtypeStruct((width, rows), F32), jax.ShapeDtypeStruct((heads, rows), F32)],
        [pltpu.VMEM((width, rows), BF), pltpu.VMEM((width, RUN), F32), pltpu.VMEM((2 * heads, RUN), F32)],
        25e9,
        14 * rows * width,
    )(info, q, kv, kv)


def cross_body(info, q_ref, came_ref, came0, came1, k_ref, v_ref, out_ref, lse_ref, keys, vt, acc, ml, *, heads, cut):
    late = info[1] > 0

    @pl.when(pl.program_id(0) == 0)
    def _():
        keys[...] = jnp.where(late, came0[...], k_ref[...])
        vt[...] = jnp.where(late, came1[...], v_ref[...]).astype(F32).T.astype(BF)

    qm = query_masks(jnp.where(late, q_ref[...], came_ref[...]), SCALE)
    start_state(acc, ml, heads)
    for j in range(keys.shape[0] // cut):
        softmax_blocks((acc, ml), heads, keys, vt, qm, j * cut, cut)
    for n in range(heads):
        out, lse_ref[n : n + 1, :] = finish_state(acc, ml, heads, n)
        out_ref[HD * n : HD * n + HD, :] = out.astype(BF)


def cross_specs(rows, part):
    own = lambda i, s: (i, 1 - s[1])
    return (
        pl.BlockSpec((RUN, part), own),
        pl.BlockSpec((RUN, part), lambda i, s: (i, 0)),
        fixed((rows, part)),
        fixed((rows, part), (0, 1)),
        pl.BlockSpec((rows, part), lambda i, s: (0, 1 - s[1])),
        pl.BlockSpec((rows, part), lambda i, s: (0, 3 - s[1])),
    )


def attend_cross(info, q, came, kv):
    rows, part = q.shape[0], q.shape[1] // 2
    heads = part // HD
    query, came_block, came0, came1, key, value = cross_specs(rows, part)
    columns = lambda count: pl.BlockSpec((count, RUN), lambda i, s: (0, i))
    return call(
        functools.partial(cross_body, heads=heads, cut=min(rows, 2048)),
        "attend_cross",
        (rows // RUN,),
        [query, came_block, came0, came1, key, value],
        [columns(part), columns(heads)],
        [jax.ShapeDtypeStruct((part, rows), BF), jax.ShapeDtypeStruct((heads, rows), F32)],
        [
            pltpu.VMEM((rows, part), BF),
            pltpu.VMEM((part, rows), BF),
            pltpu.VMEM((part, RUN), F32),
            pltpu.VMEM((2 * heads, RUN), F32),
        ],
        15e9,
        14 * rows * part,
    )(info, q, came, came, came, kv, kv)


def merge_body(info, local, lse_local, mine, lse_mine, came, lse_came, do_ref, att_ref, stat_ref, early_ref, late_ref, *, heads):
    late = info[1] > 0
    part = heads // 2
    size = do_ref.shape[0]
    do_t = do_ref[...].astype(F32).T
    outs = []
    for n in range(heads):
        other, lse_other, m = (mine, lse_mine, n) if n < part else (came, lse_came, n - part)
        rows = slice(HD * n, HD * n + HD)
        ours = lse_local[n : n + 1, :]
        theirs = jnp.where(late, lse_other[m : m + 1, :], jnp.full((1, size), NEG, F32))
        top = jnp.maximum(ours, theirs)
        a, b = jnp.exp(ours - top), jnp.exp(theirs - top)
        total = a + b
        o = (local[rows, :] * a + other[HD * m : HD * m + HD, :].astype(F32) * b) / total
        outs.append(o)
        lse = top + jnp.log(total)
        delta = jnp.sum(o * do_t[rows, :], axis=0, keepdims=True)
        stat_ref[n : n + 1, :] = lse
        stat_ref[heads + n : heads + n + 1, :] = delta
        for ref, base in ((early_ref, 0), (late_ref, part)):
            if base <= n < base + part:
                ref[n - base : n - base + 1, :] = lse
                ref[part + n - base : part + n - base + 1, :] = delta
    att_ref[...] = jnp.concatenate(outs, axis=0).T.astype(BF)


def merge(info, local, lse_local, mine, lse_mine, came, lse_came, do):
    rows, width = do.shape
    heads = width // HD
    size = min(rows, 512)
    columns = lambda count: pl.BlockSpec((count, size), lambda i, s: (0, i))
    return call(
        functools.partial(merge_body, heads=heads),
        "merge",
        (rows // size,),
        [columns(width), columns(heads)] + [columns(width // 2), columns(heads // 2)] * 2 + [row_block(size, width)],
        [row_block(size, width), columns(2 * heads), columns(heads), columns(heads)],
        [jax.ShapeDtypeStruct((rows, width), BF)]
        + [jax.ShapeDtypeStruct((count, rows), F32) for count in (2 * heads, heads, heads)],
        [],
        20 * rows * width,
        10 * rows * width,
    )(info, local, lse_local, mine, lse_mine, came, lse_came, do)


def gradient_blocks(heads, k_r, v_r, kt_r, dk_r, dv_r, dqt, qm, dm, stat, start, size, mask=None):
    def products(n):
        p, h = divmod(n, 2)
        lanes = slice(128 * p, 128 * p + 128)
        return (
            dot(k_r[pl.ds(start, size), lanes], qm[p][h], NT),
            dot(v_r[pl.ds(start, size), lanes], dm[p][h], NT),
        )

    def rest(n, s, g):
        p, h = divmod(n, 2)
        e = jnp.exp(s - stat[n : n + 1, :])
        if mask is not None:
            e = jnp.where(mask, e, 0.0)
        ds = (e * (g - stat[heads + n : heads + n + 1, :])).astype(BF)
        rows = slice(HD * n, HD * n + HD)
        dqt[rows, :] += dot(kt_r[rows, pl.ds(start, size)], ds)
        return dot(ds, qm[p][h]), dot(e.astype(BF), dm[p][h])

    now = products(0)
    before = None
    for n in range(heads):
        following = products(n + 1) if n + 1 < heads else None
        grads = rest(n, *now)
        now = following
        if n % 2:
            lanes = slice(HD * (n - 1), HD * (n + 1))
            dk_r[pl.ds(start, size), lanes] += before[0] + grads[0]
            dv_r[pl.ds(start, size), lanes] += before[1] + grads[1]
        before = grads


def local_back_body(info, q_ref, do_ref, stat_ref, k_ref, v_ref, dqx, dkx, dvx, came_q, came_k, came_v, rates, positions, out, sums, kt, dqt, dk, dv, *, heads):
    i = pl.program_id(0)
    half = info[0]
    late = info[1] > 0
    runs = k_ref.shape[0] // RUN
    width = HD * heads
    part = width // 2

    @pl.when(i == 0)
    def _():
        kt[...] = k_ref[...].astype(F32).T.astype(BF)

    @pl.when((i == 0) & late)
    def _():
        dk[...] = jnp.zeros_like(dk)
        dv[...] = jnp.zeros_like(dv)

    @pl.when((i == 0) & jnp.logical_not(late))
    def _():
        dk[:, :part] = came_k[...].astype(F32)
        dk[:, part:] = dkx[...]
        dv[:, :part] = came_v[...].astype(F32)
        dv[:, part:] = dvx[...]

    qm = query_masks(q_ref[...], SCALE)
    dm = query_masks(do_ref[...], 1.0)
    dqt[...] = jnp.zeros_like(dqt)

    def work(start, size, mask=None):
        gradient_blocks(heads, k_ref, v_ref, kt, dk, dv, dqt, qm, dm, stat_ref, start, size, mask)

    work(pl.multiple_of(i * RUN, RUN), RUN, own_mask(info[2 + i], q_ref.shape[0]))
    each_prefix(i ^ half, half, runs, work)
    zero = jnp.zeros((q_ref.shape[0], part), F32)
    more = jnp.concatenate(
        [jnp.where(late, dqx[...], zero), jnp.where(late, came_q[...].astype(F32), zero)], axis=1
    )
    found = (dqt[...] * SCALE).T + more
    rows = pl.ds(pl.multiple_of(i * RUN, RUN), RUN)
    c, d, u = rotary_tables(rates[...], positions[:, rows], -1.0)
    for p in range(width // 128):
        lanes = slice(128 * p, 128 * p + 128)
        out[rows, lanes] = turn(found[:, lanes], c, d, u).astype(BF)

    @pl.when(i == pl.num_programs(0) - 1)
    def _():
        def step(j, c):
            at = pl.ds(pl.multiple_of(j * RUN, RUN), RUN)
            c2, d2, u2 = rotary_tables(rates[...], positions[:, at], -1.0)
            for p in range(width // 128):
                lanes = slice(128 * p, 128 * p + 128)
                shifted = slice(width + 128 * p, width + 128 * p + 128)
                out[at, shifted] = turn(dk[at, lanes], c2, d2, u2).astype(BF)
            out[at, 2 * width :] = dv[at, :].astype(BF)
            return c + jnp.sum(out[at, :].astype(F32), axis=0, keepdims=True)

        sums[...] = lax.fori_loop(0, runs, step, jnp.zeros((1, 3 * width), F32))


def back_local(info, q, do, stat, kv, cross, came, tables):
    rows, width = q.shape
    heads = width // HD
    part = width // 2
    blk = row_block(RUN, width)
    few = row_block(RUN, part)
    return call(
        functools.partial(local_back_body, heads=heads),
        "back_local",
        (rows // RUN,),
        [
            blk,
            blk,
            pl.BlockSpec((2 * heads, RUN), lambda i, s: (0, i)),
            fixed((rows, width)),
            fixed((rows, width), (0, 1)),
            few,
            fixed((rows, part)),
            fixed((rows, part)),
            few,
            fixed((rows, part)),
            fixed((rows, part), (0, 1)),
            fixed((ROT // 2, 1)),
            fixed((1, rows)),
        ],
        [stay((rows, 3 * width)), stay((1, 3 * width))],
        [jax.ShapeDtypeStruct((rows, 3 * width), BF), jax.ShapeDtypeStruct((1, 3 * width), F32)],
        [
            pltpu.VMEM((width, rows), BF),
            pltpu.VMEM((width, RUN), F32),
            pltpu.VMEM((rows, width), F32),
            pltpu.VMEM((rows, width), F32),
        ],
        40e9,
        20 * rows * width,
    )(info, q, do, stat, kv, kv, *cross, came, came, came, *tables)


def cross_back_body(info, q_ref, do_ref, came_q, came_do, came0, came1, k_ref, v_ref, early, came_stat, dq_ref, dk_ref, dv_ref, send, keys, values, kt, dqt, *, heads, cut):
    late = info[1] > 0
    i = pl.program_id(0)
    part = HD * heads

    @pl.when(i == 0)
    def _():
        chosen = jnp.where(late, came0[...], k_ref[...])
        keys[...] = chosen
        kt[...] = chosen.astype(F32).T.astype(BF)
        values[...] = jnp.where(late, came1[...], v_ref[...])
        dk_ref[...] = jnp.zeros_like(dk_ref)
        dv_ref[...] = jnp.zeros_like(dv_ref)

    qm = query_masks(jnp.where(late, q_ref[...], came_q[...]), SCALE)
    dm = query_masks(jnp.where(late, do_ref[...], came_do[...]), 1.0)
    dqt[...] = jnp.zeros_like(dqt)
    stat = jnp.where(late, early[...], came_stat[...])
    for j in range(keys.shape[0] // cut):
        gradient_blocks(heads, keys, values, kt, dk_ref, dv_ref, dqt, qm, dm, stat, j * cut, cut)
    found = (dqt[...] * SCALE).T
    dq_ref[...] = found
    rows = pl.ds(pl.multiple_of(i * RUN, RUN), RUN)

    @pl.when(jnp.logical_not(late))
    def _():
        send[rows, :part] = found.astype(BF)
        send[rows, part:] = found.astype(BF)

    @pl.when(late & (i == pl.num_programs(0) - 1))
    def _():
        send[:, :part] = dk_ref[...].astype(BF)
        send[:, part:] = dv_ref[...].astype(BF)


def back_cross(info, q, do, came, kv, early, came_stat):
    rows, part = q.shape[0], q.shape[1] // 2
    heads = part // HD
    query, came_block, came0, came1, key, value = cross_specs(rows, part)
    acc = jax.ShapeDtypeStruct((rows, part), F32)
    return call(
        functools.partial(cross_back_body, heads=heads, cut=min(rows, 1024)),
        "back_cross",
        (rows // RUN,),
        [
            query,
            query,
            came_block,
            pl.BlockSpec((RUN, part), lambda i, s: (i, 1)),
            came0,
            came1,
            key,
            value,
            pl.BlockSpec((2 * heads, RUN), lambda i, s: (0, i)),
            pl.BlockSpec((2 * heads, RUN), lambda i, s: (0, i)),
        ],
        [row_block(RUN, part), stay((rows, part)), stay((rows, part)), stay((rows, 2 * part))],
        [acc, acc, acc, jax.ShapeDtypeStruct((rows, 2 * part), BF)],
        [
            pltpu.VMEM((rows, part), BF),
            pltpu.VMEM((rows, part), BF),
            pltpu.VMEM((part, rows), BF),
            pltpu.VMEM((part, RUN), F32),
        ],
        25e9,
        20 * rows * part,
    )(info, q, do, came, came, came, came, kv, kv, early, came_stat)


def input_body(info, grad, tok, cot, gain, out, *, chunk):
    xhat, inverse = norm_parts(tok[...].astype(F32))
    parts = [grad[:, lanes_of(info, chunk, r)] for r in range(tok.shape[1] // chunk)]
    e = jnp.concatenate(parts, axis=1).astype(F32) * gain[...].astype(F32)
    mean_e = jnp.mean(e, axis=-1, keepdims=True)
    mean_ex = jnp.mean(e * xhat, axis=-1, keepdims=True)
    out[...] = (cot[...].astype(F32) + (e - mean_e - xhat * mean_ex) * inverse).astype(BF)


def input_grads(info, grad, tok, cot, gain, chunk):
    rows, width = grad.shape
    steps = 4
    size = rows // steps
    share = pl.BlockSpec((size, width), lambda i, s: (s[1] * steps + i, 0))
    return call(
        functools.partial(input_body, chunk=chunk),
        "input_grad",
        (steps,),
        [row_block(size, width), share, share, fixed((1, width))],
        [row_block(size, width)],
        [jax.ShapeDtypeStruct((rows, width), BF)],
        [],
        20 * rows * width,
        8 * rows * width,
    )(info, grad, tok, cot, gain[None])[0]


def layer_body(info, branch, tok, bias, out, *, chunk):
    for r in range(tok.shape[1] // chunk):
        at = slice(r * chunk, r * chunk + chunk)
        part = branch[:, lanes_of(info, chunk, r)].astype(F32)
        out[:, at] = (tok[:, at].astype(F32) + part + bias[:, at].astype(F32)).astype(BF)


def layer_rows(info, branch, tok, bias, chunk):
    rows, width = branch.shape
    return call(
        functools.partial(layer_body, chunk=chunk),
        "layer_out",
        (1,),
        [row_block(rows, width), pl.BlockSpec((rows, width), lambda i, s: (s[1], 0)), fixed((1, width))],
        [row_block(rows, width)],
        [jax.ShapeDtypeStruct((rows, width), BF)],
        [],
        4 * branch.size,
        6 * branch.size,
    )(info, branch, tok, bias[None])[0]


def body(tokens, cotangent, piece_ids, positions, norm_gain, norm_shift, in_proj, in_bias, out_proj, up_proj, up_bias, down_proj, out_bias):
    length, depth = tokens.shape
    width = in_bias.shape[1] // 2
    hidden_width = up_bias.shape[0] // 2
    f_count, z_count = lax.axis_size("fsdp"), lax.axis_size("tp")
    x_at, c_at, f_at = lax.axis_index("cx"), lax.axis_index("cc"), lax.axis_index("fsdp")
    square = f_count == 2
    chips = 2 * f_count
    chunk = depth // chips
    me = f_at * 2 + x_at if square else 0 * f_at
    info = jnp.stack([me, lax.axis_index("tp"), c_at, x_at]).astype(jnp.int32)

    other_core = lambda value: lax.ppermute(value, "cc", SWAP)
    by_x = lambda value: lax.ppermute(value, "cx", SWAP)
    by_y = lambda value: lax.ppermute(value, "fsdp", SWAP)

    def pick(value, index, size, axis):
        return lax.dynamic_slice_in_dim(value, index * size, size, axis)

    def in_order(mine, theirs, axis):
        return jnp.where(c_at == 0, jnp.concatenate([mine, theirs], axis), jnp.concatenate([theirs, mine], axis))

    def after(value, *earlier):
        return lax.optimization_barrier((value,) + earlier)[0]

    shard = in_proj.shape[1]
    frequency = 10000.0 ** (-2.0 * jnp.arange(ROT // 2, dtype=F32) / ROT)
    rates = frequency[:, None]
    if square:
        own_at = positions.astype(F32)[None, :]
        normed, cot, weights_a, low_m, high_m, queries, kv, grad_att, came, cot_sum = start(
            tokens, cotangent, norm_gain, norm_shift, in_proj, out_proj, up_proj, down_proj, in_bias, own_at, rates, chunk
        )
    else:
        normed, cot, weights_a, low_m, high_m, cot_sum = begin(
            tokens, cotangent, norm_gain, norm_shift, in_proj, out_proj, up_proj, down_proj, chunk, square
        )
        weights_a = lax.all_gather(weights_a, ("fsdp", "cx"), axis=0, tiled=True)
        both_m = jnp.concatenate([low_m, high_m], axis=0)
        weights_m = [lax.all_gather(both_m, ("fsdp", "cx"), axis=0, tiled=True)]
    small = jnp.stack([piece_ids, positions])
    small = jnp.concatenate([small, other_core(small)], axis=1)
    pieces, rows_at = small[0], small[1]

    tables = (rates, rows_at.astype(F32)[None, :])
    bias_a = pick(in_bias, c_at, width, 1).reshape(1, 3 * width)
    bias_m = pick(up_bias, c_at, hidden_width, 0)[None]
    flags = (pieces.reshape(-1, RUN)[:, 0] > 0).astype(jnp.int32)
    scene = jnp.concatenate([jnp.stack([c_at * (length // RUN), x_at]).astype(jnp.int32), flags])

    if square:
        x_first, y_first, y_second = by_x(low_m), by_y(low_m), by_y(high_m)
    else:
        queries, kv, grad_att, send = project(info, normed, cot, weights_a, bias_a, tables, width)
        came = by_x(send)
    mine, lse_mine = attend_cross(scene, queries, came, kv)
    local, lse_local = attend_local(scene, after(queries, mine, *([x_first, y_first] if square else [])), kv)
    forward_x = lambda value: lax.ppermute(value, "cx", [(0, 1)])
    if square:
        x_second, y_back = by_x(after(high_m, mine)), by_y(x_first)
    attended, stat, stat_early, stat_late = merge(
        scene,
        after(local, x_second, y_second) if square else local,
        lse_local,
        mine,
        lse_mine,
        forward_x(mine),
        forward_x(lse_mine),
        grad_att,
    )
    stat_came = lax.ppermute(stat_late, "cx", [(1, 0)])
    if square:
        weights_m = [low_m, high_m, x_first, x_second, y_first, y_second, y_back, by_x(after(y_second, stat_came))]
    *cross, outgoing = back_cross(scene, queries, grad_att, came, kv, stat_early, stat_came)
    returned = by_x(outgoing)
    active, grad_up, up_sum, ours = branch_rows(
        normed, cot, after(attended, outgoing), bias_m, weights_a, weights_m, 3 * width
    )
    branch = lax.psum_scatter(ours, "tp", scatter_dimension=0, tiled=True)

    def scatter(value):
        return lax.psum_scatter(value, ("fsdp", "cx"), scatter_dimension=0, tiled=True)

    every = tuple(range(chips))
    every_step = tuple((block, kind) for kind in (0, 1) for block in every)

    def columns_of(*parts):
        return {kind: (slice(*source), slice(*target)) for kind, source, target in parts}

    def hidden_weight_grads(last):
        up = columns_of((0, (0, hidden_width), (0, hidden_width)))
        down = columns_of((1, (0, hidden_width), (0, hidden_width)))
        order, outputs = every_step, ((every, up), (every, down))
        if square:
            order = tuple((block, 0) for block in (1, 3, 2, 0)) + tuple((block, 1) for block in (2, 3, 1, 0))
            outputs = (((1, 3), up), ((2,), up), ((0,), up), ((2, 3), down), ((1,), down), ((0,), down))
        return outer(info, after(normed, last), cot, grad_up, active, chunk, order, outputs, "hidden_grads")

    def packed_weight_grads(last):
        wide = 3 * width
        two = 2 * width
        all_in = columns_of((0, (0, wide), (0, wide)))
        all_out = columns_of((1, (0, width), (0, width)))
        order, outputs = every_step, ((every, all_in), (every, all_out))
        if square:
            first = columns_of((0, (0, two), (0, two)))
            second = columns_of((0, (two, wide), (0, width)), (1, (0, width), (width, two)))
            order = tuple((block, kind) for block in (3, 1, 2, 0) for kind in (0, 1))
            outputs = (((1, 3), first), ((2,), first), ((0,), first), ((2, 3), second), ((1,), second), ((0,), second))
        return outer(info, after(normed, *last), cot, grad_packed, attended, chunk, order, outputs, "packed_grads")

    def add(*values):
        return functools.reduce(lambda a, b: a + b, [value.astype(F32) for value in values])

    hidden_grads = hidden_weight_grads(ours)
    if square:
        up_away, up_second, up_own, down_away, down_second, down_own = hidden_grads
        up_came, down_came = by_x(up_away), by_y(down_away)
    grad_packed, in_sum = back_local(
        scene, after(queries, hidden_grads[-1]), grad_att, stat, kv, cross, returned, tables
    )
    if square:
        up_pass = add(up_second, up_came[chunk:]).astype(BF)
        down_pass = add(down_second, down_came[chunk:]).astype(BF)
        up_last, down_last = by_y(up_pass), by_x(down_pass)
        left = after(grad_packed, up_pass, down_pass)
    else:
        left = grad_packed
    ours, gain_part, shift_part = spread(
        left, grad_up, [weights_a], weights_m, 0, 0, depth, "normed_grad", 2, (normed,)
    )
    grad_normed = lax.psum_scatter(ours, "tp", scatter_dimension=0, tiled=True)

    def to_plain(row):
        if not square:
            return row
        return jnp.concatenate([pick(row, r ^ me, chunk, 1) for r in range(chips)], axis=1)

    shift_sum = to_plain(shift_part)
    gain_sum = (to_plain(gain_part) - shift_sum * norm_shift.astype(F32)[None]) / norm_gain.astype(F32)[None]
    once = jnp.where(lax.axis_index("tp") == 0, cot_sum, 0.0)
    both = jnp.concatenate([gain_sum, shift_sum, once, in_sum, up_sum], axis=1)
    wide_size = 3 * depth

    def keep(rows):
        size = rows.shape[0] // 2
        mine, theirs = pick(rows, c_at, size, 0).astype(F32), pick(rows, 1 - c_at, size, 0).astype(BF)
        came = other_core(theirs).astype(F32)
        return jnp.where(c_at == 0, jnp.stack([mine, came]), jnp.stack([came, mine]))

    def side_by_side(two):
        return jnp.transpose(two, (1, 0, 2)).reshape(two.shape[1], 2 * two.shape[2])

    def one_below_other(two):
        return jnp.transpose(two, (0, 2, 1)).reshape(2 * two.shape[2], two.shape[1])

    if square:
        qk_away, qk_second, qk_own, vo_away, vo_second, vo_own = packed_weight_grads((both, up_last, down_last))
        both = both + by_x(both)
        hop = by_y(after(both, qk_away))
        qk_came, vo_came = by_x(qk_away), by_y(vo_away)
        layer_out = layer_rows(info, after(branch, vo_own), tokens, out_bias, chunk)
        both = both + hop
        up_two = keep(add(after(up_own, layer_out, both), up_came[:chunk], up_last))
        down_two = keep(add(after(down_own, layer_out, both), down_came[:chunk], down_last))
        qk_pass = add(after(qk_second, up_two, down_two), qk_came[chunk:]).astype(BF)
        vo_pass = add(after(vo_second, up_two, down_two), vo_came[chunk:]).astype(BF)
        qk_far, vo_far = by_y(qk_pass), by_x(vo_pass)
        upproj_grad, downproj_grad = side_by_side(after(up_two, qk_pass)), one_below_other(after(down_two, vo_pass))
        qk_two = keep(add(after(qk_own, upproj_grad), qk_came[:chunk], qk_far))
        vo_two = keep(add(after(vo_own, downproj_grad), vo_came[:chunk], vo_far))
        in_parts = [qk_two[..., :width], qk_two[..., width:], vo_two[..., :width]]
        out_two = vo_two[..., width:]
    else:
        layer_out = layer_rows(info, branch, tokens, out_bias, chunk)
        both = lax.psum(both, ("fsdp", "cx"))
        up_two, down_two = [keep(scatter(value)) for value in hidden_grads]
        upproj_grad, downproj_grad = side_by_side(up_two), one_below_other(down_two)
        in_two, out_two = [keep(scatter(value)) for value in packed_weight_grads((both,))]
        in_parts = [in_two[..., j * width : j * width + width] for j in range(3)]
    inproj_grad = jnp.stack([side_by_side(part) for part in in_parts])
    outproj_grad = one_below_other(out_two)
    swapped = other_core(after(both, upproj_grad, downproj_grad) if square else both)
    wide = both[:, :wide_size] + swapped[:, :wide_size]
    step = 1
    while step < z_count:
        wide = wide + lax.ppermute(wide, "tp", [(z, z ^ step) for z in range(z_count)])
        step *= 2
    gain_grad, shift_grad, outbias_grad = [wide[0, depth * j : depth * j + depth] for j in range(3)]
    narrow_pair = in_order(both[:, wide_size:], swapped[:, wide_size:], 0)
    inbias_grad = jnp.transpose(narrow_pair[:, : 3 * width].reshape(2, 3, width), (1, 0, 2)).reshape(3, 2 * width)
    upbias_grad = narrow_pair[:, 3 * width :].reshape(2 * hidden_width)
    input_grad = input_grads(info, after(grad_normed, inproj_grad), tokens, cotangent, norm_gain, chunk)
    return (
        layer_out,
        input_grad,
        gain_grad,
        shift_grad,
        inproj_grad,
        inbias_grad,
        outproj_grad,
        upproj_grad,
        upbias_grad,
        downproj_grad,
        outbias_grad,
    )


def solution(mesh):
    sizes = mesh.shape
    split = Mesh(
        mesh.devices.reshape(sizes["fsdp"], sizes["ctx"] // 2, 2, sizes["tp"]), ("fsdp", "cx", "cc", "tp")
    )
    group = ("fsdp", "cx", "cc")
    return jax.shard_map(
        body,
        mesh=split,
        in_specs=(
            P(group, None),
            P(group, None),
            P(group),
            P(group),
            P(),
            P(),
            P(None, group, "tp"),
            P(None, "tp"),
            P("tp", group),
            P(group, "tp"),
            P("tp"),
            P("tp", group),
            P(),
        ),
        out_specs=(
            P(group + ("tp",), None),
            P(group + ("tp",), None),
            P(),
            P(),
            P(None, group, "tp"),
            P(None, "tp"),
            P("tp", group),
            P(group, "tp"),
            P("tp"),
            P("tp", group),
            P(),
        ),
        check_vma=False,
    )
```
